32 devices in a mesh: fsdp: 2 (over x), ep: 16 (over z, y, core).
Axes of the slice: x: 2, y: 2, z: 4, core: 2. Of those that a mesh axis runs over, the one named last changes fastest.
Arguments:
- x_resid: bfloat16 [32, 64, 2048], P(('fsdp', 'ep')), may hold values from -1.5 to 1.5
- q_latent: bfloat16 [32, 64, 8, 512], P(('fsdp', 'ep')), may hold values from -3 to 3
- q_rope: bfloat16 [32, 64, 8, 64], P(('fsdp', 'ep')), may hold values from -27 to 27
- cache_latent: bfloat16 [32, 64, 512], P(('fsdp', 'ep')), may hold values from -6 to 6
- cache_rope: bfloat16 [32, 64, 64], P(('fsdp', 'ep')), may hold values from -6 to 6
- new_latent: bfloat16 [32, 64, 512], P(('fsdp', 'ep')), may hold values from -6 to 6
- new_rope: bfloat16 [32, 64, 64], P(('fsdp', 'ep')), may hold values from -6 to 6
- w_uv: bfloat16 [512, 8, 128], P('fsdp'), may hold values from -0.25 to 0.25
- w_out: bfloat16 [1024, 2048], P('fsdp'), may hold values from -0.1875 to 0.1875
- norm_gain: float32 [2048], replicated, may hold values from 0.5 to 2
- router: bfloat16 [2048, 16], replicated, may hold values from -0.026516504 to 0.026516504
- expert_ids: int32 [32, 64, 6], P(('fsdp', 'ep')), may hold values from 0 to 15, all different within a row; in each aligned block of 64 rows (0 to 63, 64 to 127, ..., all dimensions but the last counted through in order) at most 24 rows name the same one
- w_gate: bfloat16 [16, 2048, 704], P('ep'), may hold values from -0.125 to 0.125
- w_up: bfloat16 [16, 2048, 704], P('ep'), may hold values from -0.125 to 0.125
- w_down: bfloat16 [16, 704, 2048], P('ep'), may hold values from -0.21875 to 0.21875
Outputs:
- attended: bfloat16 [32, 64, 2048], P(('fsdp', 'ep'))
- layer_out: bfloat16 [32, 64, 2048], P(('fsdp', 'ep'))
The draws below stay inside these ranges and needn't reach their ends.
Inputs may be any that keep to these rules, and one draw needn't show every extreme that they name: `expert_ids`: within the 64 tokens of one sequence every expert is named exactly 24 times.
All inputs are finite; a program needn't handle non-finite values.
Results may differ from the reference program's by a relative error of at most 0.008.
Values may be sent and summed in bfloat16 or wider, within the bound.
No kernel may reach another device: no remote copies, remote signals or barrier semaphores. Data moves between devices by JAX's collectives and lax.ppermute only.
A program may use at most 64 MiB of HBM per device.

```python
import math
import jax
import jax.numpy as jnp
import numpy as np
from jax import lax

D = 2048
H = 8
LAT = 512
DR = 64
DV = 128
FFE = 704
TOPK = 6
CACHE = 64
NEW = 64
SEQS = 32
EXPERTS = 16
CAP = 24


def rope_pair(key):
    key_rope = jnp.clip(jax.random.normal(jax.random.fold_in(key, 12), (SEQS, CACHE, DR), jnp.float32), -6.0, 6.0)
    queries = jnp.clip(jax.random.normal(jax.random.fold_in(key, 13), (SEQS, NEW, H, DR), jnp.float32), -6.0, 6.0)
    return (key_rope, queries)


def draw_cache_rope(key, part):
    key_rope, queries = rope_pair(key)
    return key_rope.astype(jnp.bfloat16)


def draw_q_rope(key, part):
    key_rope, queries = rope_pair(key)
    return queries.astype(jnp.bfloat16)


def draw_router(key, part):
    inverse_root = 1.0 / D ** 0.5
    values = jnp.clip(0.3 * jax.random.normal(jax.random.fold_in(key, 22), (D, EXPERTS), jnp.float32), -1.2, 1.2)
    return (values * inverse_root).astype(jnp.bfloat16)


def steps_of(stream_key, extent, shards, smallest, top_value):
    factor_of, own = 1.0, jax.random.fold_in(stream_key, 6)
    for dim, parts in shards:
        steps = jnp.exp(jax.random.uniform(jax.random.fold_in(own, dim), (parts,), jnp.float32, smallest / len(shards), top_value / len(shards)))
        factor_of = factor_of * jnp.repeat(steps, extent[dim] // parts).reshape([-1 if axis == dim else 1 for axis in range(len(extent))])
    return factor_of


def routed_block(rng, own, number, rows, number_of, top, most, slope):
    order = jax.random.permutation(rng, number_of)
    heavy_load, usual = shares(number_of, rows * top, most, slope, True), shares(number_of, rows * top, most, slope, False)
    places = jnp.arange(number_of)

    def named(tallies, turn):
        used = int((tallies > 0).sum())
        fixed = max(1, used // 4)
        passed = fixed + (places - fixed + turn * (used - fixed)) % max(1, number_of - fixed)
        return jnp.zeros((number_of,), jnp.int32).at[order[jnp.where(places < fixed, places, passed)]].set(jnp.asarray(tallies, jnp.int32))

    tallies = jnp.where(number % 4 == 0, named(heavy_load, number // 4), named(usual, number - number // 4 - 1))
    mixed = jax.random.permutation(jax.random.fold_in(own, 3), number_of)
    source_of, taker = mixed[0:number_of // 2 * 2:2], mixed[1:number_of // 2 * 2:2]
    slack = jnp.minimum(tallies[source_of] - 1, most - tallies[taker]) // 2
    slack = jnp.where((source_of == order[0]) | (taker == order[0]) | (tallies[taker] == 0), 0, jnp.maximum(slack, 0))
    passed = jax.random.randint(jax.random.fold_in(own, 4), (number_of // 2,), 0, 1 << 20) % (slack + 1)
    tallies = tallies.at[source_of].add(-passed).at[taker].add(passed)
    items = jnp.searchsorted(jnp.cumsum(tallies), jnp.arange(rows * top), side="right").astype(jnp.int32)
    listing = items.reshape(top, rows).T
    listing = listing[jax.random.permutation(jax.random.fold_in(own, 1), rows)]
    turn = jax.random.randint(jax.random.fold_in(own, 2), (rows, 1), 0, top)
    return jnp.take_along_axis(listing, (jnp.arange(top)[None, :] + turn) % top, axis=1)


def shares(count, total, limit, skew, full):
    weights = [(1 << 20) // math.isqrt(standing ** skew) + 1 for standing in range(1, count + 1)]
    largest = limit if full else min(limit, max(-(-total // count), total * weights[0] // sum(weights)))
    least = 1 if total - largest >= count - 1 else 0
    counts, rest = [largest] + [least] * (count - 1), total - largest - least * (count - 1)
    while rest > 0:
        free = [i for i in range(1, count) if counts[i] < largest] or [i for i in range(1, count) if counts[i] < limit]
        mass, remaining = sum([weights[i] for i in free]), rest
        for i in free:
            addition = min(limit - counts[i], max(1, remaining * weights[i] // mass), rest)
            counts[i] = counts[i] + addition
            rest = rest - addition
    return np.array(counts)


def noise(stream_key, shape, scale, most, cuts=(), kind=jnp.bfloat16):
    gain = steps_of(stream_key, shape, cuts, -0.22, 0.18) if cuts else 1.0
    array = jax.random.normal(stream_key, shape, jnp.float32) * scale * gain
    return jnp.minimum(jnp.maximum(array, -most), most).astype(kind)


def setup_inputs(seed: int = 0) -> dict:
    splits = jax.random.split(jax.random.key(seed), 16)
    x_resid = noise(splits[0], (SEQS, NEW, D), 0.25, 1.5, ((0, 32),))
    q_latent = noise(splits[1], (SEQS, NEW, H, LAT), 0.5, 3.0, ((0, 32),))
    q_rope = draw_q_rope(jax.random.fold_in(splits[15], 71), 0)
    cache_latent = noise(splits[3], (SEQS, CACHE, LAT), 1.0, 6.0, ((0, 32),))
    cache_rope = draw_cache_rope(jax.random.fold_in(splits[15], 71), 0)
    new_latent = noise(splits[5], (SEQS, NEW, LAT), 1.0, 6.0, ((0, 32),))
    new_rope = noise(splits[6], (SEQS, NEW, DR), 1.0, 6.0, ((0, 32),))
    w_uv = noise(splits[7], (LAT, H, DV), LAT ** -0.5, 0.25, ((0, 2),))
    w_out = noise(splits[8], (H * DV, D), (H * DV) ** -0.5, 0.1875, ((0, 2),))
    norm_gain = jnp.clip(jnp.exp(jax.random.uniform(splits[9], (D,), jnp.float32, math.log(0.5), math.log(2.0))), 0.5, 2.0)
    router = draw_router(jax.random.fold_in(splits[15], 71), 0)
    expert_ids_keys = jax.random.split(jax.random.fold_in(splits[11], 1), SEQS * NEW // NEW)
    expert_ids_turns = jax.random.permutation(jax.random.fold_in(splits[11], 3), SEQS * NEW // NEW)
    expert_ids = jax.vmap(lambda own, number: routed_block(jax.random.fold_in(splits[11], 2), own, number, NEW, EXPERTS, TOPK, CAP, 0))(expert_ids_keys, expert_ids_turns).reshape((SEQS, NEW, TOPK))
    w_gate = noise(splits[12], (EXPERTS, D, FFE), D ** -0.5, 0.125, ((0, 16),))
    w_up = noise(splits[13], (EXPERTS, D, FFE), D ** -0.5, 0.125, ((0, 16),))
    w_down = noise(splits[14], (EXPERTS, FFE, D), FFE ** -0.5, 0.21875, ((0, 16),))
    return {"x_resid": x_resid, "q_latent": q_latent, "q_rope": q_rope, "cache_latent": cache_latent, "cache_rope": cache_rope, "new_latent": new_latent, "new_rope": new_rope, "w_uv": w_uv, "w_out": w_out, "norm_gain": norm_gain, "router": router, "expert_ids": expert_ids, "w_gate": w_gate, "w_up": w_up, "w_down": w_down}


softmax_scale = 0.07216878364870323
epsilon = 1e-06

def attend_sequence(q_latent, q_rope, cache_latent, cache_rope, new_latent, new_rope):
    new_count, head_count, latent_width = q_latent.shape
    cache_count = cache_latent.shape[0]
    keys_latent = jnp.concatenate([cache_latent, new_latent], 0)
    keys_rope = jnp.concatenate([cache_rope, new_rope], 0)
    query_rows = q_latent.reshape(new_count * head_count, latent_width)
    rope_rows = q_rope.reshape(new_count * head_count, q_rope.shape[2])
    scores = jnp.dot(query_rows, keys_latent.T, preferred_element_type=jnp.float32)
    scores = (scores + jnp.dot(rope_rows, keys_rope.T, preferred_element_type=jnp.float32)) * softmax_scale
    token_of_row = jnp.arange(new_count * head_count, dtype=jnp.int32) // head_count
    key_index = jnp.arange(keys_latent.shape[0], dtype=jnp.int32)
    visible = key_index[None, :] <= token_of_row[:, None] + cache_count
    row_top = lax.optimization_barrier(jnp.max(jnp.where(visible, scores, -jnp.inf), axis=1, keepdims=True))
    exponent = jnp.where(visible, jnp.exp(scores - row_top), 0.0)
    weights_att = (exponent / lax.optimization_barrier(jnp.sum(exponent, axis=1, keepdims=True))).astype(jnp.bfloat16)
    mixed_latent = jnp.dot(weights_att, keys_latent, preferred_element_type=jnp.float32).astype(jnp.bfloat16)
    return mixed_latent.reshape(new_count, head_count, latent_width)

def before_experts(x_resid, q_latent, q_rope, cache_latent, cache_rope, new_latent, new_rope, expert_ids, w_uv, w_out, norm_gain, router):
    mixed_latent = attend_sequence(q_latent, q_rope, cache_latent, cache_rope, new_latent, new_rope)
    heads_out = jnp.einsum('thl,lhv->thv', mixed_latent.astype(jnp.float32), w_uv.astype(jnp.float32)).astype(jnp.bfloat16)
    heads_flat = heads_out.reshape(mixed_latent.shape[0], -1)
    hidden = x_resid.astype(jnp.float32) + jnp.dot(heads_flat, w_out, preferred_element_type=jnp.float32)
    normed = hidden * lax.rsqrt(lax.optimization_barrier(jnp.mean(hidden * hidden, axis=-1, keepdims=True)) + epsilon)
    normed = (normed * norm_gain.astype(jnp.float32)).astype(jnp.bfloat16)
    logits = jnp.dot(normed, router, preferred_element_type=jnp.float32)
    choose = (expert_ids[..., None] == jnp.arange(EXPERTS, dtype=jnp.int32)).astype(jnp.float32)
    picked = lax.optimization_barrier(jnp.sum(choose * logits[:, None, :], axis=-1))
    gate_weights = jax.nn.softmax(picked, axis=-1)
    assigned = choose.reshape(-1, EXPERTS)
    earlier = jnp.cumsum(assigned, axis=0) - assigned
    slot_index = lax.optimization_barrier(jnp.sum(earlier * assigned, axis=-1)).reshape(expert_ids.shape).astype(jnp.int32)
    return (hidden, normed, gate_weights, slot_index)

def reference(x_resid, q_latent, q_rope, cache_latent, cache_rope, new_latent, new_rope, w_uv, w_out, norm_gain, router, expert_ids, w_gate, w_up, w_down):

    def per_sequence(inputs_seq):
        return before_experts(*inputs_seq, w_uv, w_out, norm_gain, router)
    hidden, normed, gate_weights, slot_index = lax.map(per_sequence, (x_resid, q_latent, q_rope, cache_latent, cache_rope, new_latent, new_rope, expert_ids))
    normed_wide = normed.astype(jnp.float32)
    slot_range = jnp.arange(CAP, dtype=jnp.int32)

    def one_expert(running, inputs_exp):
        gate_w, up_w, down_w, expert = inputs_exp
        is_mine = expert_ids == expert
        matched = (is_mine[..., None] & (slot_index[..., None] == slot_range)).astype(jnp.float32)
        placement_map = lax.optimization_barrier(jnp.sum(matched, axis=2))
        buffers = jnp.einsum('stc,std->scd', placement_map, normed_wide).astype(jnp.bfloat16)
        buffer_rows = buffers.reshape(-1, buffers.shape[2])
        gate_proj = jnp.dot(buffer_rows, gate_w, preferred_element_type=jnp.float32)
        up_proj = jnp.dot(buffer_rows, up_w, preferred_element_type=jnp.float32)
        activated = (jax.nn.silu(gate_proj) * up_proj).astype(jnp.bfloat16)
        result = jnp.dot(activated, down_w, preferred_element_type=jnp.float32).astype(jnp.bfloat16).reshape(buffers.shape)
        combine_weight = lax.optimization_barrier(jnp.sum(matched * gate_weights[..., None], axis=2))
        return (running + jnp.einsum('stc,scd->std', combine_weight, result.astype(jnp.float32)), None)
    routed_sum, _ = lax.scan(one_expert, jnp.zeros(hidden.shape, jnp.float32), (w_gate, w_up, w_down, jnp.arange(EXPERTS, dtype=jnp.int32)))
    return (hidden.astype(jnp.bfloat16), (hidden + routed_sum).astype(jnp.bfloat16))
```

```python
import jax
import jax.numpy as jnp
from jax import lax
from jax.sharding import PartitionSpec as P

softmax_scale = 0.07216878364870323
epsilon = 1e-06


def attend_local(q_latent, q_rope, cache_latent, cache_rope, new_latent, new_rope):
    new_count, head_count, latent_width = q_latent.shape
    cache_count = cache_latent.shape[0]
    keys_latent = jnp.concatenate([cache_latent, new_latent], 0)
    keys_rope = jnp.concatenate([cache_rope, new_rope], 0)
    query_rows = q_latent.reshape(new_count * head_count, latent_width)
    rope_rows = q_rope.reshape(new_count * head_count, q_rope.shape[2])
    scores = jnp.dot(query_rows, keys_latent.T, preferred_element_type=jnp.float32)
    scores = (
        scores + jnp.dot(rope_rows, keys_rope.T, preferred_element_type=jnp.float32)
    ) * softmax_scale
    token_of_row = jnp.arange(new_count * head_count, dtype=jnp.int32) // head_count
    key_index = jnp.arange(keys_latent.shape[0], dtype=jnp.int32)
    visible = key_index[None, :] <= token_of_row[:, None] + cache_count
    row_top = jnp.max(jnp.where(visible, scores, -jnp.inf), axis=1, keepdims=True)
    exponent = jnp.where(visible, jnp.exp(scores - row_top), 0.0)
    weights_att = (exponent / jnp.sum(exponent, axis=1, keepdims=True)).astype(jnp.bfloat16)
    mixed_latent = jnp.dot(weights_att, keys_latent, preferred_element_type=jnp.float32).astype(
        jnp.bfloat16
    )
    return mixed_latent.reshape(new_count, head_count, latent_width)


def up_project(mixed_latent, w_uv):
    heads_out = jnp.einsum(
        "thl,lhv->thv", mixed_latent, w_uv, preferred_element_type=jnp.float32
    )
    return heads_out.astype(jnp.bfloat16).reshape(mixed_latent.shape[0], -1)


def project_gathered(mixed_latent, w_uv, w_out):
    heads_flat = up_project(mixed_latent, lax.all_gather(w_uv, "fsdp", axis=0, tiled=True))
    column_width = w_out.shape[1] // lax.axis_size("ep")
    own_columns = lax.dynamic_slice_in_dim(
        w_out, lax.axis_index("ep") * column_width, column_width, 1
    )
    column_block = lax.all_gather(own_columns, "fsdp", axis=0, tiled=True)
    return jnp.dot(
        heads_flat,
        lax.all_gather(column_block, "ep", axis=1, tiled=True),
        preferred_element_type=jnp.float32,
    )


def project_paired(mixed_latent, w_uv, w_out):
    pair = [(0, 1), (1, 0)]
    ep = lax.axis_size("ep")
    twins = [(i, i ^ 1) for i in range(ep)]
    side = lax.axis_index("fsdp")
    lane = lax.axis_index("ep") % 2
    rows = w_uv.shape[0] // 2
    mine = lax.ppermute(
        lax.dynamic_slice_in_dim(w_uv, lane * rows, rows, 0), "fsdp", pair
    )
    theirs = lax.ppermute(mine, "ep", twins)
    far = jnp.where(
        lane == 0, jnp.concatenate([mine, theirs], 0), jnp.concatenate([theirs, mine], 0)
    )
    full = jnp.where(side == 0, jnp.concatenate([w_uv, far], 0), jnp.concatenate([far, w_uv], 0))
    heads_flat = up_project(mixed_latent, full)
    width = w_out.shape[0]
    count = heads_flat.shape[0]
    keep = lax.dynamic_slice_in_dim(heads_flat, side * width, width, 1)
    give = lax.dynamic_slice_in_dim(heads_flat, (1 - side) * width, width, 1)
    other = lax.ppermute(give, "fsdp", pair)
    both = jnp.dot(
        jnp.concatenate([other, keep], 0), w_out, preferred_element_type=jnp.float32
    )
    back = lax.ppermute(both[:count].astype(jnp.bfloat16), "fsdp", pair)
    return both[count:] + back.astype(jnp.float32)


def per_device(
    x_resid,
    q_latent,
    q_rope,
    cache_latent,
    cache_rope,
    new_latent,
    new_rope,
    w_uv,
    w_out,
    norm_gain,
    router,
    expert_ids,
    w_gate,
    w_up,
    w_down,
):
    mixed_latent = attend_local(
        q_latent[0], q_rope[0], cache_latent[0], cache_rope[0], new_latent[0], new_rope[0]
    )
    new_count = mixed_latent.shape[0]
    paired = lax.axis_size("fsdp") == 2 and lax.axis_size("ep") % 2 == 0
    project = project_paired if paired else project_gathered
    projected = project(mixed_latent, w_uv, w_out)
    hidden = x_resid[0].astype(jnp.float32) + projected
    normed = hidden * lax.rsqrt(jnp.mean(hidden * hidden, axis=-1, keepdims=True) + epsilon)
    normed = (normed * norm_gain).astype(jnp.bfloat16)
    logits = jnp.dot(normed, router, preferred_element_type=jnp.float32)
    expert_count = lax.axis_size("ep")
    top_count = expert_ids.shape[2]
    capacity = new_count * top_count // expert_count
    own_ids = expert_ids[0]
    choose = (own_ids[..., None] == jnp.arange(expert_count, dtype=jnp.int32)).astype(jnp.float32)
    picked = jnp.sum(choose * logits[:, None, :], axis=-1)
    gate_weights = jax.nn.softmax(picked, axis=-1)
    assigned = choose.reshape(-1, expert_count)
    earlier = jnp.cumsum(assigned, axis=0) - assigned
    slot_index = jnp.sum(earlier * assigned, axis=-1).reshape(own_ids.shape).astype(jnp.int32)
    target = own_ids * capacity + slot_index
    here = target[..., None] == jnp.arange(expert_count * capacity, dtype=jnp.int32)
    placed = jnp.sum(here.astype(jnp.bfloat16), axis=1)
    combine = jnp.sum(jnp.where(here, gate_weights[..., None], 0.0), axis=1)
    buffers = jnp.einsum("tp,td->pd", placed, normed, preferred_element_type=jnp.float32).astype(
        jnp.bfloat16
    )
    buffers = buffers.reshape(expert_count, capacity, -1)
    received = lax.all_to_all(buffers, "ep", split_axis=0, concat_axis=0, tiled=True)
    source_count, slot_count, width = received.shape
    buffer_rows = received.reshape(source_count * slot_count, width)
    gate_proj = jnp.dot(buffer_rows, w_gate[0], preferred_element_type=jnp.float32)
    up_proj = jnp.dot(buffer_rows, w_up[0], preferred_element_type=jnp.float32)
    activated = (jax.nn.silu(gate_proj) * up_proj).astype(jnp.bfloat16)
    result = jnp.dot(activated, w_down[0], preferred_element_type=jnp.float32).astype(jnp.bfloat16)
    result = result.reshape(source_count, slot_count, width)
    returned = lax.all_to_all(result, "ep", split_axis=0, concat_axis=0, tiled=True)
    returned_rows = returned.reshape(expert_count * capacity, -1)
    high = combine.astype(jnp.bfloat16)
    low = (combine - high.astype(jnp.float32)).astype(jnp.bfloat16)
    routed_sum = jnp.dot(high, returned_rows, preferred_element_type=jnp.float32) + jnp.dot(
        low, returned_rows, preferred_element_type=jnp.float32
    )
    return (hidden.astype(jnp.bfloat16)[None], (hidden + routed_sum).astype(jnp.bfloat16)[None])


def solution(mesh):
    placed = (
        P(("fsdp", "ep"), None, None),
        P(("fsdp", "ep"), None, None, None),
        P(("fsdp", "ep"), None, None, None),
        P(("fsdp", "ep"), None, None),
        P(("fsdp", "ep"), None, None),
        P(("fsdp", "ep"), None, None),
        P(("fsdp", "ep"), None, None),
        P("fsdp", None, None),
        P("fsdp", None),
        P(),
        P(),
        P(("fsdp", "ep"), None, None),
        P("ep", None, None),
        P("ep", None, None),
        P("ep", None, None),
    )
    return jax.shard_map(
        per_device,
        mesh=mesh,
        in_specs=placed,
        out_specs=(P(("fsdp", "ep"), None, None), P(("fsdp", "ep"), None, None)),
        check_vma=False,
    )
```

```python
import functools

import jax
import jax.numpy as jnp
from jax import lax
from jax.experimental import pallas as pl
from jax.experimental.pallas import tpu as pltpu
from jax.sharding import PartitionSpec as P

softmax_scale = 0.07216878364870323
epsilon = 1e-06


def attend_local(q_latent, q_rope, cache_latent, cache_rope, new_latent, new_rope):
    new_count, head_count, latent_width = q_latent.shape
    cache_count = cache_latent.shape[0]
    keys_latent = jnp.concatenate([cache_latent, new_latent], 0)
    keys_rope = jnp.concatenate([cache_rope, new_rope], 0)
    query_rows = q_latent.reshape(new_count * head_count, latent_width)
    rope_rows = q_rope.reshape(new_count * head_count, q_rope.shape[2])
    scores = jnp.dot(query_rows, keys_latent.T, preferred_element_type=jnp.float32)
    scores = (
        scores + jnp.dot(rope_rows, keys_rope.T, preferred_element_type=jnp.float32)
    ) * softmax_scale
    token_of_row = jnp.arange(new_count * head_count, dtype=jnp.int32) // head_count
    key_index = jnp.arange(keys_latent.shape[0], dtype=jnp.int32)
    visible = key_index[None, :] <= token_of_row[:, None] + cache_count
    row_top = jnp.max(jnp.where(visible, scores, -jnp.inf), axis=1, keepdims=True)
    exponent = jnp.where(visible, jnp.exp(scores - row_top), 0.0)
    weights_att = (exponent / jnp.sum(exponent, axis=1, keepdims=True)).astype(jnp.bfloat16)
    mixed_latent = jnp.dot(weights_att, keys_latent, preferred_element_type=jnp.float32).astype(
        jnp.bfloat16
    )
    return mixed_latent.reshape(new_count, head_count, latent_width)


def up_project(mixed_latent, w_uv):
    heads_out = jnp.einsum(
        "thl,lhv->thv", mixed_latent, w_uv, preferred_element_type=jnp.float32
    )
    return heads_out.astype(jnp.bfloat16).reshape(mixed_latent.shape[0], -1)


def project_gathered(mixed_latent, w_uv, w_out):
    heads_flat = up_project(mixed_latent, lax.all_gather(w_uv, "fsdp", axis=0, tiled=True))
    column_width = w_out.shape[1] // lax.axis_size("ep")
    own_columns = lax.dynamic_slice_in_dim(
        w_out, lax.axis_index("ep") * column_width, column_width, 1
    )
    column_block = lax.all_gather(own_columns, "fsdp", axis=0, tiled=True)
    return jnp.dot(
        heads_flat,
        lax.all_gather(column_block, "ep", axis=1, tiled=True),
        preferred_element_type=jnp.float32,
    )


def project_paired(mixed_latent, w_uv, w_out):
    pair = [(0, 1), (1, 0)]
    ep = lax.axis_size("ep")
    twins = [(i, i ^ 1) for i in range(ep)]
    side = lax.axis_index("fsdp")
    lane = lax.axis_index("ep") % 2
    rows = w_uv.shape[0] // 2
    mine = lax.ppermute(
        lax.dynamic_slice_in_dim(w_uv, lane * rows, rows, 0), "fsdp", pair
    )
    theirs = lax.ppermute(mine, "ep", twins)
    far = jnp.where(
        lane == 0, jnp.concatenate([mine, theirs], 0), jnp.concatenate([theirs, mine], 0)
    )
    full = jnp.where(side == 0, jnp.concatenate([w_uv, far], 0), jnp.concatenate([far, w_uv], 0))
    heads_flat = up_project(mixed_latent, full)
    width = w_out.shape[0]
    count = heads_flat.shape[0]
    keep = lax.dynamic_slice_in_dim(heads_flat, side * width, width, 1)
    give = lax.dynamic_slice_in_dim(heads_flat, (1 - side) * width, width, 1)
    other = lax.ppermute(give, "fsdp", pair)
    both = jnp.dot(
        jnp.concatenate([other, keep], 0), w_out, preferred_element_type=jnp.float32
    )
    back = lax.ppermute(both[:count].astype(jnp.bfloat16), "fsdp", pair)
    return both, back


def experts(rows, w_gate, w_up, w_down):
    gate_proj = jnp.dot(rows, w_gate, preferred_element_type=jnp.float32)
    up_proj = jnp.dot(rows, w_up, preferred_element_type=jnp.float32)
    activated = (jax.nn.silu(gate_proj) * up_proj).astype(jnp.bfloat16)
    return jnp.dot(activated, w_down, preferred_element_type=jnp.float32).astype(jnp.bfloat16)


def slots_of(own_ids, expert_count, capacity):
    choose = (own_ids[..., None] == jnp.arange(expert_count, dtype=jnp.int32)).astype(jnp.float32)
    assigned = choose.reshape(-1, expert_count)
    earlier = jnp.cumsum(assigned, axis=0) - assigned
    slot_index = jnp.sum(earlier * assigned, axis=-1).reshape(own_ids.shape).astype(jnp.int32)
    return own_ids * capacity + slot_index


def gates_of(normed, router, ids):
    logits = jnp.dot(normed, router, preferred_element_type=jnp.float32)
    choose = ids[..., None] == jnp.arange(router.shape[1], dtype=jnp.int32)
    picked = jnp.sum(jnp.where(choose, logits[:, None, :], 0.0), axis=-1)
    return jax.nn.softmax(picked, axis=-1)


def weighted_rows(weights, rows):
    high = weights.astype(jnp.bfloat16)
    low = (weights - high.astype(jnp.float32)).astype(jnp.bfloat16)
    return jnp.dot(
        jnp.concatenate([high, low], 1),
        jnp.concatenate([rows, rows], 0),
        preferred_element_type=jnp.float32,
    )


def routed_exchanged(normed, target, capacity, router, w_gate, w_up, w_down):
    expert_count = lax.axis_size("ep")
    gate_weights = gates_of(normed, router, target // capacity)
    here = target[..., None] == jnp.arange(expert_count * capacity, dtype=jnp.int32)
    placed = jnp.sum(here.astype(jnp.bfloat16), axis=1)
    combine = jnp.sum(jnp.where(here, gate_weights[..., None], 0.0), axis=1)
    buffers = jnp.einsum("tp,td->pd", placed, normed, preferred_element_type=jnp.float32).astype(
        jnp.bfloat16
    )
    buffers = buffers.reshape(expert_count, capacity, -1)
    received = lax.all_to_all(buffers, "ep", split_axis=0, concat_axis=0, tiled=True)
    result = experts(received.reshape(expert_count * capacity, -1), w_gate, w_up, w_down)
    result = result.reshape(expert_count, capacity, -1)
    returned = lax.all_to_all(result, "ep", split_axis=0, concat_axis=0, tiled=True)
    return weighted_rows(combine, returned.reshape(expert_count * capacity, -1))


def fused(body, outs, *args, scratch=(), flops=0, bytes_accessed=0):
    whole = pl.BlockSpec(memory_space=pltpu.VMEM)
    return pl.pallas_call(
        body,
        out_shape=[jax.ShapeDtypeStruct(shape, dtype) for shape, dtype in outs],
        in_specs=[whole] * len(args),
        out_specs=[whole] * len(outs),
        scratch_shapes=list(scratch),
        cost_estimate=pl.CostEstimate(
            flops=flops, bytes_accessed=bytes_accessed, transcendentals=0
        ),
    )(*args)


def slot_kernel(expert_count, capacity, ids_ref, target_ref):
    ids = ids_ref[...]
    top, count = ids.shape
    level = lax.broadcasted_iota(jnp.int32, (expert_count, count), 0)
    chosen = jnp.zeros((expert_count, count), jnp.float32)
    for k in range(top):
        chosen += (ids[k : k + 1] == level).astype(jnp.float32)
    rows = lax.broadcasted_iota(jnp.int32, (count, count), 0)
    columns = lax.broadcasted_iota(jnp.int32, (count, count), 1)
    ahead = (rows < columns).astype(jnp.float32).astype(jnp.bfloat16)
    earlier = jnp.dot(chosen.astype(jnp.bfloat16), ahead, preferred_element_type=jnp.float32)
    for k in range(top):
        own = ids[k : k + 1]
        slot = jnp.sum(jnp.where(own == level, earlier, 0.0), axis=0, keepdims=True)
        target_ref[k : k + 1] = own * capacity + slot.astype(jnp.int32)


def matches(target, capacity, place):
    top, count = target.shape
    row = lax.broadcasted_iota(jnp.int32, (4 * capacity, count), 0)
    slot = jnp.zeros_like(row)
    for j in range(4):
        inside = (row >= j * capacity) & (row < (j + 1) * capacity)
        slot = jnp.where(inside, (place ^ j) * capacity + row - j * capacity, slot)
    found = jnp.zeros(row.shape, jnp.float32)
    for k in range(top):
        found += (target[k : k + 1] == slot).astype(jnp.float32)
    return found


def pick_kernel(capacity, sources, *refs):
    place = lax.axis_index("ep")
    half = refs[1].shape[1]
    out = refs[3 * sources :]
    for n in range(sources):
        target_ref, low_ref, high_ref = refs[3 * n : 3 * n + 3]
        found = matches(target_ref[...], capacity, place).astype(jnp.bfloat16)
        for part, ref in enumerate((low_ref, high_ref)):
            rows = jnp.dot(found, ref[...], preferred_element_type=jnp.float32)
            rows = rows.astype(jnp.bfloat16)
            for j in range(4):
                out[j][
                    n * capacity : (n + 1) * capacity, part * half : (part + 1) * half
                ] = rows[j * capacity : (j + 1) * capacity]


def dot_rows(a, b):
    return lax.dot_general(a, b, (((1,), (1,)), ((), ())), preferred_element_type=jnp.float32)


def gate_kernel(capacity, router_ref, *refs):
    place = lax.axis_index("ep")
    expert_count = router_ref.shape[0]
    out = refs[12:]
    half = refs[1].shape[1]
    for n in range(4):
        target_ref, low_ref, high_ref = refs[3 * n : 3 * n + 3]
        target = target_ref[...]
        top, count = target.shape
        logits = dot_rows(router_ref[:, :half], low_ref[...])
        logits += dot_rows(router_ref[:, half:], high_ref[...])
        level = lax.broadcasted_iota(jnp.int32, (expert_count, count), 0)
        first = level * capacity
        chosen = jnp.zeros((expert_count, count), jnp.float32)
        for k in range(top):
            own = target[k : k + 1]
            chosen += ((own >= first) & (own < first + capacity)).astype(jnp.float32)
        inside = chosen > 0
        peak = jnp.max(jnp.where(inside, logits, -jnp.inf), axis=0, keepdims=True)
        power = jnp.where(inside, jnp.exp(logits - peak), 0.0)
        gate = power / jnp.sum(power, axis=0, keepdims=True)
        found = matches(target, capacity, place)
        row = lax.broadcasted_iota(jnp.int32, found.shape, 0)
        for j in range(4):
            own = jnp.sum(jnp.where(level == (place ^ j), gate, 0.0), axis=0, keepdims=True)
            within = (row >= j * capacity) & (row < (j + 1) * capacity)
            found = jnp.where(within, found * own, found)
        out[n][...] = found.T


def norm_kernel(x_ref, both_ref, back_ref, gain_ref, hidden_ref, attended_ref, low_ref, high_ref):
    count, width = hidden_ref.shape
    hidden = x_ref[0].astype(jnp.float32) + (
        both_ref[count:] + back_ref[...].astype(jnp.float32)
    )
    hidden_ref[...] = hidden
    attended_ref[0] = hidden.astype(jnp.bfloat16)
    square = jnp.mean(hidden * hidden, axis=-1, keepdims=True)
    normed = hidden * lax.rsqrt(square + epsilon) * gain_ref[...]
    low_ref[...] = normed[:, : width // 2].astype(jnp.bfloat16)
    high_ref[...] = normed[:, width // 2 :].astype(jnp.bfloat16)


def expert_kernel(groups, *refs):
    n = 4 * len(groups)
    gate_hbm, up_hbm, down_hbm = refs[n : n + 3]
    outs = refs[n + 3 : 2 * n + 3]
    rows_ref, gate_ref, up_ref, down_ref, sem = refs[2 * n + 3 :]
    copies = [
        pltpu.make_async_copy(source.at[0], target, sem.at[i])
        for i, (source, target) in enumerate(
            ((gate_hbm, gate_ref), (up_hbm, up_ref), (down_hbm, down_ref))
        )
    ]
    for copy in copies:
        copy.start()
    offset = 0
    for ref in refs[:n]:
        rows_ref[offset : offset + ref.shape[0]] = ref[...]
        offset += ref.shape[0]
    copies[0].wait()
    gate = dot_rows(rows_ref[...], gate_ref[...])
    copies[1].wait()
    up = dot_rows(rows_ref[...], up_ref[...])
    active = (gate / (1.0 + jnp.exp(-gate)) * up).astype(jnp.bfloat16)
    copies[2].wait()
    result = jnp.dot(active, down_ref[...], preferred_element_type=jnp.float32)
    result = result.astype(jnp.bfloat16)
    offset = 0
    for ref in outs:
        ref[...] = result[offset : offset + ref.shape[0]]
        offset += ref.shape[0]


def weigh(weights, rows):
    high = weights.astype(jnp.bfloat16)
    low = (weights - high.astype(jnp.float32)).astype(jnp.bfloat16)
    return jnp.dot(high, rows, preferred_element_type=jnp.float32) + jnp.dot(
        low, rows, preferred_element_type=jnp.float32
    )


def far_kernel(weights_ref, r0, r1, r2, r3, low_ref, high_ref):
    rows = jnp.concatenate([r[...] for r in (r0, r1, r2, r3)], 0)
    total = weigh(weights_ref[...], rows)
    half = low_ref.shape[1]
    low_ref[...] = total[:, :half].astype(jnp.bfloat16)
    high_ref[...] = total[:, half:].astype(jnp.bfloat16)


def near_kernel(
    capacity, before_w, after_w, r0, r1, r2, r3, add_low, add_high, before_ref, after_ref
):
    half = add_low.shape[1]
    blocks = (r0, r1, r2, r3)
    rows = jnp.concatenate([r[:capacity] for r in blocks], 0)
    total = weigh(before_w[...], rows)
    before_ref[:, :half] = total[:, :half].astype(jnp.bfloat16)
    before_ref[:, half:] = (total[:, half:] + add_high[...].astype(jnp.float32)).astype(
        jnp.bfloat16
    )
    rows = jnp.concatenate([r[capacity:] for r in blocks], 0)
    total = weigh(after_w[...], rows)
    after_ref[:, :half] = (total[:, :half] + add_low[...].astype(jnp.float32)).astype(
        jnp.bfloat16
    )
    after_ref[:, half:] = total[:, half:].astype(jnp.bfloat16)


def last_kernel(hidden_ref, weights_ref, r0, r1, r2, r3, x_ref, y_ref, out_ref):
    rows = jnp.concatenate([r[...] for r in (r0, r1, r2, r3)], 0)
    total = weigh(weights_ref[...], rows)
    total = total + x_ref[...].astype(jnp.float32) + y_ref[...].astype(jnp.float32)
    out_ref[...] = (hidden_ref[...] + total).astype(jnp.bfloat16)


def routed_ringed(hidden, low, high, targets, capacity, router, w_gate, w_up, w_down):
    onward, backward = ring_steps()
    traded = [[(i, i ^ j) for i in range(16)] for j in range(4)]
    count, half = low.shape
    width = 2 * half
    bf16 = jnp.bfloat16

    def send(value, steps):
        return lax.ppermute(value, "ep", steps)

    def pick(*sources):
        n = len(sources)
        return fused(
            functools.partial(pick_kernel, capacity, n),
            [((n * capacity, width), bf16)] * 4,
            *[part for source in sources for part in source],
            flops=n * 2 * 4 * capacity * count * width,
            bytes_accessed=n * 4 * width * (count + 4 * capacity),
        )

    def trade(blocks):
        return [blocks[0]] + [send(blocks[j], traded[j]) for j in (1, 2, 3)]

    before_low, after_high = send(low, onward), send(high, backward)
    before_high, after_low = send(high, onward), send(low, backward)
    own = (targets[0], low, high)
    own_rows = trade(pick(own))
    far_low, far_high = send(before_low, onward), send(after_high, backward)
    before = (targets[1], before_low, before_high)
    after = (targets[2], after_low, after_high)
    near_rows = trade(pick(before, after))
    far = (targets[3], far_low, far_high)
    far_rows = trade(pick(far))
    slots = (count, 4 * capacity)
    weights = fused(
        functools.partial(gate_kernel, capacity),
        [(slots, jnp.float32)] * 4,
        router.T,
        *own,
        *before,
        *after,
        *far,
        flops=8 * count * width * 16,
        bytes_accessed=16 * count * width,
    )
    blocks = far_rows + near_rows + own_rows
    hbm = pl.BlockSpec(memory_space=pl.ANY)
    whole = pl.BlockSpec(memory_space=pltpu.VMEM)
    hidden_width = w_gate.shape[2]
    total = 16 * capacity
    result = pl.pallas_call(
        functools.partial(expert_kernel, (1, 2, 1)),
        out_shape=[jax.ShapeDtypeStruct(b.shape, bf16) for b in blocks],
        in_specs=[whole] * 12 + [hbm] * 3,
        out_specs=[whole] * 12,
        scratch_shapes=[
            pltpu.VMEM((total, width), bf16),
            pltpu.VMEM((hidden_width, width), bf16),
            pltpu.VMEM((hidden_width, width), bf16),
            pltpu.VMEM((hidden_width, width), bf16),
            pltpu.SemaphoreType.DMA((3,)),
        ],
        cost_estimate=pl.CostEstimate(
            flops=6 * total * width * hidden_width,
            bytes_accessed=6 * width * hidden_width + 4 * total * width,
            transcendentals=0,
        ),
    )(*blocks, jnp.swapaxes(w_gate, 1, 2), jnp.swapaxes(w_up, 1, 2), w_down)
    spent = 2 * 4 * 4 * capacity * count * width
    moved = 4 * width * (count + 4 * capacity)
    far_low, far_high = fused(
        far_kernel,
        [((count, half), bf16)] * 2,
        weights[3],
        *trade(result[:4]),
        flops=spent,
        bytes_accessed=moved,
    )
    add_low, add_high = send(far_low, onward), send(far_high, backward)
    before_sum, after_sum = fused(
        functools.partial(near_kernel, capacity),
        [((count, width), bf16)] * 2,
        weights[1],
        weights[2],
        *trade(result[4:8]),
        add_low,
        add_high,
        flops=2 * spent,
        bytes_accessed=2 * moved,
    )
    from_before = send(after_sum, onward)
    from_after = send(before_sum, backward)
    return fused(
        last_kernel,
        [((count, width), bf16)],
        hidden,
        weights[0],
        *trade(result[8:]),
        from_before,
        from_after,
        flops=spent,
        bytes_accessed=2 * moved,
    )[0]


def ring_steps():
    order = (0, 1, 3, 2)
    onward = [
        (order[i] * 4 + j, order[(i + 1) % 4] * 4 + j) for i in range(4) for j in range(4)
    ]
    return onward, [(b, a) for a, b in onward]


def per_device(
    x_resid,
    q_latent,
    q_rope,
    cache_latent,
    cache_rope,
    new_latent,
    new_rope,
    w_uv,
    w_out,
    norm_gain,
    router,
    expert_ids,
    w_gate,
    w_up,
    w_down,
):
    mixed_latent = attend_local(
        q_latent[0], q_rope[0], cache_latent[0], cache_rope[0], new_latent[0], new_rope[0]
    )
    new_count = mixed_latent.shape[0]
    expert_count = lax.axis_size("ep")
    capacity = new_count * expert_ids.shape[2] // expert_count
    if lax.axis_size("fsdp") != 2 or expert_count != 16:
        projected = project_gathered(mixed_latent, w_uv, w_out)
        hidden = x_resid[0].astype(jnp.float32) + projected
        normed = hidden * lax.rsqrt(jnp.mean(hidden * hidden, axis=-1, keepdims=True) + epsilon)
        normed = (normed * norm_gain).astype(jnp.bfloat16)
        target = slots_of(expert_ids[0], expert_count, capacity)
        routed_sum = routed_exchanged(
            normed, target, capacity, router, w_gate[0], w_up[0], w_down[0]
        )
        layer_out = (hidden + routed_sum).astype(jnp.bfloat16)
        return (hidden.astype(jnp.bfloat16)[None], layer_out[None])
    onward, backward = ring_steps()
    own = fused(
        functools.partial(slot_kernel, expert_count, capacity),
        [(expert_ids.shape[:0:-1], jnp.int32)],
        expert_ids[0].T,
    )[0]
    before = lax.ppermute(own, "ep", onward)
    after = lax.ppermute(own, "ep", backward)
    far = lax.ppermute(before, "ep", onward)
    both, back = project_paired(mixed_latent, w_uv, w_out)
    back, before, after, far = lax.optimization_barrier((back, before, after, far))
    width = both.shape[1]
    halves = (new_count, width // 2)
    hidden, attended, low, high = fused(
        norm_kernel,
        [
            ((new_count, width), jnp.float32),
            ((1, new_count, width), jnp.bfloat16),
            (halves, jnp.bfloat16),
            (halves, jnp.bfloat16),
        ],
        x_resid,
        both,
        back,
        norm_gain[None],
        flops=8 * new_count * width,
        bytes_accessed=20 * new_count * width,
    )
    targets = (own, before, after, far)
    layer_out = routed_ringed(
        hidden, low, high, targets, capacity, router, w_gate, w_up, w_down
    )
    return (attended, layer_out[None])


def solution(mesh):
    placed = (
        P(("fsdp", "ep"), None, None),
        P(("fsdp", "ep"), None, None, None),
        P(("fsdp", "ep"), None, None, None),
        P(("fsdp", "ep"), None, None),
        P(("fsdp", "ep"), None, None),
        P(("fsdp", "ep"), None, None),
        P(("fsdp", "ep"), None, None),
        P("fsdp", None, None),
        P("fsdp", None),
        P(),
        P(),
        P(("fsdp", "ep"), None, None),
        P("ep", None, None),
        P("ep", None, None),
        P("ep", None, None),
    )
    return jax.shard_map(
        per_device,
        mesh=mesh,
        in_specs=placed,
        out_specs=(P(("fsdp", "ep"), None, None), P(("fsdp", "ep"), None, None)),
        check_vma=False,
    )
```

```python
import functools

import jax
import jax.numpy as jnp
from jax import lax
from jax.experimental import pallas as pl
from jax.experimental.pallas import tpu as pltpu
from jax.sharding import PartitionSpec as P

softmax_scale = 0.07216878364870323
epsilon = 1e-06


def attend_local(q_latent, q_rope, cache_latent, cache_rope, new_latent, new_rope):
    new_count, head_count, latent_width = q_latent.shape
    cache_count = cache_latent.shape[0]
    keys_latent = jnp.concatenate([cache_latent, new_latent], 0)
    keys_rope = jnp.concatenate([cache_rope, new_rope], 0)
    query_rows = q_latent.reshape(new_count * head_count, latent_width)
    rope_rows = q_rope.reshape(new_count * head_count, q_rope.shape[2])
    scores = jnp.dot(query_rows, keys_latent.T, preferred_element_type=jnp.float32)
    scores = (
        scores + jnp.dot(rope_rows, keys_rope.T, preferred_element_type=jnp.float32)
    ) * softmax_scale
    token_of_row = jnp.arange(new_count * head_count, dtype=jnp.int32) // head_count
    key_index = jnp.arange(keys_latent.shape[0], dtype=jnp.int32)
    visible = key_index[None, :] <= token_of_row[:, None] + cache_count
    row_top = jnp.max(jnp.where(visible, scores, -jnp.inf), axis=1, keepdims=True)
    exponent = jnp.where(visible, jnp.exp(scores - row_top), 0.0)
    weights_att = (exponent / jnp.sum(exponent, axis=1, keepdims=True)).astype(jnp.bfloat16)
    mixed_latent = jnp.dot(weights_att, keys_latent, preferred_element_type=jnp.float32).astype(
        jnp.bfloat16
    )
    return mixed_latent.reshape(new_count, head_count, latent_width)


def up_project(mixed_latent, w_uv):
    heads_out = jnp.einsum(
        "thl,lhv->thv", mixed_latent, w_uv, preferred_element_type=jnp.float32
    )
    return heads_out.astype(jnp.bfloat16).reshape(mixed_latent.shape[0], -1)


def project_gathered(mixed_latent, w_uv, w_out):
    heads_flat = up_project(mixed_latent, lax.all_gather(w_uv, "fsdp", axis=0, tiled=True))
    column_width = w_out.shape[1] // lax.axis_size("ep")
    own_columns = lax.dynamic_slice_in_dim(
        w_out, lax.axis_index("ep") * column_width, column_width, 1
    )
    column_block = lax.all_gather(own_columns, "fsdp", axis=0, tiled=True)
    return jnp.dot(
        heads_flat,
        lax.all_gather(column_block, "ep", axis=1, tiled=True),
        preferred_element_type=jnp.float32,
    )


def project_paired(mixed_latent, w_uv, w_out):
    pair = [(0, 1), (1, 0)]
    ep = lax.axis_size("ep")
    twins = [(i, i ^ 1) for i in range(ep)]
    side = lax.axis_index("fsdp")
    lane = lax.axis_index("ep") % 2
    rows = w_uv.shape[0] // 2
    mine = lax.ppermute(
        lax.dynamic_slice_in_dim(w_uv, lane * rows, rows, 0), "fsdp", pair
    )
    theirs = lax.ppermute(mine, "ep", twins)
    far = jnp.where(
        lane == 0, jnp.concatenate([mine, theirs], 0), jnp.concatenate([theirs, mine], 0)
    )
    full = jnp.where(side == 0, jnp.concatenate([w_uv, far], 0), jnp.concatenate([far, w_uv], 0))
    heads_flat = up_project(mixed_latent, full)
    width = w_out.shape[0]
    count = heads_flat.shape[0]
    keep = lax.dynamic_slice_in_dim(heads_flat, side * width, width, 1)
    give = lax.dynamic_slice_in_dim(heads_flat, (1 - side) * width, width, 1)
    other = lax.ppermute(give, "fsdp", pair)
    both = jnp.dot(
        jnp.concatenate([other, keep], 0), w_out, preferred_element_type=jnp.float32
    )
    back = lax.ppermute(both[:count].astype(jnp.bfloat16), "fsdp", pair)
    return both, back


def experts(rows, w_gate, w_up, w_down):
    gate_proj = jnp.dot(rows, w_gate, preferred_element_type=jnp.float32)
    up_proj = jnp.dot(rows, w_up, preferred_element_type=jnp.float32)
    activated = (jax.nn.silu(gate_proj) * up_proj).astype(jnp.bfloat16)
    return jnp.dot(activated, w_down, preferred_element_type=jnp.float32).astype(jnp.bfloat16)


def slots_of(own_ids, expert_count, capacity):
    choose = (own_ids[..., None] == jnp.arange(expert_count, dtype=jnp.int32)).astype(jnp.float32)
    assigned = choose.reshape(-1, expert_count)
    earlier = jnp.cumsum(assigned, axis=0) - assigned
    slot_index = jnp.sum(earlier * assigned, axis=-1).reshape(own_ids.shape).astype(jnp.int32)
    return own_ids * capacity + slot_index


def gates_of(normed, router, ids):
    logits = jnp.dot(normed, router, preferred_element_type=jnp.float32)
    choose = ids[..., None] == jnp.arange(router.shape[1], dtype=jnp.int32)
    picked = jnp.sum(jnp.where(choose, logits[:, None, :], 0.0), axis=-1)
    return jax.nn.softmax(picked, axis=-1)


def weighted_rows(weights, rows):
    high = weights.astype(jnp.bfloat16)
    low = (weights - high.astype(jnp.float32)).astype(jnp.bfloat16)
    return jnp.dot(
        jnp.concatenate([high, low], 1),
        jnp.concatenate([rows, rows], 0),
        preferred_element_type=jnp.float32,
    )


def routed_exchanged(normed, target, capacity, router, w_gate, w_up, w_down):
    expert_count = lax.axis_size("ep")
    gate_weights = gates_of(normed, router, target // capacity)
    here = target[..., None] == jnp.arange(expert_count * capacity, dtype=jnp.int32)
    placed = jnp.sum(here.astype(jnp.bfloat16), axis=1)
    combine = jnp.sum(jnp.where(here, gate_weights[..., None], 0.0), axis=1)
    buffers = jnp.einsum("tp,td->pd", placed, normed, preferred_element_type=jnp.float32).astype(
        jnp.bfloat16
    )
    buffers = buffers.reshape(expert_count, capacity, -1)
    received = lax.all_to_all(buffers, "ep", split_axis=0, concat_axis=0, tiled=True)
    result = experts(received.reshape(expert_count * capacity, -1), w_gate, w_up, w_down)
    result = result.reshape(expert_count, capacity, -1)
    returned = lax.all_to_all(result, "ep", split_axis=0, concat_axis=0, tiled=True)
    return weighted_rows(combine, returned.reshape(expert_count * capacity, -1))


def fused(body, outs, *args, vmem=8, flops=0, bytes_accessed=0):
    whole = pl.BlockSpec(memory_space=pltpu.VMEM)
    return pl.pallas_call(
        body,
        out_shape=[jax.ShapeDtypeStruct(shape, dtype) for shape, dtype in outs],
        in_specs=[whole] * len(args),
        out_specs=[whole] * len(outs),
        cost_estimate=pl.CostEstimate(
            flops=flops, bytes_accessed=bytes_accessed, transcendentals=0
        ),
        compiler_params=pltpu.CompilerParams(vmem_limit_bytes=vmem << 20),
    )(*args)


def slot_kernel(expert_count, capacity, ids_ref, target_ref):
    ids = ids_ref[...]
    top, count = ids.shape
    level = lax.broadcasted_iota(jnp.int32, (expert_count, count), 0)
    chosen = jnp.zeros((expert_count, count), jnp.float32)
    for k in range(top):
        chosen += (ids[k : k + 1] == level).astype(jnp.float32)
    rows = lax.broadcasted_iota(jnp.int32, (count, count), 0)
    columns = lax.broadcasted_iota(jnp.int32, (count, count), 1)
    ahead = (rows < columns).astype(jnp.float32).astype(jnp.bfloat16)
    earlier = jnp.dot(chosen.astype(jnp.bfloat16), ahead, preferred_element_type=jnp.float32)
    for k in range(top):
        own = ids[k : k + 1]
        slot = jnp.sum(jnp.where(own == level, earlier, 0.0), axis=0, keepdims=True)
        target_ref[k : k + 1] = own * capacity + slot.astype(jnp.int32)


def matches(target, capacity, place):
    top, count = target.shape
    row = lax.broadcasted_iota(jnp.int32, (4 * capacity, count), 0)
    slot = jnp.zeros_like(row)
    for j in range(4):
        inside = (row >= j * capacity) & (row < (j + 1) * capacity)
        slot = jnp.where(inside, (place ^ j) * capacity + row - j * capacity, slot)
    found = jnp.zeros(row.shape, jnp.float32)
    for k in range(top):
        found += (target[k : k + 1] == slot).astype(jnp.float32)
    return found


def pick_kernel(capacity, sources, *refs):
    place = lax.axis_index("ep")
    half = refs[1].shape[1]
    out = refs[3 * sources :]
    for n in range(sources):
        target_ref, low_ref, high_ref = refs[3 * n : 3 * n + 3]
        found = matches(target_ref[...], capacity, place).astype(jnp.bfloat16)
        for part, ref in enumerate((low_ref, high_ref)):
            rows = jnp.dot(found, ref[...], preferred_element_type=jnp.float32)
            rows = rows.astype(jnp.bfloat16)
            for j in range(4):
                out[j][
                    n * capacity : (n + 1) * capacity, part * half : (part + 1) * half
                ] = rows[j * capacity : (j + 1) * capacity]


def dot_rows(a, b):
    return lax.dot_general(a, b, (((1,), (1,)), ((), ())), preferred_element_type=jnp.float32)


def gate_kernel(capacity, router_ref, *refs):
    place = lax.axis_index("ep")
    expert_count = router_ref.shape[0]
    out = refs[12:]
    half = refs[1].shape[1]
    for n in range(4):
        target_ref, low_ref, high_ref = refs[3 * n : 3 * n + 3]
        target = target_ref[...]
        top, count = target.shape
        logits = dot_rows(router_ref[:, :half], low_ref[...])
        logits += dot_rows(router_ref[:, half:], high_ref[...])
        level = lax.broadcasted_iota(jnp.int32, (expert_count, count), 0)
        first = level * capacity
        chosen = jnp.zeros((expert_count, count), jnp.float32)
        for k in range(top):
            own = target[k : k + 1]
            chosen += ((own >= first) & (own < first + capacity)).astype(jnp.float32)
        inside = chosen > 0
        peak = jnp.max(jnp.where(inside, logits, -jnp.inf), axis=0, keepdims=True)
        power = jnp.where(inside, jnp.exp(logits - peak), 0.0)
        gate = power / jnp.sum(power, axis=0, keepdims=True)
        found = matches(target, capacity, place)
        row = lax.broadcasted_iota(jnp.int32, found.shape, 0)
        for j in range(4):
            own = jnp.sum(jnp.where(level == (place ^ j), gate, 0.0), axis=0, keepdims=True)
            within = (row >= j * capacity) & (row < (j + 1) * capacity)
            found = jnp.where(within, found * own, found)
        out[n][...] = found.T


def norm_kernel(x_ref, both_ref, back_ref, gain_ref, hidden_ref, attended_ref, low_ref, high_ref):
    count, width = hidden_ref.shape
    hidden = x_ref[0].astype(jnp.float32) + (
        both_ref[count:] + back_ref[...].astype(jnp.float32)
    )
    hidden_ref[...] = hidden
    attended_ref[0] = hidden.astype(jnp.bfloat16)
    square = jnp.mean(hidden * hidden, axis=-1, keepdims=True)
    normed = hidden * lax.rsqrt(square + epsilon) * gain_ref[...]
    low_ref[...] = normed[:, : width // 2].astype(jnp.bfloat16)
    high_ref[...] = normed[:, width // 2 :].astype(jnp.bfloat16)


def expert_kernel(*refs):
    gate_ref, up_ref, down_ref = refs[12:15]
    rows = jnp.concatenate([ref[...] for ref in refs[:12]], 0)
    active = []
    hidden_width = down_ref.shape[0]
    for start in range(0, hidden_width, 256):
        part = slice(start, min(start + 256, hidden_width))
        gate = dot_rows(rows, gate_ref[part])
        up = dot_rows(rows, up_ref[part])
        active.append((gate / (1.0 + jnp.exp(-gate)) * up).astype(jnp.bfloat16))
    active = jnp.concatenate(active, 1)
    for start in range(0, down_ref.shape[1], 512):
        part = slice(start, start + 512)
        result = jnp.dot(active, down_ref[:, part], preferred_element_type=jnp.float32)
        result = result.astype(jnp.bfloat16)
        offset = 0
        for ref in refs[15:]:
            ref[:, part] = result[offset : offset + ref.shape[0]]
            offset += ref.shape[0]


def weigh(weights, rows):
    high = weights.astype(jnp.bfloat16)
    low = (weights - high.astype(jnp.float32)).astype(jnp.bfloat16)
    return jnp.dot(high, rows, preferred_element_type=jnp.float32) + jnp.dot(
        low, rows, preferred_element_type=jnp.float32
    )


def far_kernel(weights_ref, r0, r1, r2, r3, low_ref, high_ref):
    rows = jnp.concatenate([r[...] for r in (r0, r1, r2, r3)], 0)
    total = weigh(weights_ref[...], rows)
    half = low_ref.shape[1]
    low_ref[...] = total[:, :half].astype(jnp.bfloat16)
    high_ref[...] = total[:, half:].astype(jnp.bfloat16)


def near_kernel(
    capacity, before_w, after_w, r0, r1, r2, r3, add_low, add_high, before_ref, after_ref
):
    half = add_low.shape[1]
    blocks = (r0, r1, r2, r3)
    rows = jnp.concatenate([r[:capacity] for r in blocks], 0)
    total = weigh(before_w[...], rows)
    before_ref[:, :half] = total[:, :half].astype(jnp.bfloat16)
    before_ref[:, half:] = (total[:, half:] + add_high[...].astype(jnp.float32)).astype(
        jnp.bfloat16
    )
    rows = jnp.concatenate([r[capacity:] for r in blocks], 0)
    total = weigh(after_w[...], rows)
    after_ref[:, :half] = (total[:, :half] + add_low[...].astype(jnp.float32)).astype(
        jnp.bfloat16
    )
    after_ref[:, half:] = total[:, half:].astype(jnp.bfloat16)


def last_kernel(hidden_ref, weights_ref, r0, r1, r2, r3, x_ref, y_ref, out_ref):
    rows = jnp.concatenate([r[...] for r in (r0, r1, r2, r3)], 0)
    total = weigh(weights_ref[...], rows)
    total = total + x_ref[...].astype(jnp.float32) + y_ref[...].astype(jnp.float32)
    out_ref[...] = (hidden_ref[...] + total).astype(jnp.bfloat16)


def routed_ringed(hidden, low, high, targets, capacity, router, w_gate, w_up, w_down):
    onward, backward = ring_steps()
    traded = [[(i, i ^ j) for i in range(16)] for j in range(4)]
    count, half = low.shape
    width = 2 * half
    bf16 = jnp.bfloat16

    def send(value, steps):
        return lax.ppermute(value, "ep", steps)

    def pick(*sources):
        n = len(sources)
        return fused(
            functools.partial(pick_kernel, capacity, n),
            [((n * capacity, width), bf16)] * 4,
            *[part for source in sources for part in source],
            flops=n * 2 * 4 * capacity * count * width,
            bytes_accessed=n * 4 * width * (count + 4 * capacity),
        )

    def trade(blocks):
        return [blocks[0]] + [send(blocks[j], traded[j]) for j in (1, 2, 3)]

    before_low, after_high = send(low, onward), send(high, backward)
    before_high, after_low = send(high, onward), send(low, backward)
    own = (targets[0], low, high)
    own_rows = trade(pick(own))
    before_high, after_low, own_rows = lax.optimization_barrier(
        (before_high, after_low, own_rows)
    )
    far_low, far_high = send(before_low, onward), send(after_high, backward)
    before = (targets[1], before_low, before_high)
    after = (targets[2], after_low, after_high)
    near_rows = trade(pick(before, after))
    far = (targets[3], far_low, far_high)
    far_rows = trade(pick(far))
    slots = (count, 4 * capacity)
    weights = fused(
        functools.partial(gate_kernel, capacity),
        [(slots, jnp.float32)] * 4,
        router.T,
        *own,
        *before,
        *after,
        *far,
        flops=8 * count * width * 16,
        bytes_accessed=16 * count * width,
    )
    blocks = far_rows + near_rows + own_rows
    hidden_width = w_gate.shape[2]
    total = 16 * capacity
    result = fused(
        expert_kernel,
        [(b.shape, bf16) for b in blocks],
        *blocks,
        jnp.swapaxes(w_gate[0], 0, 1),
        jnp.swapaxes(w_up[0], 0, 1),
        w_down[0],
        vmem=16,
        flops=6 * total * width * hidden_width,
        bytes_accessed=6 * width * hidden_width + 4 * total * width,
    )
    spent = 2 * 4 * 4 * capacity * count * width
    moved = 4 * width * (count + 4 * capacity)
    far_low, far_high = fused(
        far_kernel,
        [((count, half), bf16)] * 2,
        weights[3],
        *trade(result[:4]),
        flops=spent,
        bytes_accessed=moved,
    )
    add_low, add_high = send(far_low, onward), send(far_high, backward)
    before_sum, after_sum = fused(
        functools.partial(near_kernel, capacity),
        [((count, width), bf16)] * 2,
        weights[1],
        weights[2],
        *trade(result[4:8]),
        add_low,
        add_high,
        flops=2 * spent,
        bytes_accessed=2 * moved,
    )
    from_before = send(after_sum, onward)
    from_after = send(before_sum, backward)
    return fused(
        last_kernel,
        [((count, width), bf16)],
        hidden,
        weights[0],
        *trade(result[8:]),
        from_before,
        from_after,
        flops=spent,
        bytes_accessed=2 * moved,
    )[0]


def ring_steps():
    order = (0, 1, 3, 2)
    onward = [
        (order[i] * 4 + j, order[(i + 1) % 4] * 4 + j) for i in range(4) for j in range(4)
    ]
    return onward, [(b, a) for a, b in onward]


def per_device(
    x_resid,
    q_latent,
    q_rope,
    cache_latent,
    cache_rope,
    new_latent,
    new_rope,
    w_uv,
    w_out,
    norm_gain,
    router,
    expert_ids,
    w_gate,
    w_up,
    w_down,
):
    mixed_latent = attend_local(
        q_latent[0], q_rope[0], cache_latent[0], cache_rope[0], new_latent[0], new_rope[0]
    )
    new_count = mixed_latent.shape[0]
    expert_count = lax.axis_size("ep")
    capacity = new_count * expert_ids.shape[2] // expert_count
    if lax.axis_size("fsdp") != 2 or expert_count != 16:
        projected = project_gathered(mixed_latent, w_uv, w_out)
        hidden = x_resid[0].astype(jnp.float32) + projected
        normed = hidden * lax.rsqrt(jnp.mean(hidden * hidden, axis=-1, keepdims=True) + epsilon)
        normed = (normed * norm_gain).astype(jnp.bfloat16)
        target = slots_of(expert_ids[0], expert_count, capacity)
        routed_sum = routed_exchanged(
            normed, target, capacity, router, w_gate[0], w_up[0], w_down[0]
        )
        layer_out = (hidden + routed_sum).astype(jnp.bfloat16)
        return (hidden.astype(jnp.bfloat16)[None], layer_out[None])
    onward, backward = ring_steps()
    own = fused(
        functools.partial(slot_kernel, expert_count, capacity),
        [(expert_ids.shape[:0:-1], jnp.int32)],
        expert_ids[0].T,
    )[0]
    before = lax.ppermute(own, "ep", onward)
    after = lax.ppermute(own, "ep", backward)
    far = lax.ppermute(before, "ep", onward)
    both, back = project_paired(mixed_latent, w_uv, w_out)
    back, before, after, far = lax.optimization_barrier((back, before, after, far))
    width = both.shape[1]
    halves = (new_count, width // 2)
    hidden, attended, low, high = fused(
        norm_kernel,
        [
            ((new_count, width), jnp.float32),
            ((1, new_count, width), jnp.bfloat16),
            (halves, jnp.bfloat16),
            (halves, jnp.bfloat16),
        ],
        x_resid,
        both,
        back,
        norm_gain[None],
        flops=8 * new_count * width,
        bytes_accessed=20 * new_count * width,
    )
    targets = (own, before, after, far)
    layer_out = routed_ringed(
        hidden, low, high, targets, capacity, router, w_gate, w_up, w_down
    )
    return (attended, layer_out[None])


def solution(mesh):
    placed = (
        P(("fsdp", "ep"), None, None),
        P(("fsdp", "ep"), None, None, None),
        P(("fsdp", "ep"), None, None, None),
        P(("fsdp", "ep"), None, None),
        P(("fsdp", "ep"), None, None),
        P(("fsdp", "ep"), None, None),
        P(("fsdp", "ep"), None, None),
        P("fsdp", None, None),
        P("fsdp", None),
        P(),
        P(),
        P(("fsdp", "ep"), None, None),
        P("ep", None, None),
        P("ep", None, None),
        P("ep", None, None),
    )
    return jax.shard_map(
        per_device,
        mesh=mesh,
        in_specs=placed,
        out_specs=(P(("fsdp", "ep"), None, None), P(("fsdp", "ep"), None, None)),
        check_vma=False,
    )
```

```python
import functools

import jax
import jax.numpy as jnp
from jax import lax
from jax.experimental import pallas as pl
from jax.experimental.pallas import tpu as pltpu
from jax.sharding import PartitionSpec as P

softmax_scale = 0.07216878364870323
epsilon = 1e-06


def attend_local(q_latent, q_rope, cache_latent, cache_rope, new_latent, new_rope):
    new_count, head_count, latent_width = q_latent.shape
    cache_count = cache_latent.shape[0]
    keys_latent = jnp.concatenate([cache_latent, new_latent], 0)
    keys_rope = jnp.concatenate([cache_rope, new_rope], 0)
    query_rows = q_latent.reshape(new_count * head_count, latent_width)
    rope_rows = q_rope.reshape(new_count * head_count, q_rope.shape[2])
    scores = jnp.dot(query_rows, keys_latent.T, preferred_element_type=jnp.float32)
    scores = (
        scores + jnp.dot(rope_rows, keys_rope.T, preferred_element_type=jnp.float32)
    ) * softmax_scale
    token_of_row = jnp.arange(new_count * head_count, dtype=jnp.int32) // head_count
    key_index = jnp.arange(keys_latent.shape[0], dtype=jnp.int32)
    visible = key_index[None, :] <= token_of_row[:, None] + cache_count
    row_top = jnp.max(jnp.where(visible, scores, -jnp.inf), axis=1, keepdims=True)
    exponent = jnp.where(visible, jnp.exp(scores - row_top), 0.0)
    weights_att = (exponent / jnp.sum(exponent, axis=1, keepdims=True)).astype(jnp.bfloat16)
    mixed_latent = jnp.dot(weights_att, keys_latent, preferred_element_type=jnp.float32).astype(
        jnp.bfloat16
    )
    return mixed_latent.reshape(new_count, head_count, latent_width)


def up_project(mixed_latent, w_uv):
    heads_out = jnp.einsum(
        "thl,lhv->thv", mixed_latent, w_uv, preferred_element_type=jnp.float32
    )
    return heads_out.astype(jnp.bfloat16).reshape(mixed_latent.shape[0], -1)


def project_gathered(mixed_latent, w_uv, w_out):
    heads_flat = up_project(mixed_latent, lax.all_gather(w_uv, "fsdp", axis=0, tiled=True))
    column_width = w_out.shape[1] // lax.axis_size("ep")
    own_columns = lax.dynamic_slice_in_dim(
        w_out, lax.axis_index("ep") * column_width, column_width, 1
    )
    column_block = lax.all_gather(own_columns, "fsdp", axis=0, tiled=True)
    return jnp.dot(
        heads_flat,
        lax.all_gather(column_block, "ep", axis=1, tiled=True),
        preferred_element_type=jnp.float32,
    )


def project_paired(mixed_latent, w_uv, w_out):
    pair = [(0, 1), (1, 0)]
    ep = lax.axis_size("ep")
    twins = [(i, i ^ 1) for i in range(ep)]
    side = lax.axis_index("fsdp")
    lane = lax.axis_index("ep") % 2
    rows = w_uv.shape[0] // 2
    mine = lax.ppermute(
        lax.dynamic_slice_in_dim(w_uv, lane * rows, rows, 0), "fsdp", pair
    )
    theirs = lax.ppermute(mine, "ep", twins)
    far = jnp.where(
        lane == 0, jnp.concatenate([mine, theirs], 0), jnp.concatenate([theirs, mine], 0)
    )
    full = jnp.where(side == 0, jnp.concatenate([w_uv, far], 0), jnp.concatenate([far, w_uv], 0))
    heads_flat = up_project(mixed_latent, full)
    width = w_out.shape[0]
    count = heads_flat.shape[0]
    keep = lax.dynamic_slice_in_dim(heads_flat, side * width, width, 1)
    give = lax.dynamic_slice_in_dim(heads_flat, (1 - side) * width, width, 1)
    other = lax.ppermute(give, "fsdp", pair)
    both = jnp.dot(
        jnp.concatenate([other, keep], 0), w_out, preferred_element_type=jnp.float32
    )
    back = lax.ppermute(both[:count].astype(jnp.bfloat16), "fsdp", pair)
    return both, back


def experts(rows, w_gate, w_up, w_down):
    gate_proj = jnp.dot(rows, w_gate, preferred_element_type=jnp.float32)
    up_proj = jnp.dot(rows, w_up, preferred_element_type=jnp.float32)
    activated = (jax.nn.silu(gate_proj) * up_proj).astype(jnp.bfloat16)
    return jnp.dot(activated, w_down, preferred_element_type=jnp.float32).astype(jnp.bfloat16)


def slots_of(own_ids, expert_count, capacity):
    choose = (own_ids[..., None] == jnp.arange(expert_count, dtype=jnp.int32)).astype(jnp.float32)
    assigned = choose.reshape(-1, expert_count)
    earlier = jnp.cumsum(assigned, axis=0) - assigned
    slot_index = jnp.sum(earlier * assigned, axis=-1).reshape(own_ids.shape).astype(jnp.int32)
    return own_ids * capacity + slot_index


def gates_of(normed, router, ids):
    logits = jnp.dot(normed, router, preferred_element_type=jnp.float32)
    choose = ids[..., None] == jnp.arange(router.shape[1], dtype=jnp.int32)
    picked = jnp.sum(jnp.where(choose, logits[:, None, :], 0.0), axis=-1)
    return jax.nn.softmax(picked, axis=-1)


def weighted_rows(weights, rows):
    high = weights.astype(jnp.bfloat16)
    low = (weights - high.astype(jnp.float32)).astype(jnp.bfloat16)
    return jnp.dot(
        jnp.concatenate([high, low], 1),
        jnp.concatenate([rows, rows], 0),
        preferred_element_type=jnp.float32,
    )


def routed_exchanged(normed, target, capacity, router, w_gate, w_up, w_down):
    expert_count = lax.axis_size("ep")
    gate_weights = gates_of(normed, router, target // capacity)
    here = target[..., None] == jnp.arange(expert_count * capacity, dtype=jnp.int32)
    placed = jnp.sum(here.astype(jnp.bfloat16), axis=1)
    combine = jnp.sum(jnp.where(here, gate_weights[..., None], 0.0), axis=1)
    buffers = jnp.einsum("tp,td->pd", placed, normed, preferred_element_type=jnp.float32).astype(
        jnp.bfloat16
    )
    buffers = buffers.reshape(expert_count, capacity, -1)
    received = lax.all_to_all(buffers, "ep", split_axis=0, concat_axis=0, tiled=True)
    result = experts(received.reshape(expert_count * capacity, -1), w_gate, w_up, w_down)
    result = result.reshape(expert_count, capacity, -1)
    returned = lax.all_to_all(result, "ep", split_axis=0, concat_axis=0, tiled=True)
    return weighted_rows(combine, returned.reshape(expert_count * capacity, -1))


def fused(body, outs, *args, vmem=8, flops=0, bytes_accessed=0):
    whole = pl.BlockSpec(memory_space=pltpu.VMEM)
    return pl.pallas_call(
        body,
        out_shape=[jax.ShapeDtypeStruct(shape, dtype) for shape, dtype in outs],
        in_specs=[whole] * len(args),
        out_specs=[whole] * len(outs),
        cost_estimate=pl.CostEstimate(
            flops=flops, bytes_accessed=bytes_accessed, transcendentals=0
        ),
        compiler_params=pltpu.CompilerParams(vmem_limit_bytes=vmem << 20),
    )(*args)


def slot_kernel(expert_count, capacity, *refs):
    sources = len(refs) // 2
    for ids_ref, target_ref in zip(refs[:sources], refs[sources:]):
        ids = ids_ref[...]
        top, count = ids.shape
        level = lax.broadcasted_iota(jnp.int32, (expert_count, count), 0)
        chosen = jnp.zeros((expert_count, count), jnp.float32)
        for k in range(top):
            chosen += (ids[k : k + 1] == level).astype(jnp.float32)
        rows = lax.broadcasted_iota(jnp.int32, (count, count), 0)
        columns = lax.broadcasted_iota(jnp.int32, (count, count), 1)
        ahead = (rows < columns).astype(jnp.float32).astype(jnp.bfloat16)
        earlier = jnp.dot(
            chosen.astype(jnp.bfloat16), ahead, preferred_element_type=jnp.float32
        )
        for k in range(top):
            own = ids[k : k + 1]
            slot = jnp.sum(jnp.where(own == level, earlier, 0.0), axis=0, keepdims=True)
            target_ref[k : k + 1] = own * capacity + slot.astype(jnp.int32)


def matches(target, capacity, place):
    top, count = target.shape
    row = lax.broadcasted_iota(jnp.int32, (4 * capacity, count), 0)
    slot = jnp.zeros_like(row)
    for j in range(4):
        inside = (row >= j * capacity) & (row < (j + 1) * capacity)
        slot = jnp.where(inside, (place ^ j) * capacity + row - j * capacity, slot)
    found = jnp.zeros(row.shape, jnp.float32)
    for k in range(top):
        found += (target[k : k + 1] == slot).astype(jnp.float32)
    return found


def pick_kernel(capacity, sources, *refs):
    place = lax.axis_index("ep")
    position = 0
    out = refs[-4:]
    for n, pieces in enumerate(sources):
        found = matches(refs[position][...], capacity, place).astype(jnp.bfloat16)
        offset = 0
        for ref in refs[position + 1 : position + 1 + pieces]:
            rows = jnp.dot(found, ref[...], preferred_element_type=jnp.float32)
            rows = rows.astype(jnp.bfloat16)
            columns = slice(offset, offset + ref.shape[1])
            offset += ref.shape[1]
            for j in range(4):
                out[j][n * capacity : (n + 1) * capacity, columns] = rows[
                    j * capacity : (j + 1) * capacity
                ]
        position += 1 + pieces


def dot_rows(a, b):
    return lax.dot_general(a, b, (((1,), (1,)), ((), ())), preferred_element_type=jnp.float32)


def gate_kernel(capacity, router_ref, *refs):
    place = lax.axis_index("ep")
    expert_count = router_ref.shape[0]
    out = refs[12:]
    half = refs[1].shape[1]
    for n in range(4):
        target_ref, low_ref, high_ref = refs[3 * n : 3 * n + 3]
        target = target_ref[...]
        top, count = target.shape
        logits = dot_rows(router_ref[:, :half], low_ref[...])
        logits += dot_rows(router_ref[:, half:], high_ref[...])
        level = lax.broadcasted_iota(jnp.int32, (expert_count, count), 0)
        first = level * capacity
        chosen = jnp.zeros((expert_count, count), jnp.float32)
        for k in range(top):
            own = target[k : k + 1]
            chosen += ((own >= first) & (own < first + capacity)).astype(jnp.float32)
        inside = chosen > 0
        peak = jnp.max(jnp.where(inside, logits, -jnp.inf), axis=0, keepdims=True)
        power = jnp.where(inside, jnp.exp(logits - peak), 0.0)
        gate = power / jnp.sum(power, axis=0, keepdims=True)
        found = matches(target, capacity, place)
        row = lax.broadcasted_iota(jnp.int32, found.shape, 0)
        for j in range(4):
            own = jnp.sum(jnp.where(level == (place ^ j), gate, 0.0), axis=0, keepdims=True)
            within = (row >= j * capacity) & (row < (j + 1) * capacity)
            found = jnp.where(within, found * own, found)
        out[n][...] = found.T


def norm_kernel(x_ref, both_ref, back_ref, gain_ref, hidden_ref, attended_ref, low_ref, high_ref):
    count, width = hidden_ref.shape
    hidden = x_ref[0].astype(jnp.float32) + (
        both_ref[count:] + back_ref[...].astype(jnp.float32)
    )
    hidden_ref[...] = hidden
    attended_ref[0] = hidden.astype(jnp.bfloat16)
    square = jnp.mean(hidden * hidden, axis=-1, keepdims=True)
    normed = hidden * lax.rsqrt(square + epsilon) * gain_ref[...]
    low_ref[...] = normed[:, : width // 2].astype(jnp.bfloat16)
    high_ref[...] = normed[:, width // 2 :].astype(jnp.bfloat16)


def hidden_units(rows, gate_ref, up_ref):
    active = []
    for start in range(0, gate_ref.shape[0], 256):
        part = slice(start, min(start + 256, gate_ref.shape[0]))
        gate = dot_rows(rows, gate_ref[part])
        up = dot_rows(rows, up_ref[part])
        active.append((gate / (1.0 + jnp.exp(-gate)) * up).astype(jnp.bfloat16))
    return jnp.concatenate(active, 1)


def near_expert_kernel(capacity, *refs):
    first, second, own = refs[0:4], refs[4:8], refs[8:12]
    gate_ref, up_ref, down_ref = refs[12:15]
    out_first, out_second, out_own = refs[15:19], refs[19:23], refs[23:27]
    rows = [
        jnp.concatenate([a[:capacity], b[:capacity]], 1) for a, b in zip(first, second)
    ]
    rows += [
        jnp.concatenate([b[capacity:], a[capacity:]], 1) for a, b in zip(first, second)
    ]
    rows += [ref[...] for ref in own]
    active = hidden_units(jnp.concatenate(rows, 0), gate_ref, up_ref)
    width = down_ref.shape[1]
    step = width // 4
    for start in range(0, width, step):
        result = jnp.dot(
            active, down_ref[:, start : start + step], preferred_element_type=jnp.float32
        ).astype(jnp.bfloat16)
        low = start < width // 2
        columns = slice(start % (width // 2), start % (width // 2) + step)
        for j in range(4):
            blocks = [
                result[(4 * n + j) * capacity : (4 * n + j + 1) * capacity] for n in range(3)
            ]
            before_out, after_out = (out_first, out_second) if low else (out_second, out_first)
            before_out[j][:capacity, columns] = blocks[0]
            after_out[j][capacity:, columns] = blocks[1]
            out_own[j][:, start : start + step] = blocks[2]


def far_expert_kernel(*refs):
    gate_ref, up_ref, down_ref = refs[4:7]
    rows = jnp.concatenate([ref[...] for ref in refs[:4]], 0)
    active = hidden_units(rows, gate_ref, up_ref)
    capacity = refs[0].shape[0]
    for start in range(0, down_ref.shape[1], 512):
        part = slice(start, start + 512)
        result = jnp.dot(active, down_ref[:, part], preferred_element_type=jnp.float32)
        result = result.astype(jnp.bfloat16)
        for j in range(4):
            refs[7 + j][:, part] = result[j * capacity : (j + 1) * capacity]


def weigh(weights, rows):
    high = weights.astype(jnp.bfloat16)
    low = (weights - high.astype(jnp.float32)).astype(jnp.bfloat16)
    return jnp.dot(high, rows, preferred_element_type=jnp.float32) + jnp.dot(
        low, rows, preferred_element_type=jnp.float32
    )


def far_kernel(weights_ref, r0, r1, r2, r3, low_ref, high_ref):
    rows = jnp.concatenate([r[...] for r in (r0, r1, r2, r3)], 0)
    total = weigh(weights_ref[...], rows)
    half = low_ref.shape[1]
    low_ref[...] = total[:, :half].astype(jnp.bfloat16)
    high_ref[...] = total[:, half:].astype(jnp.bfloat16)


def near_kernel(capacity, before_w, after_w, r0, r1, r2, r3, *refs):
    blocks = (r0, r1, r2, r3)
    adds = refs[:-2]
    for n, weights in enumerate((before_w, after_w)):
        rows = jnp.concatenate([r[n * capacity : (n + 1) * capacity] for r in blocks], 0)
        total = weigh(weights[...], rows)
        if adds:
            total += adds[n][...].astype(jnp.float32)
        refs[len(adds) + n][...] = total.astype(jnp.bfloat16)


def last_kernel(hidden_ref, weights_ref, r0, r1, r2, r3, x_low, x_high, y_low, y_high, out_ref):
    rows = jnp.concatenate([r[...] for r in (r0, r1, r2, r3)], 0)
    total = hidden_ref[...] + weigh(weights_ref[...], rows)
    half = x_low.shape[1]
    low = x_low[...].astype(jnp.float32) + y_low[...].astype(jnp.float32)
    high = x_high[...].astype(jnp.float32) + y_high[...].astype(jnp.float32)
    out_ref[:, :half] = (total[:, :half] + low).astype(jnp.bfloat16)
    out_ref[:, half:] = (total[:, half:] + high).astype(jnp.bfloat16)


def routed_ringed(hidden, low, high, targets, capacity, router, w_gate, w_up, w_down):
    onward, backward = ring_steps()
    traded = [[(i, i ^ j) for i in range(16)] for j in range(4)]
    count, half = low.shape
    width = 2 * half
    bf16 = jnp.bfloat16

    def send(value, steps):
        return lax.ppermute(value, "ep", steps)

    def pick(*sources):
        n = len(sources)
        columns = sum(part.shape[1] for part in sources[0][1:])
        return fused(
            functools.partial(pick_kernel, capacity, [len(source) - 1 for source in sources]),
            [((n * capacity, columns), bf16)] * 4,
            *[part for source in sources for part in source],
            flops=n * 2 * 4 * capacity * count * columns,
            bytes_accessed=n * 4 * columns * (count + 4 * capacity),
        )

    def trade(blocks):
        return [blocks[0]] + [send(blocks[j], traded[j]) for j in (1, 2, 3)]

    own_slots, before_slots, after_slots, far_slots = targets
    before_low, after_high = send(low, onward), send(high, backward)
    before_high, after_low = send(high, onward), send(low, backward)
    own_rows = trade(pick((own_slots, low, high)))
    far_low, far_high = send(before_low, onward), send(after_high, backward)
    first_rows = trade(pick((before_slots, before_low), (after_slots, after_high)))
    before_high, after_low, own_rows, first_rows[0] = lax.optimization_barrier(
        (before_high, after_low, own_rows, first_rows[0])
    )
    second_rows = trade(pick((before_slots, before_high), (after_slots, after_low)))
    far_rows = trade(pick((far_slots, far_low, far_high)))
    expert_weights = (jnp.swapaxes(w_gate[0], 0, 1), jnp.swapaxes(w_up[0], 0, 1), w_down[0])
    hidden_width = w_gate.shape[2]
    unit = width * hidden_width
    blocks = first_rows + second_rows + own_rows
    near = fused(
        functools.partial(near_expert_kernel, capacity),
        [(b.shape, bf16) for b in blocks],
        *blocks,
        *expert_weights,
        vmem=16,
        flops=6 * 12 * capacity * unit,
        bytes_accessed=6 * unit + 4 * 12 * capacity * width,
    )
    slots = (count, 4 * capacity)
    weights = fused(
        functools.partial(gate_kernel, capacity),
        [(slots, jnp.float32)] * 4,
        router.T,
        *(own_slots, low, high),
        *(before_slots, before_low, before_high),
        *(after_slots, after_low, after_high),
        *(far_slots, far_low, far_high),
        flops=8 * count * width * 16,
        bytes_accessed=16 * count * width,
    )
    near, weights, far_rows = lax.optimization_barrier((near, weights, far_rows))
    result = fused(
        far_expert_kernel,
        [(b.shape, bf16) for b in far_rows],
        *far_rows,
        *expert_weights,
        vmem=16,
        flops=6 * 4 * capacity * unit,
        bytes_accessed=6 * unit + 4 * 4 * capacity * width,
    )
    spent = 2 * 4 * 4 * capacity * count * width
    moved = 4 * width * (count + 4 * capacity)
    piece = ((count, half), bf16)
    far_low, far_high = fused(
        far_kernel,
        [piece] * 2,
        weights[3],
        *trade(result),
        flops=spent,
        bytes_accessed=moved,
    )
    add_low, add_high = send(far_low, onward), send(far_high, backward)

    def near_sums(rows, *adds):
        return fused(
            functools.partial(near_kernel, capacity),
            [piece] * 2,
            weights[1],
            weights[2],
            *trade(rows),
            *adds,
            flops=spent,
            bytes_accessed=moved,
        )

    before_sum, after_sum = near_sums(near[0:4])
    from_after_low, from_before_high = send(before_sum, backward), send(after_sum, onward)
    before_sum, after_sum = near_sums(near[4:8], add_high, add_low)
    from_after_high, from_before_low = send(before_sum, backward), send(after_sum, onward)
    return fused(
        last_kernel,
        [((count, width), bf16)],
        hidden,
        weights[0],
        *trade(near[8:12]),
        from_before_low,
        from_before_high,
        from_after_low,
        from_after_high,
        flops=spent,
        bytes_accessed=2 * moved,
    )[0]


def ring_steps():
    order = (0, 1, 3, 2)
    onward = [
        (order[i] * 4 + j, order[(i + 1) % 4] * 4 + j) for i in range(4) for j in range(4)
    ]
    return onward, [(b, a) for a, b in onward]


def per_device(
    x_resid,
    q_latent,
    q_rope,
    cache_latent,
    cache_rope,
    new_latent,
    new_rope,
    w_uv,
    w_out,
    norm_gain,
    router,
    expert_ids,
    w_gate,
    w_up,
    w_down,
):
    mixed_latent = attend_local(
        q_latent[0], q_rope[0], cache_latent[0], cache_rope[0], new_latent[0], new_rope[0]
    )
    new_count = mixed_latent.shape[0]
    expert_count = lax.axis_size("ep")
    capacity = new_count * expert_ids.shape[2] // expert_count
    if lax.axis_size("fsdp") != 2 or expert_count != 16:
        projected = project_gathered(mixed_latent, w_uv, w_out)
        hidden = x_resid[0].astype(jnp.float32) + projected
        normed = hidden * lax.rsqrt(jnp.mean(hidden * hidden, axis=-1, keepdims=True) + epsilon)
        normed = (normed * norm_gain).astype(jnp.bfloat16)
        target = slots_of(expert_ids[0], expert_count, capacity)
        routed_sum = routed_exchanged(
            normed, target, capacity, router, w_gate[0], w_up[0], w_down[0]
        )
        layer_out = (hidden + routed_sum).astype(jnp.bfloat16)
        return (hidden.astype(jnp.bfloat16)[None], layer_out[None])
    onward, backward = ring_steps()
    ids = [expert_ids[0].T]
    across = [(i, i ^ 12) for i in range(16)]
    ids += [lax.ppermute(ids[0], "ep", steps) for steps in (onward, backward, across)]
    targets = fused(
        functools.partial(slot_kernel, expert_count, capacity),
        [(part.shape, jnp.int32) for part in ids],
        *ids,
    )
    mixed_latent, targets = lax.optimization_barrier((mixed_latent, targets))
    both, back = project_paired(mixed_latent, w_uv, w_out)
    width = both.shape[1]
    halves = (new_count, width // 2)
    hidden, attended, low, high = fused(
        norm_kernel,
        [
            ((new_count, width), jnp.float32),
            ((1, new_count, width), jnp.bfloat16),
            (halves, jnp.bfloat16),
            (halves, jnp.bfloat16),
        ],
        x_resid,
        both,
        back,
        norm_gain[None],
        flops=8 * new_count * width,
        bytes_accessed=20 * new_count * width,
    )
    layer_out = routed_ringed(
        hidden, low, high, targets, capacity, router, w_gate, w_up, w_down
    )
    return (attended, layer_out[None])


def solution(mesh):
    placed = (
        P(("fsdp", "ep"), None, None),
        P(("fsdp", "ep"), None, None, None),
        P(("fsdp", "ep"), None, None, None),
        P(("fsdp", "ep"), None, None),
        P(("fsdp", "ep"), None, None),
        P(("fsdp", "ep"), None, None),
        P(("fsdp", "ep"), None, None),
        P("fsdp", None, None),
        P("fsdp", None),
        P(),
        P(),
        P(("fsdp", "ep"), None, None),
        P("ep", None, None),
        P("ep", None, None),
        P("ep", None, None),
    )
    return jax.shard_map(
        per_device,
        mesh=mesh,
        in_specs=placed,
        out_specs=(P(("fsdp", "ep"), None, None), P(("fsdp", "ep"), None, None)),
        check_vma=False,
    )
```

```python
import functools

import jax
import jax.numpy as jnp
from jax import lax
from jax.experimental import pallas as pl
from jax.experimental.pallas import tpu as pltpu
from jax.sharding import PartitionSpec as P


softmax_scale = 0.07216878364870323
epsilon = 1e-06


def attend_local(q_latent, q_rope, cache_latent, cache_rope, new_latent, new_rope):
    new_count, head_count, latent_width = q_latent.shape
    cache_count = cache_latent.shape[0]
    keys_latent = jnp.concatenate([cache_latent, new_latent], 0)
    keys_rope = jnp.concatenate([cache_rope, new_rope], 0)
    query_rows = q_latent.reshape(new_count * head_count, latent_width)
    rope_rows = q_rope.reshape(new_count * head_count, q_rope.shape[2])
    scores = jnp.dot(query_rows, keys_latent.T, preferred_element_type=jnp.float32)
    scores = (
        scores + jnp.dot(rope_rows, keys_rope.T, preferred_element_type=jnp.float32)
    ) * softmax_scale
    token_of_row = jnp.arange(new_count * head_count, dtype=jnp.int32) // head_count
    key_index = jnp.arange(keys_latent.shape[0], dtype=jnp.int32)
    visible = key_index[None, :] <= token_of_row[:, None] + cache_count
    row_top = jnp.max(jnp.where(visible, scores, -jnp.inf), axis=1, keepdims=True)
    exponent = jnp.where(visible, jnp.exp(scores - row_top), 0.0)
    weights_att = (exponent / jnp.sum(exponent, axis=1, keepdims=True)).astype(jnp.bfloat16)
    mixed_latent = jnp.dot(weights_att, keys_latent, preferred_element_type=jnp.float32).astype(
        jnp.bfloat16
    )
    return mixed_latent.reshape(new_count, head_count, latent_width)


def up_project(mixed_latent, w_uv):
    heads_out = jnp.einsum(
        "thl,lhv->thv", mixed_latent, w_uv, preferred_element_type=jnp.float32
    )
    return heads_out.astype(jnp.bfloat16).reshape(mixed_latent.shape[0], -1)


def project_gathered(mixed_latent, w_uv, w_out):
    heads_flat = up_project(mixed_latent, lax.all_gather(w_uv, "fsdp", axis=0, tiled=True))
    column_width = w_out.shape[1] // lax.axis_size("ep")
    own_columns = lax.dynamic_slice_in_dim(
        w_out, lax.axis_index("ep") * column_width, column_width, 1
    )
    column_block = lax.all_gather(own_columns, "fsdp", axis=0, tiled=True)
    return jnp.dot(
        heads_flat,
        lax.all_gather(column_block, "ep", axis=1, tiled=True),
        preferred_element_type=jnp.float32,
    )


def project_paired(mixed_latent, w_uv, w_out):
    pair = [(0, 1), (1, 0)]
    ep = lax.axis_size("ep")
    twins = [(i, i ^ 1) for i in range(ep)]
    side = lax.axis_index("fsdp")
    lane = lax.axis_index("ep") % 2
    rows = w_uv.shape[0] // 2
    mine = lax.ppermute(
        lax.dynamic_slice_in_dim(w_uv, lane * rows, rows, 0), "fsdp", pair
    )
    theirs = lax.ppermute(mine, "ep", twins)
    far = jnp.where(
        lane == 0, jnp.concatenate([mine, theirs], 0), jnp.concatenate([theirs, mine], 0)
    )
    full = jnp.where(side == 0, jnp.concatenate([w_uv, far], 0), jnp.concatenate([far, w_uv], 0))
    heads_flat = up_project(mixed_latent, full)
    width = w_out.shape[0]
    count = heads_flat.shape[0]
    keep = lax.dynamic_slice_in_dim(heads_flat, side * width, width, 1)
    give = lax.dynamic_slice_in_dim(heads_flat, (1 - side) * width, width, 1)
    other = lax.ppermute(give, "fsdp", pair)
    both = jnp.dot(
        jnp.concatenate([other, keep], 0), w_out, preferred_element_type=jnp.float32
    )
    back = lax.ppermute(both[:count].astype(jnp.bfloat16), "fsdp", pair)
    return both, back


def experts(rows, w_gate, w_up, w_down):
    gate_proj = jnp.dot(rows, w_gate, preferred_element_type=jnp.float32)
    up_proj = jnp.dot(rows, w_up, preferred_element_type=jnp.float32)
    activated = (jax.nn.silu(gate_proj) * up_proj).astype(jnp.bfloat16)
    return jnp.dot(activated, w_down, preferred_element_type=jnp.float32).astype(jnp.bfloat16)


def slots_of(own_ids, expert_count, capacity):
    choose = (own_ids[..., None] == jnp.arange(expert_count, dtype=jnp.int32)).astype(jnp.float32)
    assigned = choose.reshape(-1, expert_count)
    earlier = jnp.cumsum(assigned, axis=0) - assigned
    slot_index = jnp.sum(earlier * assigned, axis=-1).reshape(own_ids.shape).astype(jnp.int32)
    return own_ids * capacity + slot_index


def gates_of(normed, router, ids):
    logits = jnp.dot(normed, router, preferred_element_type=jnp.float32)
    choose = ids[..., None] == jnp.arange(router.shape[1], dtype=jnp.int32)
    picked = jnp.sum(jnp.where(choose, logits[:, None, :], 0.0), axis=-1)
    return jax.nn.softmax(picked, axis=-1)


def weighted_rows(weights, rows):
    high = weights.astype(jnp.bfloat16)
    low = (weights - high.astype(jnp.float32)).astype(jnp.bfloat16)
    return jnp.dot(
        jnp.concatenate([high, low], 1),
        jnp.concatenate([rows, rows], 0),
        preferred_element_type=jnp.float32,
    )


def routed_exchanged(normed, target, capacity, router, w_gate, w_up, w_down):
    expert_count = lax.axis_size("ep")
    gate_weights = gates_of(normed, router, target // capacity)
    here = target[..., None] == jnp.arange(expert_count * capacity, dtype=jnp.int32)
    placed = jnp.sum(here.astype(jnp.bfloat16), axis=1)
    combine = jnp.sum(jnp.where(here, gate_weights[..., None], 0.0), axis=1)
    buffers = jnp.einsum("tp,td->pd", placed, normed, preferred_element_type=jnp.float32).astype(
        jnp.bfloat16
    )
    buffers = buffers.reshape(expert_count, capacity, -1)
    received = lax.all_to_all(buffers, "ep", split_axis=0, concat_axis=0, tiled=True)
    result = experts(received.reshape(expert_count * capacity, -1), w_gate, w_up, w_down)
    result = result.reshape(expert_count, capacity, -1)
    returned = lax.all_to_all(result, "ep", split_axis=0, concat_axis=0, tiled=True)
    return weighted_rows(combine, returned.reshape(expert_count * capacity, -1))


def fused(body, outs, *args, vmem=8, flops=0, bytes_accessed=0):
    whole = pl.BlockSpec(memory_space=pltpu.VMEM)
    return pl.pallas_call(
        body,
        out_shape=[jax.ShapeDtypeStruct(shape, dtype) for shape, dtype in outs],
        in_specs=[whole] * len(args),
        out_specs=[whole] * len(outs),
        cost_estimate=pl.CostEstimate(
            flops=flops, bytes_accessed=bytes_accessed, transcendentals=0
        ),
        compiler_params=pltpu.CompilerParams(vmem_limit_bytes=vmem << 20),
    )(*args)


def slot_kernel(expert_count, capacity, *refs):
    sources = len(refs) // 2
    for ids_ref, target_ref in zip(refs[:sources], refs[sources:]):
        ids = ids_ref[...]
        top, count = ids.shape
        level = lax.broadcasted_iota(jnp.int32, (expert_count, count), 0)
        chosen = jnp.zeros((expert_count, count), jnp.float32)
        for k in range(top):
            chosen += (ids[k : k + 1] == level).astype(jnp.float32)
        rows = lax.broadcasted_iota(jnp.int32, (count, count), 0)
        columns = lax.broadcasted_iota(jnp.int32, (count, count), 1)
        ahead = (rows < columns).astype(jnp.float32).astype(jnp.bfloat16)
        earlier = jnp.dot(
            chosen.astype(jnp.bfloat16), ahead, preferred_element_type=jnp.float32
        )
        for k in range(top):
            own = ids[k : k + 1]
            slot = jnp.sum(jnp.where(own == level, earlier, 0.0), axis=0, keepdims=True)
            target_ref[k : k + 1] = own * capacity + slot.astype(jnp.int32)


def matches(target, capacity, place):
    top, count = target.shape
    row = lax.broadcasted_iota(jnp.int32, (4 * capacity, count), 0)
    slot = jnp.zeros_like(row)
    for j in range(4):
        inside = (row >= j * capacity) & (row < (j + 1) * capacity)
        slot = jnp.where(inside, (place ^ j) * capacity + row - j * capacity, slot)
    found = jnp.zeros(row.shape, jnp.float32)
    for k in range(top):
        found += (target[k : k + 1] == slot).astype(jnp.float32)
    return found


def pick_kernel(capacity, sources, *refs):
    place = lax.axis_index("ep")
    position = 0
    out = refs[-4:]
    for n, pieces in enumerate(sources):
        found = matches(refs[position][...], capacity, place).astype(jnp.bfloat16)
        offset = 0
        for ref in refs[position + 1 : position + 1 + pieces]:
            rows = jnp.dot(found, ref[...], preferred_element_type=jnp.float32)
            rows = rows.astype(jnp.bfloat16)
            columns = slice(offset, offset + ref.shape[1])
            offset += ref.shape[1]
            for j in range(4):
                out[j][n * capacity : (n + 1) * capacity, columns] = rows[
                    j * capacity : (j + 1) * capacity
                ]
        position += 1 + pieces


def dot_rows(a, b):
    return lax.dot_general(a, b, (((1,), (1,)), ((), ())), preferred_element_type=jnp.float32)


def gate_kernel(capacity, router_ref, *refs):
    place = lax.axis_index("ep")
    expert_count = router_ref.shape[0]
    out = refs[12:]
    half = refs[1].shape[1]
    for n in range(4):
        target_ref, low_ref, high_ref = refs[3 * n : 3 * n + 3]
        target = target_ref[...]
        top, count = target.shape
        logits = dot_rows(router_ref[:, :half], low_ref[...])
        logits += dot_rows(router_ref[:, half:], high_ref[...])
        level = lax.broadcasted_iota(jnp.int32, (expert_count, count), 0)
        first = level * capacity
        chosen = jnp.zeros((expert_count, count), jnp.float32)
        for k in range(top):
            own = target[k : k + 1]
            chosen += ((own >= first) & (own < first + capacity)).astype(jnp.float32)
        inside = chosen > 0
        peak = jnp.max(jnp.where(inside, logits, -jnp.inf), axis=0, keepdims=True)
        power = jnp.where(inside, jnp.exp(logits - peak), 0.0)
        gate = power / jnp.sum(power, axis=0, keepdims=True)
        found = matches(target, capacity, place)
        row = lax.broadcasted_iota(jnp.int32, found.shape, 0)
        for j in range(4):
            own = jnp.sum(jnp.where(level == (place ^ j), gate, 0.0), axis=0, keepdims=True)
            within = (row >= j * capacity) & (row < (j + 1) * capacity)
            found = jnp.where(within, found * own, found)
        out[n][...] = found.T


def norm_kernel(x_ref, both_ref, back_ref, gain_ref, hidden_ref, attended_ref, low_ref, high_ref):
    count, width = hidden_ref.shape
    hidden = x_ref[0].astype(jnp.float32) + (
        both_ref[count:] + back_ref[...].astype(jnp.float32)
    )
    hidden_ref[...] = hidden
    attended_ref[0] = hidden.astype(jnp.bfloat16)
    square = jnp.mean(hidden * hidden, axis=-1, keepdims=True)
    normed = hidden * lax.rsqrt(square + epsilon) * gain_ref[...]
    low_ref[...] = normed[:, : width // 2].astype(jnp.bfloat16)
    high_ref[...] = normed[:, width // 2 :].astype(jnp.bfloat16)


def hidden_units(rows, gate_ref, up_ref):
    active = []
    for start in range(0, gate_ref.shape[0], 256):
        part = slice(start, min(start + 256, gate_ref.shape[0]))
        gate = dot_rows(rows, gate_ref[part])
        up = dot_rows(rows, up_ref[part])
        active.append((gate / (1.0 + jnp.exp(-gate)) * up).astype(jnp.bfloat16))
    return jnp.concatenate(active, 1)


def near_expert_kernel(capacity, *refs):
    first, second, own = refs[0:4], refs[4:8], refs[8:12]
    gate_ref, up_ref, down_ref = refs[12:15]
    out_first, out_second, out_own = refs[15:19], refs[19:23], refs[23:27]
    rows = [
        jnp.concatenate([a[:capacity], b[:capacity]], 1) for a, b in zip(first, second)
    ]
    rows += [
        jnp.concatenate([b[capacity:], a[capacity:]], 1) for a, b in zip(first, second)
    ]
    rows += [ref[...] for ref in own]
    active = hidden_units(jnp.concatenate(rows, 0), gate_ref, up_ref)
    width = down_ref.shape[1]
    step = width // 4
    for start in range(0, width, step):
        result = jnp.dot(
            active, down_ref[:, start : start + step], preferred_element_type=jnp.float32
        ).astype(jnp.bfloat16)
        low = start < width // 2
        columns = slice(start % (width // 2), start % (width // 2) + step)
        for j in range(4):
            blocks = [
                result[(4 * n + j) * capacity : (4 * n + j + 1) * capacity] for n in range(3)
            ]
            before_out, after_out = (out_first, out_second) if low else (out_second, out_first)
            before_out[j][:capacity, columns] = blocks[0]
            after_out[j][capacity:, columns] = blocks[1]
            out_own[j][:, start : start + step] = blocks[2]


def far_expert_kernel(*refs):
    gate_ref, up_ref, down_ref = refs[4:7]
    rows = jnp.concatenate([ref[...] for ref in refs[:4]], 0)
    active = hidden_units(rows, gate_ref, up_ref)
    capacity = refs[0].shape[0]
    for start in range(0, down_ref.shape[1], 512):
        part = slice(start, start + 512)
        result = jnp.dot(active, down_ref[:, part], preferred_element_type=jnp.float32)
        result = result.astype(jnp.bfloat16)
        for j in range(4):
            refs[7 + j][:, part] = result[j * capacity : (j + 1) * capacity]


def weigh(weights, rows):
    high = weights.astype(jnp.bfloat16)
    low = (weights - high.astype(jnp.float32)).astype(jnp.bfloat16)
    return jnp.dot(high, rows, preferred_element_type=jnp.float32) + jnp.dot(
        low, rows, preferred_element_type=jnp.float32
    )


def far_kernel(weights_ref, r0, r1, r2, r3, low_ref, high_ref):
    rows = jnp.concatenate([r[...] for r in (r0, r1, r2, r3)], 0)
    total = weigh(weights_ref[...], rows)
    half = low_ref.shape[1]
    low_ref[...] = total[:, :half].astype(jnp.bfloat16)
    high_ref[...] = total[:, half:].astype(jnp.bfloat16)


def near_kernel(capacity, before_w, after_w, r0, r1, r2, r3, *refs):
    blocks = (r0, r1, r2, r3)
    adds = refs[:-2]
    for n, weights in enumerate((before_w, after_w)):
        rows = jnp.concatenate([r[n * capacity : (n + 1) * capacity] for r in blocks], 0)
        total = weigh(weights[...], rows)
        if adds:
            total += adds[n][...].astype(jnp.float32)
        refs[len(adds) + n][...] = total.astype(jnp.bfloat16)


def last_kernel(hidden_ref, weights_ref, r0, r1, r2, r3, x_low, x_high, y_low, y_high, out_ref):
    rows = jnp.concatenate([r[...] for r in (r0, r1, r2, r3)], 0)
    total = hidden_ref[...] + weigh(weights_ref[...], rows)
    half = x_low.shape[1]
    low = x_low[...].astype(jnp.float32) + y_low[...].astype(jnp.float32)
    high = x_high[...].astype(jnp.float32) + y_high[...].astype(jnp.float32)
    out_ref[:, :half] = (total[:, :half] + low).astype(jnp.bfloat16)
    out_ref[:, half:] = (total[:, half:] + high).astype(jnp.bfloat16)


def routed_ringed(hidden, low, high, targets, capacity, router, w_gate, w_up, w_down):
    onward, backward = ring_steps()
    traded = [[(i, i ^ j) for i in range(16)] for j in range(4)]
    count, half = low.shape
    width = 2 * half
    bf16 = jnp.bfloat16

    def send(value, steps):
        return lax.ppermute(value, "ep", steps)

    def pick(*sources):
        n = len(sources)
        columns = sum(part.shape[1] for part in sources[0][1:])
        return fused(
            functools.partial(pick_kernel, capacity, [len(source) - 1 for source in sources]),
            [((n * capacity, columns), bf16)] * 4,
            *[part for source in sources for part in source],
            flops=n * 2 * 4 * capacity * count * columns,
            bytes_accessed=n * 4 * columns * (count + 4 * capacity),
        )

    def trade(blocks):
        return [blocks[0]] + [send(blocks[j], traded[j]) for j in (1, 2, 3)]

    own_slots, before_slots, after_slots, far_slots = targets
    before_low, after_high = send(low, onward), send(high, backward)
    before_high, after_low = send(high, onward), send(low, backward)
    own_rows = trade(pick((own_slots, low, high)))
    far_low, far_high = send(before_low, onward), send(after_high, backward)
    first_rows = trade(pick((before_slots, before_low), (after_slots, after_high)))
    before_high, after_low, own_rows, first_rows[0] = lax.optimization_barrier(
        (before_high, after_low, own_rows, first_rows[0])
    )
    second_rows = trade(pick((before_slots, before_high), (after_slots, after_low)))
    far_rows = trade(pick((far_slots, far_low, far_high)))
    expert_weights = (jnp.swapaxes(w_gate[0], 0, 1), jnp.swapaxes(w_up[0], 0, 1), w_down[0])
    hidden_width = w_gate.shape[2]
    unit = width * hidden_width
    far_rows[0], far_low, far_high = lax.optimization_barrier((far_rows[0], far_low, far_high))
    slots = (count, 4 * capacity)
    weights = fused(
        functools.partial(gate_kernel, capacity),
        [(slots, jnp.float32)] * 4,
        router.T,
        *(own_slots, low, high),
        *(before_slots, before_low, before_high),
        *(after_slots, after_low, after_high),
        *(far_slots, far_low, far_high),
        flops=8 * count * width * 16,
        bytes_accessed=16 * count * width,
    )
    own_rows, weights = lax.optimization_barrier((own_rows, weights))
    blocks = first_rows + second_rows + own_rows
    near = fused(
        functools.partial(near_expert_kernel, capacity),
        [(b.shape, bf16) for b in blocks],
        *blocks,
        *expert_weights,
        vmem=16,
        flops=6 * 12 * capacity * unit,
        bytes_accessed=6 * unit + 4 * 12 * capacity * width,
    )
    near, far_rows = lax.optimization_barrier((near, far_rows))
    result = fused(
        far_expert_kernel,
        [(b.shape, bf16) for b in far_rows],
        *far_rows,
        *expert_weights,
        vmem=16,
        flops=6 * 4 * capacity * unit,
        bytes_accessed=6 * unit + 4 * 4 * capacity * width,
    )
    spent = 2 * 4 * 4 * capacity * count * width
    moved = 4 * width * (count + 4 * capacity)
    piece = ((count, half), bf16)
    far_low, far_high = fused(
        far_kernel,
        [piece] * 2,
        weights[3],
        *trade(result),
        flops=spent,
        bytes_accessed=moved,
    )
    add_low, add_high = send(far_low, onward), send(far_high, backward)

    def near_sums(rows, *adds):
        return fused(
            functools.partial(near_kernel, capacity),
            [piece] * 2,
            weights[1],
            weights[2],
            *trade(rows),
            *adds,
            flops=spent,
            bytes_accessed=moved,
        )

    before_sum, after_sum = near_sums(near[0:4])
    from_after_low = send(before_sum, backward)
    from_before_high = send(after_sum, onward)
    before_sum, after_sum = near_sums(near[4:8], add_high, add_low)
    from_after_high = send(before_sum, backward)
    from_before_low = send(after_sum, onward)
    return fused(
        last_kernel,
        [((count, width), bf16)],
        hidden,
        weights[0],
        *trade(near[8:12]),
        from_before_low,
        from_before_high,
        from_after_low,
        from_after_high,
        flops=spent,
        bytes_accessed=2 * moved,
    )[0]


def ring_steps():
    order = (0, 1, 3, 2)
    onward = [
        (order[i] * 4 + j, order[(i + 1) % 4] * 4 + j) for i in range(4) for j in range(4)
    ]
    return onward, [(b, a) for a, b in onward]


def per_device(
    x_resid,
    q_latent,
    q_rope,
    cache_latent,
    cache_rope,
    new_latent,
    new_rope,
    w_uv,
    w_out,
    norm_gain,
    router,
    expert_ids,
    w_gate,
    w_up,
    w_down,
):
    mixed_latent = attend_local(
        q_latent[0], q_rope[0], cache_latent[0], cache_rope[0], new_latent[0], new_rope[0]
    )
    new_count = mixed_latent.shape[0]
    expert_count = lax.axis_size("ep")
    capacity = new_count * expert_ids.shape[2] // expert_count
    if lax.axis_size("fsdp") != 2 or expert_count != 16:
        projected = project_gathered(mixed_latent, w_uv, w_out)
        hidden = x_resid[0].astype(jnp.float32) + projected
        normed = hidden * lax.rsqrt(jnp.mean(hidden * hidden, axis=-1, keepdims=True) + epsilon)
        normed = (normed * norm_gain).astype(jnp.bfloat16)
        target = slots_of(expert_ids[0], expert_count, capacity)
        routed_sum = routed_exchanged(
            normed, target, capacity, router, w_gate[0], w_up[0], w_down[0]
        )
        layer_out = (hidden + routed_sum).astype(jnp.bfloat16)
        return (hidden.astype(jnp.bfloat16)[None], layer_out[None])
    onward, backward = ring_steps()
    ids = [expert_ids[0].T]
    across = [(i, i ^ 12) for i in range(16)]
    ids += [lax.ppermute(ids[0], "ep", steps) for steps in (onward, backward, across)]
    targets = fused(
        functools.partial(slot_kernel, expert_count, capacity),
        [(part.shape, jnp.int32) for part in ids],
        *ids,
    )
    both, back = project_paired(mixed_latent, w_uv, w_out)
    back, targets = lax.optimization_barrier((back, targets))
    width = both.shape[1]
    halves = (new_count, width // 2)
    hidden, attended, low, high = fused(
        norm_kernel,
        [
            ((new_count, width), jnp.float32),
            ((1, new_count, width), jnp.bfloat16),
            (halves, jnp.bfloat16),
            (halves, jnp.bfloat16),
        ],
        x_resid,
        both,
        back,
        norm_gain[None],
        flops=8 * new_count * width,
        bytes_accessed=20 * new_count * width,
    )
    layer_out = routed_ringed(
        hidden, low, high, targets, capacity, router, w_gate, w_up, w_down
    )
    return (attended, layer_out[None])


def solution(mesh):
    placed = (
        P(("fsdp", "ep"), None, None),
        P(("fsdp", "ep"), None, None, None),
        P(("fsdp", "ep"), None, None, None),
        P(("fsdp", "ep"), None, None),
        P(("fsdp", "ep"), None, None),
        P(("fsdp", "ep"), None, None),
        P(("fsdp", "ep"), None, None),
        P("fsdp", None, None),
        P("fsdp", None),
        P(),
        P(),
        P(("fsdp", "ep"), None, None),
        P("ep", None, None),
        P("ep", None, None),
        P("ep", None, None),
    )

    return jax.shard_map(
        per_device,
        mesh=mesh,
        in_specs=placed,
        out_specs=(P(("fsdp", "ep"), None, None), P(("fsdp", "ep"), None, None)),
        check_vma=False,
    )
```

```python
import functools

import jax
import jax.numpy as jnp
from jax import lax
from jax.experimental import pallas as pl
from jax.experimental.pallas import tpu as pltpu
from jax.sharding import PartitionSpec as P


softmax_scale = 0.07216878364870323
epsilon = 1e-06


def attend_local(q_latent, q_rope, cache_latent, cache_rope, new_latent, new_rope):
    new_count, head_count, latent_width = q_latent.shape
    cache_count = cache_latent.shape[0]
    keys_latent = jnp.concatenate([cache_latent, new_latent], 0)
    keys_rope = jnp.concatenate([cache_rope, new_rope], 0)
    query_rows = q_latent.reshape(new_count * head_count, latent_width)
    rope_rows = q_rope.reshape(new_count * head_count, q_rope.shape[2])
    scores = jnp.dot(query_rows, keys_latent.T, preferred_element_type=jnp.float32)
    scores = (
        scores + jnp.dot(rope_rows, keys_rope.T, preferred_element_type=jnp.float32)
    ) * softmax_scale
    token_of_row = jnp.arange(new_count * head_count, dtype=jnp.int32) // head_count
    key_index = jnp.arange(keys_latent.shape[0], dtype=jnp.int32)
    visible = key_index[None, :] <= token_of_row[:, None] + cache_count
    row_top = jnp.max(jnp.where(visible, scores, -jnp.inf), axis=1, keepdims=True)
    exponent = jnp.where(visible, jnp.exp(scores - row_top), 0.0)
    weights_att = (exponent / jnp.sum(exponent, axis=1, keepdims=True)).astype(jnp.bfloat16)
    mixed_latent = jnp.dot(weights_att, keys_latent, preferred_element_type=jnp.float32).astype(
        jnp.bfloat16
    )
    return mixed_latent.reshape(new_count, head_count, latent_width)


def up_project(mixed_latent, w_uv):
    heads_out = jnp.einsum(
        "thl,lhv->thv", mixed_latent, w_uv, preferred_element_type=jnp.float32
    )
    return heads_out.astype(jnp.bfloat16).reshape(mixed_latent.shape[0], -1)


def project_gathered(mixed_latent, w_uv, w_out):
    heads_flat = up_project(mixed_latent, lax.all_gather(w_uv, "fsdp", axis=0, tiled=True))
    column_width = w_out.shape[1] // lax.axis_size("ep")
    own_columns = lax.dynamic_slice_in_dim(
        w_out, lax.axis_index("ep") * column_width, column_width, 1
    )
    column_block = lax.all_gather(own_columns, "fsdp", axis=0, tiled=True)
    return jnp.dot(
        heads_flat,
        lax.all_gather(column_block, "ep", axis=1, tiled=True),
        preferred_element_type=jnp.float32,
    )


def project_paired(mixed_latent, w_uv, w_out):
    pair = [(0, 1), (1, 0)]
    ep = lax.axis_size("ep")
    twins = [(i, i ^ 1) for i in range(ep)]
    side = lax.axis_index("fsdp")
    lane = lax.axis_index("ep") % 2
    rows, depth = w_uv.shape[0] // 2, w_uv.shape[2]
    heads = w_out.shape[0] // depth

    def own_heads(array, which):
        return lax.dynamic_slice_in_dim(array, which * heads, heads, 1)

    mine = lax.ppermute(
        lax.dynamic_slice(
            w_uv, (lane * rows, (1 - side) * heads, 0), (rows, heads, depth)
        ),
        "fsdp",
        pair,
    )
    other = lax.ppermute(own_heads(mixed_latent, 1 - side), "fsdp", pair)
    theirs = lax.ppermute(mine, "ep", twins)
    far = jnp.where(
        lane == 0, jnp.concatenate([mine, theirs], 0), jnp.concatenate([theirs, mine], 0)
    )
    near = own_heads(w_uv, side)
    full = jnp.where(side == 0, jnp.concatenate([near, far], 0), jnp.concatenate([far, near], 0))
    partial = jnp.dot(up_project(other, full), w_out, preferred_element_type=jnp.float32)
    back = lax.ppermute(partial.astype(jnp.bfloat16), "fsdp", pair)
    kept = up_project(own_heads(mixed_latent, side), full)
    return jnp.dot(kept, w_out, preferred_element_type=jnp.float32), back


def experts(rows, w_gate, w_up, w_down):
    gate_proj = jnp.dot(rows, w_gate, preferred_element_type=jnp.float32)
    up_proj = jnp.dot(rows, w_up, preferred_element_type=jnp.float32)
    activated = (jax.nn.silu(gate_proj) * up_proj).astype(jnp.bfloat16)
    return jnp.dot(activated, w_down, preferred_element_type=jnp.float32).astype(jnp.bfloat16)


def slots_of(own_ids, expert_count, capacity):
    choose = (own_ids[..., None] == jnp.arange(expert_count, dtype=jnp.int32)).astype(jnp.float32)
    assigned = choose.reshape(-1, expert_count)
    earlier = jnp.cumsum(assigned, axis=0) - assigned
    slot_index = jnp.sum(earlier * assigned, axis=-1).reshape(own_ids.shape).astype(jnp.int32)
    return own_ids * capacity + slot_index


def gates_of(normed, router, ids):
    logits = jnp.dot(normed, router, preferred_element_type=jnp.float32)
    choose = ids[..., None] == jnp.arange(router.shape[1], dtype=jnp.int32)
    picked = jnp.sum(jnp.where(choose, logits[:, None, :], 0.0), axis=-1)
    return jax.nn.softmax(picked, axis=-1)


def weighted_rows(weights, rows):
    high = weights.astype(jnp.bfloat16)
    low = (weights - high.astype(jnp.float32)).astype(jnp.bfloat16)
    return jnp.dot(
        jnp.concatenate([high, low], 1),
        jnp.concatenate([rows, rows], 0),
        preferred_element_type=jnp.float32,
    )


def routed_exchanged(normed, target, capacity, router, w_gate, w_up, w_down):
    expert_count = lax.axis_size("ep")
    gate_weights = gates_of(normed, router, target // capacity)
    here = target[..., None] == jnp.arange(expert_count * capacity, dtype=jnp.int32)
    placed = jnp.sum(here.astype(jnp.bfloat16), axis=1)
    combine = jnp.sum(jnp.where(here, gate_weights[..., None], 0.0), axis=1)
    buffers = jnp.einsum("tp,td->pd", placed, normed, preferred_element_type=jnp.float32).astype(
        jnp.bfloat16
    )
    buffers = buffers.reshape(expert_count, capacity, -1)
    received = lax.all_to_all(buffers, "ep", split_axis=0, concat_axis=0, tiled=True)
    result = experts(received.reshape(expert_count * capacity, -1), w_gate, w_up, w_down)
    result = result.reshape(expert_count, capacity, -1)
    returned = lax.all_to_all(result, "ep", split_axis=0, concat_axis=0, tiled=True)
    return weighted_rows(combine, returned.reshape(expert_count * capacity, -1))


def fused(body, outs, *args, vmem=8, flops=0, bytes_accessed=0):
    whole = pl.BlockSpec(memory_space=pltpu.VMEM)
    return pl.pallas_call(
        body,
        out_shape=[jax.ShapeDtypeStruct(shape, dtype) for shape, dtype in outs],
        in_specs=[whole] * len(args),
        out_specs=[whole] * len(outs),
        cost_estimate=pl.CostEstimate(
            flops=flops, bytes_accessed=bytes_accessed, transcendentals=0
        ),
        compiler_params=pltpu.CompilerParams(vmem_limit_bytes=vmem << 20),
    )(*args)


def slot_kernel(expert_count, capacity, *refs):
    sources = len(refs) // 2
    for ids_ref, target_ref in zip(refs[:sources], refs[sources:]):
        ids = ids_ref[...]
        top, count = ids.shape
        level = lax.broadcasted_iota(jnp.int32, (expert_count, count), 0)
        chosen = jnp.zeros((expert_count, count), jnp.float32)
        for k in range(top):
            chosen += (ids[k : k + 1] == level).astype(jnp.float32)
        rows = lax.broadcasted_iota(jnp.int32, (count, count), 0)
        columns = lax.broadcasted_iota(jnp.int32, (count, count), 1)
        ahead = (rows < columns).astype(jnp.float32).astype(jnp.bfloat16)
        earlier = jnp.dot(
            chosen.astype(jnp.bfloat16), ahead, preferred_element_type=jnp.float32
        )
        for k in range(top):
            own = ids[k : k + 1]
            slot = jnp.sum(jnp.where(own == level, earlier, 0.0), axis=0, keepdims=True)
            target_ref[k : k + 1] = own * capacity + slot.astype(jnp.int32)


def matches(target, capacity, place):
    top, count = target.shape
    row = lax.broadcasted_iota(jnp.int32, (4 * capacity, count), 0)
    slot = jnp.zeros_like(row)
    for j in range(4):
        inside = (row >= j * capacity) & (row < (j + 1) * capacity)
        slot = jnp.where(inside, (place ^ j) * capacity + row - j * capacity, slot)
    found = jnp.zeros(row.shape, jnp.float32)
    for k in range(top):
        found += (target[k : k + 1] == slot).astype(jnp.float32)
    return found


def pick_kernel(capacity, sources, *refs):
    place = lax.axis_index("ep")
    position = 0
    local_ref, twin_ref, cross_ref = refs[-3:]
    count = len(sources)
    for n, pieces in enumerate(sources):
        found = matches(refs[position][...], capacity, place).astype(jnp.bfloat16)
        offset = 0
        spots = ((local_ref, n), (twin_ref, n), (cross_ref, n), (cross_ref, count + n))
        for ref in refs[position + 1 : position + 1 + pieces]:
            rows = jnp.dot(found, ref[...], preferred_element_type=jnp.float32)
            rows = rows.astype(jnp.bfloat16)
            columns = slice(offset, offset + ref.shape[1])
            offset += ref.shape[1]
            for j, (out, spot) in enumerate(spots):
                out[spot * capacity : (spot + 1) * capacity, columns] = rows[
                    j * capacity : (j + 1) * capacity
                ]
        position += 1 + pieces


def join_kernel(own_ref, got_ref, out_ref):
    count = own_ref.shape[0]
    out_ref[:count] = own_ref[...]
    out_ref[count:] = got_ref[count:]


def dot_rows(a, b):
    return lax.dot_general(a, b, (((1,), (1,)), ((), ())), preferred_element_type=jnp.float32)


def gate_kernel(capacity, router_ref, *refs):
    place = lax.axis_index("ep")
    expert_count = router_ref.shape[0]
    out = refs[12:]
    half = refs[1].shape[1]
    for n in range(4):
        target_ref, low_ref, high_ref = refs[3 * n : 3 * n + 3]
        target = target_ref[...]
        top, count = target.shape
        logits = dot_rows(router_ref[:, :half], low_ref[...])
        logits += dot_rows(router_ref[:, half:], high_ref[...])
        level = lax.broadcasted_iota(jnp.int32, (expert_count, count), 0)
        first = level * capacity
        chosen = jnp.zeros((expert_count, count), jnp.float32)
        for k in range(top):
            own = target[k : k + 1]
            chosen += ((own >= first) & (own < first + capacity)).astype(jnp.float32)
        inside = chosen > 0
        peak = jnp.max(jnp.where(inside, logits, -jnp.inf), axis=0, keepdims=True)
        power = jnp.where(inside, jnp.exp(logits - peak), 0.0)
        gate = power / jnp.sum(power, axis=0, keepdims=True)
        found = matches(target, capacity, place)
        row = lax.broadcasted_iota(jnp.int32, found.shape, 0)
        for j in range(4):
            own = jnp.sum(jnp.where(level == (place ^ j), gate, 0.0), axis=0, keepdims=True)
            within = (row >= j * capacity) & (row < (j + 1) * capacity)
            found = jnp.where(within, found * own, found)
        out[n][...] = found.T


def norm_kernel(x_ref, part_ref, back_ref, gain_ref, hidden_ref, attended_ref, low_ref, high_ref):
    width = hidden_ref.shape[1]
    hidden = x_ref[0].astype(jnp.float32) + (
        part_ref[...] + back_ref[...].astype(jnp.float32)
    )
    hidden_ref[...] = hidden
    attended_ref[0] = hidden.astype(jnp.bfloat16)
    square = jnp.mean(hidden * hidden, axis=-1, keepdims=True)
    normed = hidden * lax.rsqrt(square + epsilon) * gain_ref[...]
    low_ref[...] = normed[:, : width // 2].astype(jnp.bfloat16)
    high_ref[...] = normed[:, width // 2 :].astype(jnp.bfloat16)


def hidden_units(rows, gate_ref, up_ref):
    active = []
    for start in range(0, gate_ref.shape[0], 256):
        part = slice(start, min(start + 256, gate_ref.shape[0]))
        gate = dot_rows(rows, gate_ref[part])
        up = dot_rows(rows, up_ref[part])
        active.append((gate / (1.0 + jnp.exp(-gate)) * up).astype(jnp.bfloat16))
    return jnp.concatenate(active, 1)


def arrived(local_ref, got_ref, traded_ref):
    count = local_ref.shape[0]
    return jnp.concatenate([local_ref[...], got_ref[:count], traded_ref[...]], 0)


def near_expert_kernel(capacity, *refs):
    first, second, own = (arrived(*refs[n : n + 3]) for n in (0, 3, 6))
    gate_ref, up_ref, down_ref = refs[9:12]
    first_out, second_out, own_out = refs[12:15], refs[15:18], refs[18:21]
    rows = []
    for n in range(8):
        part = slice(n * capacity, (n + 1) * capacity)
        pieces = (first[part], second[part]) if n % 2 == 0 else (second[part], first[part])
        rows.append(jnp.concatenate(pieces, 1))
    active = hidden_units(jnp.concatenate(rows + [own], 0), gate_ref, up_ref)
    width = down_ref.shape[1]
    step = width // 4
    for start in range(0, width, step):
        result = jnp.dot(
            active, down_ref[:, start : start + step], preferred_element_type=jnp.float32
        ).astype(jnp.bfloat16)
        columns = slice(start % (width // 2), start % (width // 2) + step)
        for n in range(8):
            block = result[n * capacity : (n + 1) * capacity]
            outs = first_out if (start < width // 2) == (n % 2 == 0) else second_out
            out = outs[min(n // 2, 2)]
            spot = n % 2 if n < 6 else n - 4
            out[spot * capacity : (spot + 1) * capacity, columns] = block
        for n in range(4):
            block = result[(8 + n) * capacity : (9 + n) * capacity]
            out = own_out[min(n, 2)]
            spot = max(n - 2, 0)
            out[spot * capacity : (spot + 1) * capacity, start : start + step] = block


def far_expert_kernel(local_ref, got_ref, traded_ref, gate_ref, up_ref, down_ref, *outs):
    active = hidden_units(arrived(local_ref, got_ref, traded_ref), gate_ref, up_ref)
    capacity = local_ref.shape[0]
    for start in range(0, down_ref.shape[1], 512):
        part = slice(start, start + 512)
        result = jnp.dot(active, down_ref[:, part], preferred_element_type=jnp.float32)
        result = result.astype(jnp.bfloat16)
        outs[0][:, part] = result[:capacity]
        outs[1][:, part] = result[capacity : 2 * capacity]
        outs[2][:, part] = result[2 * capacity :]


def weigh(weights, rows):
    high = weights.astype(jnp.bfloat16)
    low = (weights - high.astype(jnp.float32)).astype(jnp.bfloat16)
    return jnp.dot(high, rows, preferred_element_type=jnp.float32) + jnp.dot(
        low, rows, preferred_element_type=jnp.float32
    )


def returned(local_ref, got_ref, cross_ref, n, capacity):
    count = local_ref.shape[0]
    part = slice(n * capacity, (n + 1) * capacity)
    late = slice(count + n * capacity, count + (n + 1) * capacity)
    return jnp.concatenate(
        [local_ref[part], got_ref[part], cross_ref[part], cross_ref[late]], 0
    )


def far_kernel(weights_ref, local_ref, got_ref, cross_ref, low_ref, high_ref):
    rows = returned(local_ref, got_ref, cross_ref, 0, local_ref.shape[0])
    total = weigh(weights_ref[...], rows)
    half = low_ref.shape[1]
    low_ref[...] = total[:, :half].astype(jnp.bfloat16)
    high_ref[...] = total[:, half:].astype(jnp.bfloat16)


def near_kernel(capacity, before_w, after_w, local_ref, got_ref, cross_ref, *refs):
    adds = refs[:-2]
    for n, weights in enumerate((before_w, after_w)):
        total = weigh(weights[...], returned(local_ref, got_ref, cross_ref, n, capacity))
        if adds:
            total += adds[n][...].astype(jnp.float32)
        refs[len(adds) + n][...] = total.astype(jnp.bfloat16)


def last_kernel(
    hidden_ref,
    weights_ref,
    local_ref,
    got_ref,
    cross_ref,
    x_low,
    x_high,
    y_low,
    y_high,
    out_ref,
):
    rows = returned(local_ref, got_ref, cross_ref, 0, local_ref.shape[0])
    total = hidden_ref[...] + weigh(weights_ref[...], rows)
    half = x_low.shape[1]
    low = x_low[...].astype(jnp.float32) + y_low[...].astype(jnp.float32)
    high = x_high[...].astype(jnp.float32) + y_high[...].astype(jnp.float32)
    out_ref[:, :half] = (total[:, :half] + low).astype(jnp.bfloat16)
    out_ref[:, half:] = (total[:, half:] + high).astype(jnp.bfloat16)


def routed_ringed(hidden, low, high, targets, capacity, router, w_gate, w_up, w_down):
    onward, backward = ring_steps()
    over_core, over_y = ([(i, i ^ j) for i in range(16)] for j in (1, 2))
    count, half = low.shape
    width = 2 * half
    bf16 = jnp.bfloat16

    def send(value, steps):
        return lax.ppermute(value, "ep", steps)

    def pick(*sources):
        n = len(sources)
        columns = sum(part.shape[1] for part in sources[0][1:])
        return fused(
            functools.partial(pick_kernel, capacity, [len(source) - 1 for source in sources]),
            [((m * capacity, columns), bf16) for m in (n, n, 2 * n)],
            *[part for source in sources for part in source],
            flops=n * 2 * 4 * capacity * count * columns,
            bytes_accessed=n * 4 * columns * (count + 4 * capacity),
        )

    def join(own, got):
        return fused(
            join_kernel,
            [(got.shape, bf16)],
            own,
            got,
            bytes_accessed=4 * got.shape[0] * got.shape[1],
        )[0]

    def trade(blocks):
        local, twin, cross = blocks
        got = send(cross, over_y)
        return [local, got, send(join(twin, got), over_core)]

    def untrade(blocks):
        local, cross, twin = blocks
        got = send(twin, over_core)
        return [local, got, send(join(cross, got), over_y)]

    own_slots, before_slots, after_slots, far_slots = targets
    before_low, after_high = send(low, onward), send(high, backward)
    before_high, after_low = send(high, onward), send(low, backward)
    own_rows = trade(pick((own_slots, low, high)))
    far_low, far_high = send(before_low, onward), send(after_high, backward)
    first_rows = trade(pick((before_slots, before_low), (after_slots, after_high)))
    second_rows = trade(pick((before_slots, before_high), (after_slots, after_low)))
    far_rows = trade(pick((far_slots, far_low, far_high)))
    expert_weights = (jnp.swapaxes(w_gate[0], 0, 1), jnp.swapaxes(w_up[0], 0, 1), w_down[0])
    hidden_width = w_gate.shape[2]
    unit = width * hidden_width
    far_rows[0], far_low, far_high = lax.optimization_barrier((far_rows[0], far_low, far_high))
    slots = (count, 4 * capacity)
    weights = fused(
        functools.partial(gate_kernel, capacity),
        [(slots, jnp.float32)] * 4,
        router.T,
        *(own_slots, low, high),
        *(before_slots, before_low, before_high),
        *(after_slots, after_low, after_high),
        *(far_slots, far_low, far_high),
        flops=8 * count * width * 16,
        bytes_accessed=16 * count * width,
    )
    own_rows, weights = lax.optimization_barrier((own_rows, weights))
    blocks = first_rows + second_rows + own_rows
    outs = []
    for local, _, twin in (first_rows, second_rows, own_rows):
        outs += [(local.shape, bf16), (local.shape, bf16), (twin.shape, bf16)]
    near = fused(
        functools.partial(near_expert_kernel, capacity),
        outs,
        *blocks,
        *expert_weights,
        vmem=16,
        flops=6 * 12 * capacity * unit,
        bytes_accessed=6 * unit + 4 * 12 * capacity * width,
    )
    result = fused(
        far_expert_kernel,
        [(far_rows[n].shape, bf16) for n in (0, 0, 2)],
        *far_rows,
        *expert_weights,
        vmem=16,
        flops=6 * 4 * capacity * unit,
        bytes_accessed=6 * unit + 4 * 4 * capacity * width,
    )
    spent = 2 * 4 * 4 * capacity * count * width
    moved = 4 * width * (count + 4 * capacity)
    piece = ((count, half), bf16)
    far_low, far_high = fused(
        far_kernel,
        [piece] * 2,
        weights[3],
        *untrade(result),
        flops=spent,
        bytes_accessed=moved,
    )
    add_low, add_high = send(far_low, onward), send(far_high, backward)

    def near_sums(rows, *adds):
        return fused(
            functools.partial(near_kernel, capacity),
            [piece] * 2,
            weights[1],
            weights[2],
            *untrade(rows),
            *adds,
            flops=spent,
            bytes_accessed=moved,
        )

    before_sum, after_sum = near_sums(near[0:3])
    from_after_low = send(before_sum, backward)
    from_before_high = send(after_sum, onward)
    before_sum, after_sum = near_sums(near[3:6], add_high, add_low)
    from_after_high = send(before_sum, backward)
    from_before_low = send(after_sum, onward)
    return fused(
        last_kernel,
        [((count, width), bf16)],
        hidden,
        weights[0],
        *untrade(near[6:9]),
        from_before_low,
        from_before_high,
        from_after_low,
        from_after_high,
        flops=spent,
        bytes_accessed=2 * moved,
    )[0]


def ring_steps():
    order = (0, 1, 3, 2)
    onward = [
        (order[i] * 4 + j, order[(i + 1) % 4] * 4 + j) for i in range(4) for j in range(4)
    ]
    return onward, [(b, a) for a, b in onward]


def per_device(
    x_resid,
    q_latent,
    q_rope,
    cache_latent,
    cache_rope,
    new_latent,
    new_rope,
    w_uv,
    w_out,
    norm_gain,
    router,
    expert_ids,
    w_gate,
    w_up,
    w_down,
):
    mixed_latent = attend_local(
        q_latent[0], q_rope[0], cache_latent[0], cache_rope[0], new_latent[0], new_rope[0]
    )
    new_count = mixed_latent.shape[0]
    expert_count = lax.axis_size("ep")
    capacity = new_count * expert_ids.shape[2] // expert_count
    if lax.axis_size("fsdp") != 2 or expert_count != 16:
        projected = project_gathered(mixed_latent, w_uv, w_out)
        hidden = x_resid[0].astype(jnp.float32) + projected
        normed = hidden * lax.rsqrt(jnp.mean(hidden * hidden, axis=-1, keepdims=True) + epsilon)
        normed = (normed * norm_gain).astype(jnp.bfloat16)
        target = slots_of(expert_ids[0], expert_count, capacity)
        routed_sum = routed_exchanged(
            normed, target, capacity, router, w_gate[0], w_up[0], w_down[0]
        )
        layer_out = (hidden + routed_sum).astype(jnp.bfloat16)
        return (hidden.astype(jnp.bfloat16)[None], layer_out[None])
    onward, backward = ring_steps()
    ids = [expert_ids[0].T]
    across = [(i, i ^ 12) for i in range(16)]
    ids += [lax.ppermute(ids[0], "ep", steps) for steps in (onward, backward, across)]
    targets = fused(
        functools.partial(slot_kernel, expert_count, capacity),
        [(part.shape, jnp.int32) for part in ids],
        *ids,
    )
    part, back = project_paired(mixed_latent, w_uv, w_out)
    back, targets = lax.optimization_barrier((back, targets))
    width = part.shape[1]
    halves = (new_count, width // 2)
    hidden, attended, low, high = fused(
        norm_kernel,
        [
            ((new_count, width), jnp.float32),
            ((1, new_count, width), jnp.bfloat16),
            (halves, jnp.bfloat16),
            (halves, jnp.bfloat16),
        ],
        x_resid,
        part,
        back,
        norm_gain[None],
        flops=8 * new_count * width,
        bytes_accessed=20 * new_count * width,
    )
    layer_out = routed_ringed(
        hidden, low, high, targets, capacity, router, w_gate, w_up, w_down
    )
    return (attended, layer_out[None])


def solution(mesh):
    placed = (
        P(("fsdp", "ep"), None, None),
        P(("fsdp", "ep"), None, None, None),
        P(("fsdp", "ep"), None, None, None),
        P(("fsdp", "ep"), None, None),
        P(("fsdp", "ep"), None, None),
        P(("fsdp", "ep"), None, None),
        P(("fsdp", "ep"), None, None),
        P("fsdp", None, None),
        P("fsdp", None),
        P(),
        P(),
        P(("fsdp", "ep"), None, None),
        P("ep", None, None),
        P("ep", None, None),
        P("ep", None, None),
    )

    return jax.shard_map(
        per_device,
        mesh=mesh,
        in_specs=placed,
        out_specs=(P(("fsdp", "ep"), None, None), P(("fsdp", "ep"), None, None)),
        check_vma=False,
    )
```

```python
import functools

import jax
import jax.numpy as jnp
from jax import lax
from jax.experimental import pallas as pl
from jax.experimental.pallas import tpu as pltpu
from jax.sharding import PartitionSpec as P


softmax_scale = 0.07216878364870323
epsilon = 1e-06


def attend_local(q_latent, q_rope, cache_latent, cache_rope, new_latent, new_rope):
    new_count, head_count, latent_width = q_latent.shape
    cache_count = cache_latent.shape[0]
    keys_latent = jnp.concatenate([cache_latent, new_latent], 0)
    keys_rope = jnp.concatenate([cache_rope, new_rope], 0)
    query_rows = q_latent.reshape(new_count * head_count, latent_width)
    rope_rows = q_rope.reshape(new_count * head_count, q_rope.shape[2])
    scores = jnp.dot(query_rows, keys_latent.T, preferred_element_type=jnp.float32)
    scores = (
        scores + jnp.dot(rope_rows, keys_rope.T, preferred_element_type=jnp.float32)
    ) * softmax_scale
    token_of_row = jnp.arange(new_count * head_count, dtype=jnp.int32) // head_count
    key_index = jnp.arange(keys_latent.shape[0], dtype=jnp.int32)
    visible = key_index[None, :] <= token_of_row[:, None] + cache_count
    row_top = jnp.max(jnp.where(visible, scores, -jnp.inf), axis=1, keepdims=True)
    exponent = jnp.where(visible, jnp.exp(scores - row_top), 0.0)
    weights_att = (exponent / jnp.sum(exponent, axis=1, keepdims=True)).astype(jnp.bfloat16)
    mixed_latent = jnp.dot(weights_att, keys_latent, preferred_element_type=jnp.float32).astype(
        jnp.bfloat16
    )
    return mixed_latent.reshape(new_count, head_count, latent_width)


def up_project(mixed_latent, w_uv):
    heads_out = jnp.einsum(
        "thl,lhv->thv", mixed_latent, w_uv, preferred_element_type=jnp.float32
    )
    return heads_out.astype(jnp.bfloat16).reshape(mixed_latent.shape[0], -1)


def project_gathered(mixed_latent, w_uv, w_out):
    heads_flat = up_project(mixed_latent, lax.all_gather(w_uv, "fsdp", axis=0, tiled=True))
    column_width = w_out.shape[1] // lax.axis_size("ep")
    own_columns = lax.dynamic_slice_in_dim(
        w_out, lax.axis_index("ep") * column_width, column_width, 1
    )
    column_block = lax.all_gather(own_columns, "fsdp", axis=0, tiled=True)
    return jnp.dot(
        heads_flat,
        lax.all_gather(column_block, "ep", axis=1, tiled=True),
        preferred_element_type=jnp.float32,
    )


def project_paired(mixed_latent, w_uv, w_out):
    pair = [(0, 1), (1, 0)]
    ep = lax.axis_size("ep")
    twins = [(i, i ^ 1) for i in range(ep)]
    side = lax.axis_index("fsdp")
    lane = lax.axis_index("ep") % 2
    rows, depth = w_uv.shape[0] // 2, w_uv.shape[2]
    heads = w_out.shape[0] // depth

    def own_heads(array, which):
        return lax.dynamic_slice_in_dim(array, which * heads, heads, 1)

    mine = lax.ppermute(
        lax.dynamic_slice(
            w_uv, (lane * rows, (1 - side) * heads, 0), (rows, heads, depth)
        ),
        "fsdp",
        pair,
    )
    other = lax.ppermute(own_heads(mixed_latent, 1 - side), "fsdp", pair)
    theirs = lax.ppermute(mine, "ep", twins)
    far = jnp.where(
        lane == 0, jnp.concatenate([mine, theirs], 0), jnp.concatenate([theirs, mine], 0)
    )
    near = own_heads(w_uv, side)
    full = jnp.where(side == 0, jnp.concatenate([near, far], 0), jnp.concatenate([far, near], 0))
    partial = jnp.dot(up_project(other, full), w_out, preferred_element_type=jnp.float32)
    back = lax.ppermute(partial.astype(jnp.bfloat16), "fsdp", pair)
    kept = up_project(own_heads(mixed_latent, side), full)
    return jnp.dot(kept, w_out, preferred_element_type=jnp.float32), back


def experts(rows, w_gate, w_up, w_down):
    gate_proj = jnp.dot(rows, w_gate, preferred_element_type=jnp.float32)
    up_proj = jnp.dot(rows, w_up, preferred_element_type=jnp.float32)
    activated = (jax.nn.silu(gate_proj) * up_proj).astype(jnp.bfloat16)
    return jnp.dot(activated, w_down, preferred_element_type=jnp.float32).astype(jnp.bfloat16)


def slots_of(own_ids, expert_count, capacity):
    choose = (own_ids[..., None] == jnp.arange(expert_count, dtype=jnp.int32)).astype(jnp.float32)
    assigned = choose.reshape(-1, expert_count)
    earlier = jnp.cumsum(assigned, axis=0) - assigned
    slot_index = jnp.sum(earlier * assigned, axis=-1).reshape(own_ids.shape).astype(jnp.int32)
    return own_ids * capacity + slot_index


def gates_of(normed, router, ids):
    logits = jnp.dot(normed, router, preferred_element_type=jnp.float32)
    choose = ids[..., None] == jnp.arange(router.shape[1], dtype=jnp.int32)
    picked = jnp.sum(jnp.where(choose, logits[:, None, :], 0.0), axis=-1)
    return jax.nn.softmax(picked, axis=-1)


def weighted_rows(weights, rows):
    high = weights.astype(jnp.bfloat16)
    low = (weights - high.astype(jnp.float32)).astype(jnp.bfloat16)
    return jnp.dot(
        jnp.concatenate([high, low], 1),
        jnp.concatenate([rows, rows], 0),
        preferred_element_type=jnp.float32,
    )


def routed_exchanged(normed, target, capacity, router, w_gate, w_up, w_down):
    expert_count = lax.axis_size("ep")
    gate_weights = gates_of(normed, router, target // capacity)
    here = target[..., None] == jnp.arange(expert_count * capacity, dtype=jnp.int32)
    placed = jnp.sum(here.astype(jnp.bfloat16), axis=1)
    combine = jnp.sum(jnp.where(here, gate_weights[..., None], 0.0), axis=1)
    buffers = jnp.einsum("tp,td->pd", placed, normed, preferred_element_type=jnp.float32).astype(
        jnp.bfloat16
    )
    buffers = buffers.reshape(expert_count, capacity, -1)
    received = lax.all_to_all(buffers, "ep", split_axis=0, concat_axis=0, tiled=True)
    result = experts(received.reshape(expert_count * capacity, -1), w_gate, w_up, w_down)
    result = result.reshape(expert_count, capacity, -1)
    returned = lax.all_to_all(result, "ep", split_axis=0, concat_axis=0, tiled=True)
    return weighted_rows(combine, returned.reshape(expert_count * capacity, -1))


def fused(body, outs, *args, vmem=8, flops=0, bytes_accessed=0):
    whole = pl.BlockSpec(memory_space=pltpu.VMEM)
    return pl.pallas_call(
        body,
        out_shape=[jax.ShapeDtypeStruct(shape, dtype) for shape, dtype in outs],
        in_specs=[whole] * len(args),
        out_specs=[whole] * len(outs),
        cost_estimate=pl.CostEstimate(
            flops=flops, bytes_accessed=bytes_accessed, transcendentals=0
        ),
        compiler_params=pltpu.CompilerParams(vmem_limit_bytes=vmem << 20),
    )(*args)


def slot_kernel(expert_count, capacity, *refs):
    sources = len(refs) // 2
    for ids_ref, target_ref in zip(refs[:sources], refs[sources:]):
        ids = ids_ref[...]
        top, count = ids.shape
        level = lax.broadcasted_iota(jnp.int32, (expert_count, count), 0)
        chosen = jnp.zeros((expert_count, count), jnp.float32)
        for k in range(top):
            chosen += (ids[k : k + 1] == level).astype(jnp.float32)
        rows = lax.broadcasted_iota(jnp.int32, (count, count), 0)
        columns = lax.broadcasted_iota(jnp.int32, (count, count), 1)
        ahead = (rows < columns).astype(jnp.float32).astype(jnp.bfloat16)
        earlier = jnp.dot(
            chosen.astype(jnp.bfloat16), ahead, preferred_element_type=jnp.float32
        )
        for k in range(top):
            own = ids[k : k + 1]
            slot = jnp.sum(jnp.where(own == level, earlier, 0.0), axis=0, keepdims=True)
            target_ref[k : k + 1] = own * capacity + slot.astype(jnp.int32)


def matches(target, capacity, place):
    top, count = target.shape
    row = lax.broadcasted_iota(jnp.int32, (4 * capacity, count), 0)
    slot = jnp.zeros_like(row)
    for j in range(4):
        inside = (row >= j * capacity) & (row < (j + 1) * capacity)
        slot = jnp.where(inside, (place ^ j) * capacity + row - j * capacity, slot)
    found = jnp.zeros(row.shape, jnp.float32)
    for k in range(top):
        found += (target[k : k + 1] == slot).astype(jnp.float32)
    return found


def pick_kernel(capacity, sources, *refs):
    place = lax.axis_index("ep")
    position = 0
    out = refs[-4:]
    for n, pieces in enumerate(sources):
        found = matches(refs[position][...], capacity, place).astype(jnp.bfloat16)
        offset = 0
        for ref in refs[position + 1 : position + 1 + pieces]:
            rows = jnp.dot(found, ref[...], preferred_element_type=jnp.float32)
            rows = rows.astype(jnp.bfloat16)
            columns = slice(offset, offset + ref.shape[1])
            offset += ref.shape[1]
            for j in range(4):
                out[j][n * capacity : (n + 1) * capacity, columns] = rows[
                    j * capacity : (j + 1) * capacity
                ]
        position += 1 + pieces


def dot_rows(a, b):
    return lax.dot_general(a, b, (((1,), (1,)), ((), ())), preferred_element_type=jnp.float32)


def gate_kernel(capacity, router_ref, *refs):
    place = lax.axis_index("ep")
    expert_count = router_ref.shape[0]
    out = refs[12:]
    half = refs[1].shape[1]
    for n in range(4):
        target_ref, low_ref, high_ref = refs[3 * n : 3 * n + 3]
        target = target_ref[...]
        top, count = target.shape
        logits = dot_rows(router_ref[:, :half], low_ref[...])
        logits += dot_rows(router_ref[:, half:], high_ref[...])
        level = lax.broadcasted_iota(jnp.int32, (expert_count, count), 0)
        first = level * capacity
        chosen = jnp.zeros((expert_count, count), jnp.float32)
        for k in range(top):
            own = target[k : k + 1]
            chosen += ((own >= first) & (own < first + capacity)).astype(jnp.float32)
        inside = chosen > 0
        peak = jnp.max(jnp.where(inside, logits, -jnp.inf), axis=0, keepdims=True)
        power = jnp.where(inside, jnp.exp(logits - peak), 0.0)
        gate = power / jnp.sum(power, axis=0, keepdims=True)
        found = matches(target, capacity, place)
        row = lax.broadcasted_iota(jnp.int32, found.shape, 0)
        for j in range(4):
            own = jnp.sum(jnp.where(level == (place ^ j), gate, 0.0), axis=0, keepdims=True)
            within = (row >= j * capacity) & (row < (j + 1) * capacity)
            found = jnp.where(within, found * own, found)
        out[n][...] = found.T


def norm_kernel(x_ref, part_ref, back_ref, gain_ref, hidden_ref, attended_ref, low_ref, high_ref):
    width = hidden_ref.shape[1]
    hidden = x_ref[0].astype(jnp.float32) + (
        part_ref[...] + back_ref[...].astype(jnp.float32)
    )
    hidden_ref[...] = hidden
    attended_ref[0] = hidden.astype(jnp.bfloat16)
    square = jnp.mean(hidden * hidden, axis=-1, keepdims=True)
    normed = hidden * lax.rsqrt(square + epsilon) * gain_ref[...]
    low_ref[...] = normed[:, : width // 2].astype(jnp.bfloat16)
    high_ref[...] = normed[:, width // 2 :].astype(jnp.bfloat16)


def hidden_units(rows, gate_ref, up_ref):
    active = []
    for start in range(0, gate_ref.shape[0], 256):
        part = slice(start, min(start + 256, gate_ref.shape[0]))
        gate = dot_rows(rows, gate_ref[part])
        up = dot_rows(rows, up_ref[part])
        active.append((gate / (1.0 + jnp.exp(-gate)) * up).astype(jnp.bfloat16))
    return jnp.concatenate(active, 1)


def near_expert_kernel(capacity, *refs):
    first, second, own = refs[0:4], refs[4:8], refs[8:12]
    gate_ref, up_ref, down_ref = refs[12:15]
    out_first, out_second, out_own = refs[15:19], refs[19:23], refs[23:27]
    rows = [
        jnp.concatenate([a[:capacity], b[:capacity]], 1) for a, b in zip(first, second)
    ]
    rows += [
        jnp.concatenate([b[capacity:], a[capacity:]], 1) for a, b in zip(first, second)
    ]
    rows += [ref[...] for ref in own]
    active = hidden_units(jnp.concatenate(rows, 0), gate_ref, up_ref)
    width = down_ref.shape[1]
    step = width // 4
    for start in range(0, width, step):
        result = jnp.dot(
            active, down_ref[:, start : start + step], preferred_element_type=jnp.float32
        ).astype(jnp.bfloat16)
        low = start < width // 2
        columns = slice(start % (width // 2), start % (width // 2) + step)
        for j in range(4):
            blocks = [
                result[(4 * n + j) * capacity : (4 * n + j + 1) * capacity] for n in range(3)
            ]
            before_out, after_out = (out_first, out_second) if low else (out_second, out_first)
            before_out[j][:capacity, columns] = blocks[0]
            after_out[j][capacity:, columns] = blocks[1]
            out_own[j][:, start : start + step] = blocks[2]


def far_expert_kernel(*refs):
    gate_ref, up_ref, down_ref = refs[4:7]
    rows = jnp.concatenate([ref[...] for ref in refs[:4]], 0)
    active = hidden_units(rows, gate_ref, up_ref)
    capacity = refs[0].shape[0]
    for start in range(0, down_ref.shape[1], 512):
        part = slice(start, start + 512)
        result = jnp.dot(active, down_ref[:, part], preferred_element_type=jnp.float32)
        result = result.astype(jnp.bfloat16)
        for j in range(4):
            refs[7 + j][:, part] = result[j * capacity : (j + 1) * capacity]


def weigh(weights, rows):
    high = weights.astype(jnp.bfloat16)
    low = (weights - high.astype(jnp.float32)).astype(jnp.bfloat16)
    return jnp.dot(high, rows, preferred_element_type=jnp.float32) + jnp.dot(
        low, rows, preferred_element_type=jnp.float32
    )


def far_kernel(weights_ref, r0, r1, r2, r3, low_ref, high_ref):
    rows = jnp.concatenate([r[...] for r in (r0, r1, r2, r3)], 0)
    total = weigh(weights_ref[...], rows)
    half = low_ref.shape[1]
    low_ref[...] = total[:, :half].astype(jnp.bfloat16)
    high_ref[...] = total[:, half:].astype(jnp.bfloat16)


def near_kernel(capacity, before_w, after_w, r0, r1, r2, r3, *refs):
    blocks = (r0, r1, r2, r3)
    adds = refs[:-2]
    for n, weights in enumerate((before_w, after_w)):
        rows = jnp.concatenate([r[n * capacity : (n + 1) * capacity] for r in blocks], 0)
        total = weigh(weights[...], rows)
        if adds:
            total += adds[n][...].astype(jnp.float32)
        refs[len(adds) + n][...] = total.astype(jnp.bfloat16)


def last_kernel(hidden_ref, weights_ref, r0, r1, r2, r3, x_low, x_high, y_low, y_high, out_ref):
    rows = jnp.concatenate([r[...] for r in (r0, r1, r2, r3)], 0)
    total = hidden_ref[...] + weigh(weights_ref[...], rows)
    half = x_low.shape[1]
    low = x_low[...].astype(jnp.float32) + y_low[...].astype(jnp.float32)
    high = x_high[...].astype(jnp.float32) + y_high[...].astype(jnp.float32)
    out_ref[:, :half] = (total[:, :half] + low).astype(jnp.bfloat16)
    out_ref[:, half:] = (total[:, half:] + high).astype(jnp.bfloat16)


def routed_ringed(hidden, low, high, targets, capacity, router, w_gate, w_up, w_down):
    onward, backward = ring_steps()
    traded = [[(i, i ^ j) for i in range(16)] for j in range(4)]
    count, half = low.shape
    width = 2 * half
    bf16 = jnp.bfloat16

    def send(value, steps):
        return lax.ppermute(value, "ep", steps)

    def pick(*sources):
        n = len(sources)
        columns = sum(part.shape[1] for part in sources[0][1:])
        return fused(
            functools.partial(pick_kernel, capacity, [len(source) - 1 for source in sources]),
            [((n * capacity, columns), bf16)] * 4,
            *[part for source in sources for part in source],
            flops=n * 2 * 4 * capacity * count * columns,
            bytes_accessed=n * 4 * columns * (count + 4 * capacity),
        )

    def trade(blocks):
        across = [send(blocks[j], traded[j]) for j in (2, 3)]
        return [blocks[0], send(blocks[1], traded[1])] + across

    own_slots, before_slots, after_slots, far_slots = targets
    before_low, after_high = send(low, onward), send(high, backward)
    before_high, after_low = send(high, onward), send(low, backward)
    own_rows = trade(pick((own_slots, low, high)))
    far_low, far_high = send(before_low, onward), send(after_high, backward)
    first_rows = trade(pick((before_slots, before_low), (after_slots, after_high)))
    before_high, after_low, own_rows, first_rows[0] = lax.optimization_barrier(
        (before_high, after_low, own_rows, first_rows[0])
    )
    second_rows = trade(pick((before_slots, before_high), (after_slots, after_low)))
    far_rows = trade(pick((far_slots, far_low, far_high)))
    expert_weights = (jnp.swapaxes(w_gate[0], 0, 1), jnp.swapaxes(w_up[0], 0, 1), w_down[0])
    hidden_width = w_gate.shape[2]
    unit = width * hidden_width
    far_rows[0], far_low, far_high = lax.optimization_barrier((far_rows[0], far_low, far_high))
    slots = (count, 4 * capacity)
    weights = fused(
        functools.partial(gate_kernel, capacity),
        [(slots, jnp.float32)] * 4,
        router.T,
        *(own_slots, low, high),
        *(before_slots, before_low, before_high),
        *(after_slots, after_low, after_high),
        *(far_slots, far_low, far_high),
        flops=8 * count * width * 16,
        bytes_accessed=16 * count * width,
    )
    own_rows, weights = lax.optimization_barrier((own_rows, weights))
    blocks = first_rows + second_rows + own_rows
    near = fused(
        functools.partial(near_expert_kernel, capacity),
        [(b.shape, bf16) for b in blocks],
        *blocks,
        *expert_weights,
        vmem=16,
        flops=6 * 12 * capacity * unit,
        bytes_accessed=6 * unit + 4 * 12 * capacity * width,
    )
    near, far_rows = lax.optimization_barrier((near, far_rows))
    result = fused(
        far_expert_kernel,
        [(b.shape, bf16) for b in far_rows],
        *far_rows,
        *expert_weights,
        vmem=16,
        flops=6 * 4 * capacity * unit,
        bytes_accessed=6 * unit + 4 * 4 * capacity * width,
    )
    spent = 2 * 4 * 4 * capacity * count * width
    moved = 4 * width * (count + 4 * capacity)
    piece = ((count, half), bf16)
    far_low, far_high = fused(
        far_kernel,
        [piece] * 2,
        weights[3],
        *trade(result),
        flops=spent,
        bytes_accessed=moved,
    )
    add_low, add_high = send(far_low, onward), send(far_high, backward)

    def near_sums(rows, *adds):
        return fused(
            functools.partial(near_kernel, capacity),
            [piece] * 2,
            weights[1],
            weights[2],
            *trade(rows),
            *adds,
            flops=spent,
            bytes_accessed=moved,
        )

    before_sum, after_sum = near_sums(near[0:4])
    from_after_low = send(before_sum, backward)
    from_before_high = send(after_sum, onward)
    before_sum, after_sum = near_sums(near[4:8], add_high, add_low)
    from_after_high = send(before_sum, backward)
    from_before_low = send(after_sum, onward)
    return fused(
        last_kernel,
        [((count, width), bf16)],
        hidden,
        weights[0],
        *trade(near[8:12]),
        from_before_low,
        from_before_high,
        from_after_low,
        from_after_high,
        flops=spent,
        bytes_accessed=2 * moved,
    )[0]


def ring_steps():
    order = (0, 1, 3, 2)
    onward = [
        (order[i] * 4 + j, order[(i + 1) % 4] * 4 + j) for i in range(4) for j in range(4)
    ]
    return onward, [(b, a) for a, b in onward]


def per_device(
    x_resid,
    q_latent,
    q_rope,
    cache_latent,
    cache_rope,
    new_latent,
    new_rope,
    w_uv,
    w_out,
    norm_gain,
    router,
    expert_ids,
    w_gate,
    w_up,
    w_down,
):
    mixed_latent = attend_local(
        q_latent[0], q_rope[0], cache_latent[0], cache_rope[0], new_latent[0], new_rope[0]
    )
    new_count = mixed_latent.shape[0]
    expert_count = lax.axis_size("ep")
    capacity = new_count * expert_ids.shape[2] // expert_count
    if lax.axis_size("fsdp") != 2 or expert_count != 16:
        projected = project_gathered(mixed_latent, w_uv, w_out)
        hidden = x_resid[0].astype(jnp.float32) + projected
        normed = hidden * lax.rsqrt(jnp.mean(hidden * hidden, axis=-1, keepdims=True) + epsilon)
        normed = (normed * norm_gain).astype(jnp.bfloat16)
        target = slots_of(expert_ids[0], expert_count, capacity)
        routed_sum = routed_exchanged(
            normed, target, capacity, router, w_gate[0], w_up[0], w_down[0]
        )
        layer_out = (hidden + routed_sum).astype(jnp.bfloat16)
        return (hidden.astype(jnp.bfloat16)[None], layer_out[None])
    onward, backward = ring_steps()
    ids = [expert_ids[0].T]
    across = [(i, i ^ 12) for i in range(16)]
    ids += [lax.ppermute(ids[0], "ep", steps) for steps in (onward, backward)]
    ids.append(lax.ppermute(ids[0], "ep", across))
    targets = fused(
        functools.partial(slot_kernel, expert_count, capacity),
        [(part.shape, jnp.int32) for part in ids],
        *ids,
    )
    part, back = project_paired(mixed_latent, w_uv, w_out)
    back, targets = lax.optimization_barrier((back, targets))
    width = part.shape[1]
    halves = (new_count, width // 2)
    hidden, attended, low, high = fused(
        norm_kernel,
        [
            ((new_count, width), jnp.float32),
            ((1, new_count, width), jnp.bfloat16),
            (halves, jnp.bfloat16),
            (halves, jnp.bfloat16),
        ],
        x_resid,
        part,
        back,
        norm_gain[None],
        flops=8 * new_count * width,
        bytes_accessed=20 * new_count * width,
    )
    layer_out = routed_ringed(
        hidden, low, high, targets, capacity, router, w_gate, w_up, w_down
    )
    return (attended, layer_out[None])


def solution(mesh):
    placed = (
        P(("fsdp", "ep"), None, None),
        P(("fsdp", "ep"), None, None, None),
        P(("fsdp", "ep"), None, None, None),
        P(("fsdp", "ep"), None, None),
        P(("fsdp", "ep"), None, None),
        P(("fsdp", "ep"), None, None),
        P(("fsdp", "ep"), None, None),
        P("fsdp", None, None),
        P("fsdp", None),
        P(),
        P(),
        P(("fsdp", "ep"), None, None),
        P("ep", None, None),
        P("ep", None, None),
        P("ep", None, None),
    )

    return jax.shard_map(
        per_device,
        mesh=mesh,
        in_specs=placed,
        out_specs=(P(("fsdp", "ep"), None, None), P(("fsdp", "ep"), None, None)),
        check_vma=False,
    )
```

```python
import functools

import jax
import jax.numpy as jnp
from jax import lax
from jax.experimental import pallas as pl
from jax.experimental.pallas import tpu as pltpu
from jax.sharding import PartitionSpec as P


softmax_scale = 0.07216878364870323
epsilon = 1e-06


def attend_local(q_latent, q_rope, cache_latent, cache_rope, new_latent, new_rope):
    new_count, head_count, latent_width = q_latent.shape
    cache_count = cache_latent.shape[0]
    keys_latent = jnp.concatenate([cache_latent, new_latent], 0)
    keys_rope = jnp.concatenate([cache_rope, new_rope], 0)
    query_rows = q_latent.reshape(new_count * head_count, latent_width)
    rope_rows = q_rope.reshape(new_count * head_count, q_rope.shape[2])
    scores = jnp.dot(query_rows, keys_latent.T, preferred_element_type=jnp.float32)
    scores = (
        scores + jnp.dot(rope_rows, keys_rope.T, preferred_element_type=jnp.float32)
    ) * softmax_scale
    token_of_row = jnp.arange(new_count * head_count, dtype=jnp.int32) // head_count
    key_index = jnp.arange(keys_latent.shape[0], dtype=jnp.int32)
    visible = key_index[None, :] <= token_of_row[:, None] + cache_count
    row_top = jnp.max(jnp.where(visible, scores, -jnp.inf), axis=1, keepdims=True)
    exponent = jnp.where(visible, jnp.exp(scores - row_top), 0.0)
    weights_att = (exponent / jnp.sum(exponent, axis=1, keepdims=True)).astype(jnp.bfloat16)
    mixed_latent = jnp.dot(weights_att, keys_latent, preferred_element_type=jnp.float32).astype(
        jnp.bfloat16
    )
    return mixed_latent.reshape(new_count, head_count, latent_width)


def up_project(mixed_latent, w_uv):
    heads_out = jnp.einsum(
        "thl,lhv->thv", mixed_latent, w_uv, preferred_element_type=jnp.float32
    )
    return heads_out.astype(jnp.bfloat16).reshape(mixed_latent.shape[0], -1)


def project_gathered(mixed_latent, w_uv, w_out):
    heads_flat = up_project(mixed_latent, lax.all_gather(w_uv, "fsdp", axis=0, tiled=True))
    column_width = w_out.shape[1] // lax.axis_size("ep")
    own_columns = lax.dynamic_slice_in_dim(
        w_out, lax.axis_index("ep") * column_width, column_width, 1
    )
    column_block = lax.all_gather(own_columns, "fsdp", axis=0, tiled=True)
    return jnp.dot(
        heads_flat,
        lax.all_gather(column_block, "ep", axis=1, tiled=True),
        preferred_element_type=jnp.float32,
    )


def project_paired(mixed_latent, w_uv, w_out):
    pair = [(0, 1), (1, 0)]
    ep = lax.axis_size("ep")
    twins = [(i, i ^ 1) for i in range(ep)]
    side = lax.axis_index("fsdp")
    lane = lax.axis_index("ep") % 2
    rows, depth = w_uv.shape[0] // 2, w_uv.shape[2]
    heads = w_out.shape[0] // depth

    def own_heads(array, which):
        return lax.dynamic_slice_in_dim(array, which * heads, heads, 1)

    mine = lax.ppermute(
        lax.dynamic_slice(
            w_uv, (lane * rows, (1 - side) * heads, 0), (rows, heads, depth)
        ),
        "fsdp",
        pair,
    )
    by_head = jnp.swapaxes(mixed_latent, 0, 1)
    give = lax.dynamic_slice_in_dim(by_head, (1 - side) * heads, heads, 0)
    kept = lax.dynamic_slice_in_dim(by_head, side * heads, heads, 0)
    other = lax.ppermute(give, "fsdp", pair)
    theirs = lax.ppermute(mine, "ep", twins)
    far = jnp.where(
        lane == 0, jnp.concatenate([mine, theirs], 0), jnp.concatenate([theirs, mine], 0)
    )
    near = own_heads(w_uv, side)
    full = jnp.where(side == 0, jnp.concatenate([near, far], 0), jnp.concatenate([far, near], 0))
    full = jnp.swapaxes(full, 0, 1)
    count, width = mixed_latent.shape[0], w_out.shape[1]

    def project(mixed, dtype):
        return fused(
            project_kernel,
            [((count, width), dtype)],
            mixed,
            full,
            w_out,
            flops=2 * count * w_out.shape[0] * (width + full.shape[1]),
            bytes_accessed=2 * w_out.shape[0] * (width + full.shape[1]),
        )[0]

    partial = project(other, jnp.bfloat16)
    back = lax.ppermute(partial, "fsdp", pair)
    return project(kept, jnp.float32), back


def project_kernel(mixed_ref, values_ref, out_w_ref, result_ref):
    parts = [
        jnp.dot(mixed_ref[h], values_ref[h], preferred_element_type=jnp.float32)
        for h in range(values_ref.shape[0])
    ]
    flat = jnp.concatenate(parts, 1).astype(jnp.bfloat16)
    total = jnp.dot(flat, out_w_ref[...], preferred_element_type=jnp.float32)
    result_ref[...] = total.astype(result_ref.dtype)


def experts(rows, w_gate, w_up, w_down):
    gate_proj = jnp.dot(rows, w_gate, preferred_element_type=jnp.float32)
    up_proj = jnp.dot(rows, w_up, preferred_element_type=jnp.float32)
    activated = (jax.nn.silu(gate_proj) * up_proj).astype(jnp.bfloat16)
    return jnp.dot(activated, w_down, preferred_element_type=jnp.float32).astype(jnp.bfloat16)


def slots_of(own_ids, expert_count, capacity):
    choose = (own_ids[..., None] == jnp.arange(expert_count, dtype=jnp.int32)).astype(jnp.float32)
    assigned = choose.reshape(-1, expert_count)
    earlier = jnp.cumsum(assigned, axis=0) - assigned
    slot_index = jnp.sum(earlier * assigned, axis=-1).reshape(own_ids.shape).astype(jnp.int32)
    return own_ids * capacity + slot_index


def gates_of(normed, router, ids):
    logits = jnp.dot(normed, router, preferred_element_type=jnp.float32)
    choose = ids[..., None] == jnp.arange(router.shape[1], dtype=jnp.int32)
    picked = jnp.sum(jnp.where(choose, logits[:, None, :], 0.0), axis=-1)
    return jax.nn.softmax(picked, axis=-1)


def weighted_rows(weights, rows):
    high = weights.astype(jnp.bfloat16)
    low = (weights - high.astype(jnp.float32)).astype(jnp.bfloat16)
    return jnp.dot(
        jnp.concatenate([high, low], 1),
        jnp.concatenate([rows, rows], 0),
        preferred_element_type=jnp.float32,
    )


def routed_exchanged(normed, target, capacity, router, w_gate, w_up, w_down):
    expert_count = lax.axis_size("ep")
    gate_weights = gates_of(normed, router, target // capacity)
    here = target[..., None] == jnp.arange(expert_count * capacity, dtype=jnp.int32)
    placed = jnp.sum(here.astype(jnp.bfloat16), axis=1)
    combine = jnp.sum(jnp.where(here, gate_weights[..., None], 0.0), axis=1)
    buffers = jnp.einsum("tp,td->pd", placed, normed, preferred_element_type=jnp.float32).astype(
        jnp.bfloat16
    )
    buffers = buffers.reshape(expert_count, capacity, -1)
    received = lax.all_to_all(buffers, "ep", split_axis=0, concat_axis=0, tiled=True)
    result = experts(received.reshape(expert_count * capacity, -1), w_gate, w_up, w_down)
    result = result.reshape(expert_count, capacity, -1)
    returned = lax.all_to_all(result, "ep", split_axis=0, concat_axis=0, tiled=True)
    return weighted_rows(combine, returned.reshape(expert_count * capacity, -1))


def fused(body, outs, *args, vmem=8, flops=0, bytes_accessed=0):
    whole = pl.BlockSpec(memory_space=pltpu.VMEM)
    return pl.pallas_call(
        body,
        out_shape=[jax.ShapeDtypeStruct(shape, dtype) for shape, dtype in outs],
        in_specs=[whole] * len(args),
        out_specs=[whole] * len(outs),
        cost_estimate=pl.CostEstimate(
            flops=flops, bytes_accessed=bytes_accessed, transcendentals=0
        ),
        compiler_params=pltpu.CompilerParams(vmem_limit_bytes=vmem << 20),
    )(*args)


def slot_kernel(expert_count, capacity, *refs):
    sources = len(refs) // 2
    for ids_ref, target_ref in zip(refs[:sources], refs[sources:]):
        ids = ids_ref[...]
        top, count = ids.shape
        level = lax.broadcasted_iota(jnp.int32, (expert_count, count), 0)
        chosen = jnp.zeros((expert_count, count), jnp.float32)
        for k in range(top):
            chosen += (ids[k : k + 1] == level).astype(jnp.float32)
        rows = lax.broadcasted_iota(jnp.int32, (count, count), 0)
        columns = lax.broadcasted_iota(jnp.int32, (count, count), 1)
        ahead = (rows < columns).astype(jnp.float32).astype(jnp.bfloat16)
        earlier = jnp.dot(
            chosen.astype(jnp.bfloat16), ahead, preferred_element_type=jnp.float32
        )
        for k in range(top):
            own = ids[k : k + 1]
            slot = jnp.sum(jnp.where(own == level, earlier, 0.0), axis=0, keepdims=True)
            target_ref[k : k + 1] = own * capacity + slot.astype(jnp.int32)


def matches(target, capacity, place):
    top, count = target.shape
    row = lax.broadcasted_iota(jnp.int32, (4 * capacity, count), 0)
    slot = jnp.zeros_like(row)
    for j in range(4):
        inside = (row >= j * capacity) & (row < (j + 1) * capacity)
        slot = jnp.where(inside, (place ^ j) * capacity + row - j * capacity, slot)
    found = jnp.zeros(row.shape, jnp.float32)
    for k in range(top):
        found += (target[k : k + 1] == slot).astype(jnp.float32)
    return found


def pick_kernel(capacity, sources, *refs):
    place = lax.axis_index("ep")
    position = 0
    out = refs[-4:]
    for n, pieces in enumerate(sources):
        found = matches(refs[position][...], capacity, place).astype(jnp.bfloat16)
        offset = 0
        for ref in refs[position + 1 : position + 1 + pieces]:
            rows = jnp.dot(found, ref[...], preferred_element_type=jnp.float32)
            rows = rows.astype(jnp.bfloat16)
            columns = slice(offset, offset + ref.shape[1])
            offset += ref.shape[1]
            for j in range(4):
                out[j][n * capacity : (n + 1) * capacity, columns] = rows[
                    j * capacity : (j + 1) * capacity
                ]
        position += 1 + pieces


def dot_rows(a, b):
    return lax.dot_general(a, b, (((1,), (1,)), ((), ())), preferred_element_type=jnp.float32)


def gate_kernel(capacity, router_ref, *refs):
    place = lax.axis_index("ep")
    expert_count = router_ref.shape[0]
    out = refs[12:]
    half = refs[1].shape[1]
    for n in range(4):
        target_ref, low_ref, high_ref = refs[3 * n : 3 * n + 3]
        target = target_ref[...]
        top, count = target.shape
        logits = dot_rows(router_ref[:, :half], low_ref[...])
        logits += dot_rows(router_ref[:, half:], high_ref[...])
        level = lax.broadcasted_iota(jnp.int32, (expert_count, count), 0)
        first = level * capacity
        chosen = jnp.zeros((expert_count, count), jnp.float32)
        for k in range(top):
            own = target[k : k + 1]
            chosen += ((own >= first) & (own < first + capacity)).astype(jnp.float32)
        inside = chosen > 0
        peak = jnp.max(jnp.where(inside, logits, -jnp.inf), axis=0, keepdims=True)
        power = jnp.where(inside, jnp.exp(logits - peak), 0.0)
        gate = power / jnp.sum(power, axis=0, keepdims=True)
        found = matches(target, capacity, place)
        row = lax.broadcasted_iota(jnp.int32, found.shape, 0)
        for j in range(4):
            own = jnp.sum(jnp.where(level == (place ^ j), gate, 0.0), axis=0, keepdims=True)
            within = (row >= j * capacity) & (row < (j + 1) * capacity)
            found = jnp.where(within, found * own, found)
        out[n][...] = found.T


def norm_kernel(x_ref, part_ref, back_ref, gain_ref, hidden_ref, attended_ref, low_ref, high_ref):
    width = hidden_ref.shape[1]
    hidden = x_ref[0].astype(jnp.float32) + (
        part_ref[...] + back_ref[...].astype(jnp.float32)
    )
    hidden_ref[...] = hidden
    attended_ref[0] = hidden.astype(jnp.bfloat16)
    square = jnp.mean(hidden * hidden, axis=-1, keepdims=True)
    normed = hidden * lax.rsqrt(square + epsilon) * gain_ref[...]
    low_ref[...] = normed[:, : width // 2].astype(jnp.bfloat16)
    high_ref[...] = normed[:, width // 2 :].astype(jnp.bfloat16)


def hidden_units(rows, gate_ref, up_ref):
    active = []
    for start in range(0, gate_ref.shape[0], 256):
        part = slice(start, min(start + 256, gate_ref.shape[0]))
        gate = dot_rows(rows, gate_ref[part])
        up = dot_rows(rows, up_ref[part])
        active.append((gate / (1.0 + jnp.exp(-gate)) * up).astype(jnp.bfloat16))
    return jnp.concatenate(active, 1)


def near_expert_kernel(capacity, *refs):
    first, second, own = refs[0:4], refs[4:8], refs[8:12]
    gate_ref, up_ref, down_ref = refs[12:15]
    out_first, out_second, out_own = refs[15:19], refs[19:23], refs[23:27]
    rows = [
        jnp.concatenate([a[:capacity], b[:capacity]], 1) for a, b in zip(first, second)
    ]
    rows += [
        jnp.concatenate([b[capacity:], a[capacity:]], 1) for a, b in zip(first, second)
    ]
    rows += [ref[...] for ref in own]
    active = hidden_units(jnp.concatenate(rows, 0), gate_ref, up_ref)
    width = down_ref.shape[1]
    step = width // 4
    for start in range(0, width, step):
        result = jnp.dot(
            active, down_ref[:, start : start + step], preferred_element_type=jnp.float32
        ).astype(jnp.bfloat16)
        low = start < width // 2
        columns = slice(start % (width // 2), start % (width // 2) + step)
        for j in range(4):
            blocks = [
                result[(4 * n + j) * capacity : (4 * n + j + 1) * capacity] for n in range(3)
            ]
            before_out, after_out = (out_first, out_second) if low else (out_second, out_first)
            before_out[j][:capacity, columns] = blocks[0]
            after_out[j][capacity:, columns] = blocks[1]
            out_own[j][:, start : start + step] = blocks[2]


def far_expert_kernel(*refs):
    gate_ref, up_ref, down_ref = refs[4:7]
    rows = jnp.concatenate([ref[...] for ref in refs[:4]], 0)
    active = hidden_units(rows, gate_ref, up_ref)
    capacity = refs[0].shape[0]
    for start in range(0, down_ref.shape[1], 512):
        part = slice(start, start + 512)
        result = jnp.dot(active, down_ref[:, part], preferred_element_type=jnp.float32)
        result = result.astype(jnp.bfloat16)
        for j in range(4):
            refs[7 + j][:, part] = result[j * capacity : (j + 1) * capacity]


def weigh(weights, rows):
    high = weights.astype(jnp.bfloat16)
    low = (weights - high.astype(jnp.float32)).astype(jnp.bfloat16)
    return jnp.dot(high, rows, preferred_element_type=jnp.float32) + jnp.dot(
        low, rows, preferred_element_type=jnp.float32
    )


def far_kernel(weights_ref, r0, r1, r2, r3, low_ref, high_ref):
    rows = jnp.concatenate([r[...] for r in (r0, r1, r2, r3)], 0)
    total = weigh(weights_ref[...], rows)
    half = low_ref.shape[1]
    low_ref[...] = total[:, :half].astype(jnp.bfloat16)
    high_ref[...] = total[:, half:].astype(jnp.bfloat16)


def near_kernel(capacity, before_w, after_w, r0, r1, r2, r3, *refs):
    blocks = (r0, r1, r2, r3)
    adds = refs[:-2]
    for n, weights in enumerate((before_w, after_w)):
        rows = jnp.concatenate([r[n * capacity : (n + 1) * capacity] for r in blocks], 0)
        total = weigh(weights[...], rows)
        if adds:
            total += adds[n][...].astype(jnp.float32)
        refs[len(adds) + n][...] = total.astype(jnp.bfloat16)


def last_kernel(hidden_ref, weights_ref, r0, r1, r2, r3, x_low, x_high, y_low, y_high, out_ref):
    rows = jnp.concatenate([r[...] for r in (r0, r1, r2, r3)], 0)
    total = hidden_ref[...] + weigh(weights_ref[...], rows)
    half = x_low.shape[1]
    low = x_low[...].astype(jnp.float32) + y_low[...].astype(jnp.float32)
    high = x_high[...].astype(jnp.float32) + y_high[...].astype(jnp.float32)
    out_ref[:, :half] = (total[:, :half] + low).astype(jnp.bfloat16)
    out_ref[:, half:] = (total[:, half:] + high).astype(jnp.bfloat16)


def routed_ringed(hidden, low, high, targets, capacity, router, w_gate, w_up, w_down):
    onward, backward = ring_steps()
    traded = [[(i, i ^ j) for i in range(16)] for j in range(4)]
    count, half = low.shape
    width = 2 * half
    bf16 = jnp.bfloat16

    def send(value, steps):
        return lax.ppermute(value, "ep", steps)

    def pick(*sources):
        n = len(sources)
        columns = sum(part.shape[1] for part in sources[0][1:])
        return fused(
            functools.partial(pick_kernel, capacity, [len(source) - 1 for source in sources]),
            [((n * capacity, columns), bf16)] * 4,
            *[part for source in sources for part in source],
            flops=n * 2 * 4 * capacity * count * columns,
            bytes_accessed=n * 4 * columns * (count + 4 * capacity),
        )

    def trade(blocks):
        across = [send(blocks[j], traded[j]) for j in (2, 3)]
        return [blocks[0], send(blocks[1], traded[1])] + across

    own_slots, before_slots, after_slots, far_slots = targets
    before_low, after_high = send(low, onward), send(high, backward)
    before_high, after_low = send(high, onward), send(low, backward)
    own_rows = trade(pick((own_slots, low, high)))
    far_low, far_high = send(before_low, onward), send(after_high, backward)
    first_rows = trade(pick((before_slots, before_low), (after_slots, after_high)))
    before_high, after_low, own_rows, first_rows[0] = lax.optimization_barrier(
        (before_high, after_low, own_rows, first_rows[0])
    )
    second_rows = trade(pick((before_slots, before_high), (after_slots, after_low)))
    far_rows = trade(pick((far_slots, far_low, far_high)))
    expert_weights = (jnp.swapaxes(w_gate[0], 0, 1), jnp.swapaxes(w_up[0], 0, 1), w_down[0])
    hidden_width = w_gate.shape[2]
    unit = width * hidden_width
    far_rows[0], far_low, far_high = lax.optimization_barrier((far_rows[0], far_low, far_high))
    slots = (count, 4 * capacity)
    weights = fused(
        functools.partial(gate_kernel, capacity),
        [(slots, jnp.float32)] * 4,
        router.T,
        *(own_slots, low, high),
        *(before_slots, before_low, before_high),
        *(after_slots, after_low, after_high),
        *(far_slots, far_low, far_high),
        flops=8 * count * width * 16,
        bytes_accessed=16 * count * width,
    )
    own_rows, weights = lax.optimization_barrier((own_rows, weights))
    blocks = first_rows + second_rows + own_rows
    near = fused(
        functools.partial(near_expert_kernel, capacity),
        [(b.shape, bf16) for b in blocks],
        *blocks,
        *expert_weights,
        vmem=16,
        flops=6 * 12 * capacity * unit,
        bytes_accessed=6 * unit + 4 * 12 * capacity * width,
    )
    near, far_rows = lax.optimization_barrier((near, far_rows))
    result = fused(
        far_expert_kernel,
        [(b.shape, bf16) for b in far_rows],
        *far_rows,
        *expert_weights,
        vmem=16,
        flops=6 * 4 * capacity * unit,
        bytes_accessed=6 * unit + 4 * 4 * capacity * width,
    )
    spent = 2 * 4 * 4 * capacity * count * width
    moved = 4 * width * (count + 4 * capacity)
    piece = ((count, half), bf16)
    far_low, far_high = fused(
        far_kernel,
        [piece] * 2,
        weights[3],
        *trade(result),
        flops=spent,
        bytes_accessed=moved,
    )
    add_low, add_high = send(far_low, onward), send(far_high, backward)

    def near_sums(rows, *adds):
        return fused(
            functools.partial(near_kernel, capacity),
            [piece] * 2,
            weights[1],
            weights[2],
            *trade(rows),
            *adds,
            flops=spent,
            bytes_accessed=moved,
        )

    before_sum, after_sum = near_sums(near[0:4])
    from_after_low = send(before_sum, backward)
    from_before_high = send(after_sum, onward)
    before_sum, after_sum = near_sums(near[4:8], add_high, add_low)
    from_after_high = send(before_sum, backward)
    from_before_low = send(after_sum, onward)
    return fused(
        last_kernel,
        [((count, width), bf16)],
        hidden,
        weights[0],
        *trade(near[8:12]),
        from_before_low,
        from_before_high,
        from_after_low,
        from_after_high,
        flops=spent,
        bytes_accessed=2 * moved,
    )[0]


def ring_steps():
    order = (0, 1, 3, 2)
    onward = [
        (order[i] * 4 + j, order[(i + 1) % 4] * 4 + j) for i in range(4) for j in range(4)
    ]
    return onward, [(b, a) for a, b in onward]


def per_device(
    x_resid,
    q_latent,
    q_rope,
    cache_latent,
    cache_rope,
    new_latent,
    new_rope,
    w_uv,
    w_out,
    norm_gain,
    router,
    expert_ids,
    w_gate,
    w_up,
    w_down,
):
    mixed_latent = attend_local(
        q_latent[0], q_rope[0], cache_latent[0], cache_rope[0], new_latent[0], new_rope[0]
    )
    new_count = mixed_latent.shape[0]
    expert_count = lax.axis_size("ep")
    capacity = new_count * expert_ids.shape[2] // expert_count
    if lax.axis_size("fsdp") != 2 or expert_count != 16:
        projected = project_gathered(mixed_latent, w_uv, w_out)
        hidden = x_resid[0].astype(jnp.float32) + projected
        normed = hidden * lax.rsqrt(jnp.mean(hidden * hidden, axis=-1, keepdims=True) + epsilon)
        normed = (normed * norm_gain).astype(jnp.bfloat16)
        target = slots_of(expert_ids[0], expert_count, capacity)
        routed_sum = routed_exchanged(
            normed, target, capacity, router, w_gate[0], w_up[0], w_down[0]
        )
        layer_out = (hidden + routed_sum).astype(jnp.bfloat16)
        return (hidden.astype(jnp.bfloat16)[None], layer_out[None])
    onward, backward = ring_steps()
    ids = [expert_ids[0].T]
    across = [(i, i ^ 12) for i in range(16)]
    ids += [lax.ppermute(ids[0], "ep", steps) for steps in (onward, backward)]
    ids.append(lax.ppermute(ids[0], "ep", across))
    targets = fused(
        functools.partial(slot_kernel, expert_count, capacity),
        [(part.shape, jnp.int32) for part in ids],
        *ids,
    )
    part, back = project_paired(mixed_latent, w_uv, w_out)
    back, targets = lax.optimization_barrier((back, targets))
    width = part.shape[1]
    halves = (new_count, width // 2)
    hidden, attended, low, high = fused(
        norm_kernel,
        [
            ((new_count, width), jnp.float32),
            ((1, new_count, width), jnp.bfloat16),
            (halves, jnp.bfloat16),
            (halves, jnp.bfloat16),
        ],
        x_resid,
        part,
        back,
        norm_gain[None],
        flops=8 * new_count * width,
        bytes_accessed=20 * new_count * width,
    )
    layer_out = routed_ringed(
        hidden, low, high, targets, capacity, router, w_gate, w_up, w_down
    )
    return (attended, layer_out[None])


def solution(mesh):
    placed = (
        P(("fsdp", "ep"), None, None),
        P(("fsdp", "ep"), None, None, None),
        P(("fsdp", "ep"), None, None, None),
        P(("fsdp", "ep"), None, None),
        P(("fsdp", "ep"), None, None),
        P(("fsdp", "ep"), None, None),
        P(("fsdp", "ep"), None, None),
        P("fsdp", None, None),
        P("fsdp", None),
        P(),
        P(),
        P(("fsdp", "ep"), None, None),
        P("ep", None, None),
        P("ep", None, None),
        P("ep", None, None),
    )

    return jax.shard_map(
        per_device,
        mesh=mesh,
        in_specs=placed,
        out_specs=(P(("fsdp", "ep"), None, None), P(("fsdp", "ep"), None, None)),
        check_vma=False,
    )
```

```python
import functools

import jax
import jax.numpy as jnp
from jax import lax
from jax.experimental import pallas as pl
from jax.experimental.pallas import tpu as pltpu
from jax.sharding import PartitionSpec as P


softmax_scale = 0.07216878364870323
epsilon = 1e-06


def attend_local(q_latent, q_rope, cache_latent, cache_rope, new_latent, new_rope):
    new_count, head_count, latent_width = q_latent.shape
    cache_count = cache_latent.shape[0]
    keys_latent = jnp.concatenate([cache_latent, new_latent], 0)
    keys_rope = jnp.concatenate([cache_rope, new_rope], 0)
    query_rows = q_latent.reshape(new_count * head_count, latent_width)
    rope_rows = q_rope.reshape(new_count * head_count, q_rope.shape[2])
    scores = jnp.dot(query_rows, keys_latent.T, preferred_element_type=jnp.float32)
    scores = (
        scores + jnp.dot(rope_rows, keys_rope.T, preferred_element_type=jnp.float32)
    ) * softmax_scale
    token_of_row = jnp.arange(new_count * head_count, dtype=jnp.int32) // head_count
    key_index = jnp.arange(keys_latent.shape[0], dtype=jnp.int32)
    visible = key_index[None, :] <= token_of_row[:, None] + cache_count
    row_top = jnp.max(jnp.where(visible, scores, -jnp.inf), axis=1, keepdims=True)
    exponent = jnp.where(visible, jnp.exp(scores - row_top), 0.0)
    weights_att = (exponent / jnp.sum(exponent, axis=1, keepdims=True)).astype(jnp.bfloat16)
    mixed_latent = jnp.dot(weights_att, keys_latent, preferred_element_type=jnp.float32).astype(
        jnp.bfloat16
    )
    return mixed_latent.reshape(new_count, head_count, latent_width)


def up_project(mixed_latent, w_uv):
    heads_out = jnp.einsum(
        "thl,lhv->thv", mixed_latent, w_uv, preferred_element_type=jnp.float32
    )
    return heads_out.astype(jnp.bfloat16).reshape(mixed_latent.shape[0], -1)


def project_gathered(mixed_latent, w_uv, w_out):
    heads_flat = up_project(mixed_latent, lax.all_gather(w_uv, "fsdp", axis=0, tiled=True))
    column_width = w_out.shape[1] // lax.axis_size("ep")
    own_columns = lax.dynamic_slice_in_dim(
        w_out, lax.axis_index("ep") * column_width, column_width, 1
    )
    column_block = lax.all_gather(own_columns, "fsdp", axis=0, tiled=True)
    return jnp.dot(
        heads_flat,
        lax.all_gather(column_block, "ep", axis=1, tiled=True),
        preferred_element_type=jnp.float32,
    )


def project_paired(give, kept, w_uv, w_out):
    pair = [(0, 1), (1, 0)]
    ep = lax.axis_size("ep")
    twins = [(i, i ^ 1) for i in range(ep)]
    side = lax.axis_index("fsdp")
    lane = lax.axis_index("ep") % 2
    rows, depth = w_uv.shape[0] // 2, w_uv.shape[2]
    heads = w_out.shape[0] // depth

    def own_heads(array, which):
        return lax.dynamic_slice_in_dim(array, which * heads, heads, 1)

    mine = lax.ppermute(
        lax.dynamic_slice(
            w_uv, (lane * rows, (1 - side) * heads, 0), (rows, heads, depth)
        ),
        "fsdp",
        pair,
    )
    other = lax.ppermute(give, "fsdp", pair)
    theirs = lax.ppermute(mine, "ep", twins)
    far = jnp.where(
        lane == 0, jnp.concatenate([mine, theirs], 0), jnp.concatenate([theirs, mine], 0)
    )
    near = own_heads(w_uv, side)
    full = jnp.where(side == 0, jnp.concatenate([near, far], 0), jnp.concatenate([far, near], 0))
    full = jnp.swapaxes(full, 0, 1)
    count, width = kept.shape[1], w_out.shape[1]

    def project(mixed, dtype):
        return fused(
            project_kernel,
            [((count, width), dtype)],
            mixed,
            full,
            w_out,
            flops=2 * count * w_out.shape[0] * (width + full.shape[1]),
            bytes_accessed=2 * w_out.shape[0] * (width + full.shape[1]),
        )[0]

    partial = project(other, jnp.bfloat16)
    back = lax.ppermute(partial, "fsdp", pair)
    return project(kept, jnp.float32), back


def attend_kernel(head_count, *refs):
    sources, (give_ref, kept_ref) = refs[:6], refs[6:8]
    q_ref, rope_ref, keys_ref, ropes_ref, sem = refs[8:]
    cached = sources[2].shape[0]
    targets = (
        q_ref,
        rope_ref,
        keys_ref.at[:cached],
        ropes_ref.at[:cached],
        keys_ref.at[cached:],
        ropes_ref.at[cached:],
    )
    copies = [
        pltpu.make_async_copy(source, target, sem.at[n])
        for n, (source, target) in enumerate(zip(sources, targets))
    ]
    for copy in copies:
        copy.start()
    side = lax.axis_index("fsdp")
    heads, count, _ = kept_ref.shape
    for copy in copies:
        copy.wait()
    keys = keys_ref[...]
    ropes = ropes_ref[...]
    scores = dot_rows(q_ref[...], keys) + dot_rows(rope_ref[...], ropes)
    scores = scores * softmax_scale
    row = lax.broadcasted_iota(jnp.int32, scores.shape, 0)
    key = lax.broadcasted_iota(jnp.int32, scores.shape, 1)
    visible = (key - cached) * head_count <= row
    top = jnp.max(jnp.where(visible, scores, -jnp.inf), axis=1, keepdims=True)
    exponent = jnp.where(visible, jnp.exp(scores - top), 0.0)
    weights = (exponent / jnp.sum(exponent, axis=1, keepdims=True)).astype(jnp.bfloat16)
    mixed = jnp.dot(weights, keys, preferred_element_type=jnp.float32).astype(jnp.bfloat16)
    token = lax.broadcasted_iota(jnp.int32, (count, count * head_count), 0)
    source = lax.broadcasted_iota(jnp.int32, (count, count * head_count), 1)
    for which, out in ((1 - side, give_ref), (side, kept_ref)):
        for h in range(heads):
            found = (source == token * head_count + which * heads + h).astype(jnp.float32)
            rows = jnp.dot(
                found.astype(jnp.bfloat16), mixed, preferred_element_type=jnp.float32
            )
            out[h] = rows.astype(jnp.bfloat16)


def attend_by_head(heads, q_latent, q_rope, cache_latent, cache_rope, new_latent, new_rope):
    count, head_count, width = q_latent.shape
    keys = cache_latent.shape[0] + new_latent.shape[0]
    rows = count * head_count
    rope_width = q_rope.shape[2]
    shapes = ((rows, width), (rows, rope_width), (keys, width), (keys, rope_width))
    return pl.pallas_call(
        functools.partial(attend_kernel, head_count),
        out_shape=[jax.ShapeDtypeStruct((heads, count, width), jnp.bfloat16)] * 2,
        in_specs=[pl.BlockSpec(memory_space=pltpu.HBM)] * 6,
        out_specs=[pl.BlockSpec(memory_space=pltpu.VMEM)] * 2,
        scratch_shapes=[pltpu.VMEM(shape, jnp.bfloat16) for shape in shapes]
        + [pltpu.SemaphoreType.DMA((6,))],
        cost_estimate=pl.CostEstimate(
            flops=2 * rows * width * (2 * keys + rows),
            bytes_accessed=8 * rows * width,
            transcendentals=rows * keys,
        ),
        compiler_params=pltpu.CompilerParams(vmem_limit_bytes=12 << 20),
    )(
        q_latent.reshape(rows, width),
        q_rope.reshape(rows, rope_width),
        cache_latent,
        cache_rope,
        new_latent,
        new_rope,
    )


def project_kernel(mixed_ref, values_ref, out_w_ref, result_ref):
    parts = [
        jnp.dot(mixed_ref[h], values_ref[h], preferred_element_type=jnp.float32)
        for h in range(values_ref.shape[0])
    ]
    flat = jnp.concatenate(parts, 1).astype(jnp.bfloat16)
    total = jnp.dot(flat, out_w_ref[...], preferred_element_type=jnp.float32)
    result_ref[...] = total.astype(result_ref.dtype)


def experts(rows, w_gate, w_up, w_down):
    gate_proj = jnp.dot(rows, w_gate, preferred_element_type=jnp.float32)
    up_proj = jnp.dot(rows, w_up, preferred_element_type=jnp.float32)
    activated = (jax.nn.silu(gate_proj) * up_proj).astype(jnp.bfloat16)
    return jnp.dot(activated, w_down, preferred_element_type=jnp.float32).astype(jnp.bfloat16)


def slots_of(own_ids, expert_count, capacity):
    choose = (own_ids[..., None] == jnp.arange(expert_count, dtype=jnp.int32)).astype(jnp.float32)
    assigned = choose.reshape(-1, expert_count)
    earlier = jnp.cumsum(assigned, axis=0) - assigned
    slot_index = jnp.sum(earlier * assigned, axis=-1).reshape(own_ids.shape).astype(jnp.int32)
    return own_ids * capacity + slot_index


def gates_of(normed, router, ids):
    logits = jnp.dot(normed, router, preferred_element_type=jnp.float32)
    choose = ids[..., None] == jnp.arange(router.shape[1], dtype=jnp.int32)
    picked = jnp.sum(jnp.where(choose, logits[:, None, :], 0.0), axis=-1)
    return jax.nn.softmax(picked, axis=-1)


def weighted_rows(weights, rows):
    high = weights.astype(jnp.bfloat16)
    low = (weights - high.astype(jnp.float32)).astype(jnp.bfloat16)
    return jnp.dot(
        jnp.concatenate([high, low], 1),
        jnp.concatenate([rows, rows], 0),
        preferred_element_type=jnp.float32,
    )


def routed_exchanged(normed, target, capacity, router, w_gate, w_up, w_down):
    expert_count = lax.axis_size("ep")
    gate_weights = gates_of(normed, router, target // capacity)
    here = target[..., None] == jnp.arange(expert_count * capacity, dtype=jnp.int32)
    placed = jnp.sum(here.astype(jnp.bfloat16), axis=1)
    combine = jnp.sum(jnp.where(here, gate_weights[..., None], 0.0), axis=1)
    buffers = jnp.einsum("tp,td->pd", placed, normed, preferred_element_type=jnp.float32).astype(
        jnp.bfloat16
    )
    buffers = buffers.reshape(expert_count, capacity, -1)
    received = lax.all_to_all(buffers, "ep", split_axis=0, concat_axis=0, tiled=True)
    result = experts(received.reshape(expert_count * capacity, -1), w_gate, w_up, w_down)
    result = result.reshape(expert_count, capacity, -1)
    returned = lax.all_to_all(result, "ep", split_axis=0, concat_axis=0, tiled=True)
    return weighted_rows(combine, returned.reshape(expert_count * capacity, -1))


def fused(body, outs, *args, vmem=8, flops=0, bytes_accessed=0):
    whole = pl.BlockSpec(memory_space=pltpu.VMEM)
    return pl.pallas_call(
        body,
        out_shape=[jax.ShapeDtypeStruct(shape, dtype) for shape, dtype in outs],
        in_specs=[whole] * len(args),
        out_specs=[whole] * len(outs),
        cost_estimate=pl.CostEstimate(
            flops=flops, bytes_accessed=bytes_accessed, transcendentals=0
        ),
        compiler_params=pltpu.CompilerParams(vmem_limit_bytes=vmem << 20),
    )(*args)


def slot_kernel(expert_count, capacity, *refs):
    sources = len(refs) // 2
    for ids_ref, target_ref in zip(refs[:sources], refs[sources:]):
        ids = ids_ref[...]
        top, count = ids.shape
        level = lax.broadcasted_iota(jnp.int32, (expert_count, count), 0)
        chosen = jnp.zeros((expert_count, count), jnp.float32)
        for k in range(top):
            chosen += (ids[k : k + 1] == level).astype(jnp.float32)
        rows = lax.broadcasted_iota(jnp.int32, (count, count), 0)
        columns = lax.broadcasted_iota(jnp.int32, (count, count), 1)
        ahead = (rows < columns).astype(jnp.float32).astype(jnp.bfloat16)
        earlier = jnp.dot(
            chosen.astype(jnp.bfloat16), ahead, preferred_element_type=jnp.float32
        )
        for k in range(top):
            own = ids[k : k + 1]
            slot = jnp.sum(jnp.where(own == level, earlier, 0.0), axis=0, keepdims=True)
            target_ref[k : k + 1] = own * capacity + slot.astype(jnp.int32)


def matches(target, capacity, place):
    top, count = target.shape
    row = lax.broadcasted_iota(jnp.int32, (4 * capacity, count), 0)
    slot = jnp.zeros_like(row)
    for j in range(4):
        inside = (row >= j * capacity) & (row < (j + 1) * capacity)
        slot = jnp.where(inside, (place ^ j) * capacity + row - j * capacity, slot)
    found = jnp.zeros(row.shape, jnp.float32)
    for k in range(top):
        found += (target[k : k + 1] == slot).astype(jnp.float32)
    return found


def pick_kernel(capacity, sources, *refs):
    place = lax.axis_index("ep")
    position = 0
    out = refs[-4:]
    for n, pieces in enumerate(sources):
        found = matches(refs[position][...], capacity, place).astype(jnp.bfloat16)
        offset = 0
        for ref in refs[position + 1 : position + 1 + pieces]:
            rows = jnp.dot(found, ref[...], preferred_element_type=jnp.float32)
            rows = rows.astype(jnp.bfloat16)
            columns = slice(offset, offset + ref.shape[1])
            offset += ref.shape[1]
            for j in range(4):
                out[j][n * capacity : (n + 1) * capacity, columns] = rows[
                    j * capacity : (j + 1) * capacity
                ]
        position += 1 + pieces


def dot_rows(a, b):
    return lax.dot_general(a, b, (((1,), (1,)), ((), ())), preferred_element_type=jnp.float32)


def gate_kernel(capacity, router_ref, *refs):
    place = lax.axis_index("ep")
    expert_count = router_ref.shape[0]
    out = refs[12:]
    half = refs[1].shape[1]
    for n in range(4):
        target_ref, low_ref, high_ref = refs[3 * n : 3 * n + 3]
        target = target_ref[...]
        top, count = target.shape
        logits = dot_rows(router_ref[:, :half], low_ref[...])
        logits += dot_rows(router_ref[:, half:], high_ref[...])
        level = lax.broadcasted_iota(jnp.int32, (expert_count, count), 0)
        first = level * capacity
        chosen = jnp.zeros((expert_count, count), jnp.float32)
        for k in range(top):
            own = target[k : k + 1]
            chosen += ((own >= first) & (own < first + capacity)).astype(jnp.float32)
        inside = chosen > 0
        peak = jnp.max(jnp.where(inside, logits, -jnp.inf), axis=0, keepdims=True)
        power = jnp.where(inside, jnp.exp(logits - peak), 0.0)
        gate = power / jnp.sum(power, axis=0, keepdims=True)
        found = matches(target, capacity, place)
        row = lax.broadcasted_iota(jnp.int32, found.shape, 0)
        for j in range(4):
            own = jnp.sum(jnp.where(level == (place ^ j), gate, 0.0), axis=0, keepdims=True)
            within = (row >= j * capacity) & (row < (j + 1) * capacity)
            found = jnp.where(within, found * own, found)
        out[n][...] = found.T


def norm_kernel(x_ref, part_ref, back_ref, gain_ref, hidden_ref, attended_ref, low_ref, high_ref):
    width = hidden_ref.shape[1]
    hidden = x_ref[0].astype(jnp.float32) + (
        part_ref[...] + back_ref[...].astype(jnp.float32)
    )
    hidden_ref[...] = hidden
    attended_ref[0] = hidden.astype(jnp.bfloat16)
    square = jnp.mean(hidden * hidden, axis=-1, keepdims=True)
    normed = hidden * lax.rsqrt(square + epsilon) * gain_ref[...]
    low_ref[...] = normed[:, : width // 2].astype(jnp.bfloat16)
    high_ref[...] = normed[:, width // 2 :].astype(jnp.bfloat16)


def hidden_units(rows, gate_ref, up_ref):
    active = []
    for start in range(0, gate_ref.shape[0], 256):
        part = slice(start, min(start + 256, gate_ref.shape[0]))
        gate = dot_rows(rows, gate_ref[part])
        up = dot_rows(rows, up_ref[part])
        active.append((gate / (1.0 + jnp.exp(-gate)) * up).astype(jnp.bfloat16))
    return jnp.concatenate(active, 1)


def near_expert_kernel(capacity, *refs):
    first, second, own = refs[0:4], refs[4:8], refs[8:12]
    gate_ref, up_ref, down_ref = refs[12:15]
    out_first, out_second, out_own = refs[15:19], refs[19:23], refs[23:27]
    rows = [
        jnp.concatenate([a[:capacity], b[:capacity]], 1) for a, b in zip(first, second)
    ]
    rows += [
        jnp.concatenate([b[capacity:], a[capacity:]], 1) for a, b in zip(first, second)
    ]
    rows += [ref[...] for ref in own]
    active = hidden_units(jnp.concatenate(rows, 0), gate_ref, up_ref)
    width = down_ref.shape[1]
    step = width // 4
    for start in range(0, width, step):
        result = jnp.dot(
            active, down_ref[:, start : start + step], preferred_element_type=jnp.float32
        ).astype(jnp.bfloat16)
        low = start < width // 2
        columns = slice(start % (width // 2), start % (width // 2) + step)
        for j in range(4):
            blocks = [
                result[(4 * n + j) * capacity : (4 * n + j + 1) * capacity] for n in range(3)
            ]
            before_out, after_out = (out_first, out_second) if low else (out_second, out_first)
            before_out[j][:capacity, columns] = blocks[0]
            after_out[j][capacity:, columns] = blocks[1]
            out_own[j][:, start : start + step] = blocks[2]


def far_expert_kernel(*refs):
    gate_ref, up_ref, down_ref = refs[4:7]
    rows = jnp.concatenate([ref[...] for ref in refs[:4]], 0)
    active = hidden_units(rows, gate_ref, up_ref)
    capacity = refs[0].shape[0]
    for start in range(0, down_ref.shape[1], 512):
        part = slice(start, start + 512)
        result = jnp.dot(active, down_ref[:, part], preferred_element_type=jnp.float32)
        result = result.astype(jnp.bfloat16)
        for j in range(4):
            refs[7 + j][:, part] = result[j * capacity : (j + 1) * capacity]


def weigh(weights, rows):
    high = weights.astype(jnp.bfloat16)
    low = (weights - high.astype(jnp.float32)).astype(jnp.bfloat16)
    return jnp.dot(high, rows, preferred_element_type=jnp.float32) + jnp.dot(
        low, rows, preferred_element_type=jnp.float32
    )


def far_kernel(weights_ref, r0, r1, r2, r3, low_ref, high_ref):
    rows = jnp.concatenate([r[...] for r in (r0, r1, r2, r3)], 0)
    total = weigh(weights_ref[...], rows)
    half = low_ref.shape[1]
    low_ref[...] = total[:, :half].astype(jnp.bfloat16)
    high_ref[...] = total[:, half:].astype(jnp.bfloat16)


def near_kernel(capacity, before_w, after_w, r0, r1, r2, r3, *refs):
    blocks = (r0, r1, r2, r3)
    adds = refs[:-2]
    for n, weights in enumerate((before_w, after_w)):
        rows = jnp.concatenate([r[n * capacity : (n + 1) * capacity] for r in blocks], 0)
        total = weigh(weights[...], rows)
        if adds:
            total += adds[n][...].astype(jnp.float32)
        refs[len(adds) + n][...] = total.astype(jnp.bfloat16)


def last_kernel(hidden_ref, weights_ref, r0, r1, r2, r3, x_low, x_high, y_low, y_high, out_ref):
    rows = jnp.concatenate([r[...] for r in (r0, r1, r2, r3)], 0)
    total = hidden_ref[...] + weigh(weights_ref[...], rows)
    half = x_low.shape[1]
    low = x_low[...].astype(jnp.float32) + y_low[...].astype(jnp.float32)
    high = x_high[...].astype(jnp.float32) + y_high[...].astype(jnp.float32)
    out_ref[:, :half] = (total[:, :half] + low).astype(jnp.bfloat16)
    out_ref[:, half:] = (total[:, half:] + high).astype(jnp.bfloat16)


def routed_ringed(hidden, low, high, targets, capacity, router, w_gate, w_up, w_down):
    onward, backward = ring_steps()
    traded = [[(i, i ^ j) for i in range(16)] for j in range(4)]
    count, half = low.shape
    width = 2 * half
    bf16 = jnp.bfloat16

    def send(value, steps):
        return lax.ppermute(value, "ep", steps)

    def pick(*sources):
        n = len(sources)
        columns = sum(part.shape[1] for part in sources[0][1:])
        return fused(
            functools.partial(pick_kernel, capacity, [len(source) - 1 for source in sources]),
            [((n * capacity, columns), bf16)] * 4,
            *[part for source in sources for part in source],
            flops=n * 2 * 4 * capacity * count * columns,
            bytes_accessed=n * 4 * columns * (count + 4 * capacity),
        )

    def trade(blocks):
        across = [send(blocks[j], traded[j]) for j in (2, 3)]
        return [blocks[0], send(blocks[1], traded[1])] + across

    own_slots, before_slots, after_slots, far_slots = targets
    before_low, after_high = send(low, onward), send(high, backward)
    before_high, after_low = send(high, onward), send(low, backward)
    own_rows = trade(pick((own_slots, low, high)))
    far_low, far_high = send(before_low, onward), send(after_high, backward)
    first_rows = trade(pick((before_slots, before_low), (after_slots, after_high)))
    before_high, after_low, own_rows, first_rows[0] = lax.optimization_barrier(
        (before_high, after_low, own_rows, first_rows[0])
    )
    second_rows = trade(pick((before_slots, before_high), (after_slots, after_low)))
    far_rows = trade(pick((far_slots, far_low, far_high)))
    expert_weights = (jnp.swapaxes(w_gate[0], 0, 1), jnp.swapaxes(w_up[0], 0, 1), w_down[0])
    hidden_width = w_gate.shape[2]
    unit = width * hidden_width
    far_rows[0], far_low, far_high = lax.optimization_barrier((far_rows[0], far_low, far_high))
    slots = (count, 4 * capacity)
    weights = fused(
        functools.partial(gate_kernel, capacity),
        [(slots, jnp.float32)] * 4,
        router.T,
        *(own_slots, low, high),
        *(before_slots, before_low, before_high),
        *(after_slots, after_low, after_high),
        *(far_slots, far_low, far_high),
        flops=8 * count * width * 16,
        bytes_accessed=16 * count * width,
    )
    own_rows, weights = lax.optimization_barrier((own_rows, weights))
    blocks = first_rows + second_rows + own_rows
    near = fused(
        functools.partial(near_expert_kernel, capacity),
        [(b.shape, bf16) for b in blocks],
        *blocks,
        *expert_weights,
        vmem=16,
        flops=6 * 12 * capacity * unit,
        bytes_accessed=6 * unit + 4 * 12 * capacity * width,
    )
    near, far_rows = lax.optimization_barrier((near, far_rows))
    result = fused(
        far_expert_kernel,
        [(b.shape, bf16) for b in far_rows],
        *far_rows,
        *expert_weights,
        vmem=16,
        flops=6 * 4 * capacity * unit,
        bytes_accessed=6 * unit + 4 * 4 * capacity * width,
    )
    spent = 2 * 4 * 4 * capacity * count * width
    moved = 4 * width * (count + 4 * capacity)
    piece = ((count, half), bf16)
    far_low, far_high = fused(
        far_kernel,
        [piece] * 2,
        weights[3],
        *trade(result),
        flops=spent,
        bytes_accessed=moved,
    )
    add_low, add_high = send(far_low, onward), send(far_high, backward)

    def near_sums(rows, *adds):
        return fused(
            functools.partial(near_kernel, capacity),
            [piece] * 2,
            weights[1],
            weights[2],
            *trade(rows),
            *adds,
            flops=spent,
            bytes_accessed=moved,
        )

    before_sum, after_sum = near_sums(near[0:4])
    from_after_low = send(before_sum, backward)
    from_before_high = send(after_sum, onward)
    before_sum, after_sum = near_sums(near[4:8], add_high, add_low)
    from_after_high = send(before_sum, backward)
    from_before_low = send(after_sum, onward)
    return fused(
        last_kernel,
        [((count, width), bf16)],
        hidden,
        weights[0],
        *trade(near[8:12]),
        from_before_low,
        from_before_high,
        from_after_low,
        from_after_high,
        flops=spent,
        bytes_accessed=2 * moved,
    )[0]


def ring_steps():
    order = (0, 1, 3, 2)
    onward = [
        (order[i] * 4 + j, order[(i + 1) % 4] * 4 + j) for i in range(4) for j in range(4)
    ]
    return onward, [(b, a) for a, b in onward]


def per_device(
    x_resid,
    q_latent,
    q_rope,
    cache_latent,
    cache_rope,
    new_latent,
    new_rope,
    w_uv,
    w_out,
    norm_gain,
    router,
    expert_ids,
    w_gate,
    w_up,
    w_down,
):
    sequence = (
        q_latent[0],
        q_rope[0],
        cache_latent[0],
        cache_rope[0],
        new_latent[0],
        new_rope[0],
    )
    new_count = q_latent.shape[1]
    expert_count = lax.axis_size("ep")
    capacity = new_count * expert_ids.shape[2] // expert_count
    if lax.axis_size("fsdp") != 2 or expert_count != 16:
        projected = project_gathered(attend_local(*sequence), w_uv, w_out)
        hidden = x_resid[0].astype(jnp.float32) + projected
        normed = hidden * lax.rsqrt(jnp.mean(hidden * hidden, axis=-1, keepdims=True) + epsilon)
        normed = (normed * norm_gain).astype(jnp.bfloat16)
        target = slots_of(expert_ids[0], expert_count, capacity)
        routed_sum = routed_exchanged(
            normed, target, capacity, router, w_gate[0], w_up[0], w_down[0]
        )
        layer_out = (hidden + routed_sum).astype(jnp.bfloat16)
        return (hidden.astype(jnp.bfloat16)[None], layer_out[None])
    onward, backward = ring_steps()
    ids = [expert_ids[0].T]
    across = [(i, i ^ 12) for i in range(16)]
    ids += [lax.ppermute(ids[0], "ep", steps) for steps in (onward, backward)]
    ids.append(lax.ppermute(ids[0], "ep", across))
    targets = fused(
        functools.partial(slot_kernel, expert_count, capacity),
        [(part.shape, jnp.int32) for part in ids],
        *ids,
    )
    give, kept = attend_by_head(w_out.shape[0] // w_uv.shape[2], *sequence)
    part, back = project_paired(give, kept, w_uv, w_out)
    back, targets = lax.optimization_barrier((back, targets))
    width = part.shape[1]
    halves = (new_count, width // 2)
    hidden, attended, low, high = fused(
        norm_kernel,
        [
            ((new_count, width), jnp.float32),
            ((1, new_count, width), jnp.bfloat16),
            (halves, jnp.bfloat16),
            (halves, jnp.bfloat16),
        ],
        x_resid,
        part,
        back,
        norm_gain[None],
        flops=8 * new_count * width,
        bytes_accessed=20 * new_count * width,
    )
    layer_out = routed_ringed(
        hidden, low, high, targets, capacity, router, w_gate, w_up, w_down
    )
    return (attended, layer_out[None])


def solution(mesh):
    placed = (
        P(("fsdp", "ep"), None, None),
        P(("fsdp", "ep"), None, None, None),
        P(("fsdp", "ep"), None, None, None),
        P(("fsdp", "ep"), None, None),
        P(("fsdp", "ep"), None, None),
        P(("fsdp", "ep"), None, None),
        P(("fsdp", "ep"), None, None),
        P("fsdp", None, None),
        P("fsdp", None),
        P(),
        P(),
        P(("fsdp", "ep"), None, None),
        P("ep", None, None),
        P("ep", None, None),
        P("ep", None, None),
    )

    return jax.shard_map(
        per_device,
        mesh=mesh,
        in_specs=placed,
        out_specs=(P(("fsdp", "ep"), None, None), P(("fsdp", "ep"), None, None)),
        check_vma=False,
    )
```
